32 devices in a mesh: tiles: 2 (over y), pat: 16 (over z, x, core).
Axes of the slice: x: 2, y: 2, z: 4, core: 2. Of those that a mesh axis runs over, the one named last changes fastest.
Arguments:
- slab_phase: float32 [6, 1024, 1024], P('tiles', 'pat'), parts along dimension 0, may hold values from -2 to 2
- pupil_phase: float32 [1024, 1024], P('pat'), may hold values from -5 to 5
- pupil_mask: int32 [1024, 1024], P('pat'), may hold values from 0 to 1, as said below
- led_code: int32 [4, 2], replicated, may hold values from 0 to 1, as said below
- led_freq: int32 [2, 2], replicated, may hold values from -32 to 32
- measured: int32 [8, 1024, 1024], P('tiles', 'pat'), parts along dimension 0, may hold values from 1 to 2048
Outputs:
- phase_grad: float32 [6, 1024, 1024], P('tiles', 'pat'), parts along dimension 0
The draws below stay inside these ranges and needn't reach their ends.
There are 2 independent parts, one for each index of `tiles`. The reference program is written for one: setup_inputs(seed, part) draws one part's arguments, and reference() takes and returns one part's arrays. A program takes and returns all parts, laid end to end along the dimension named above; an argument that names none is the same for every part. Nothing has to cross between parts.
Inputs may be any that keep to these rules, and one draw needn't show every extreme that they name: `pupil_mask`: 1 at every frequency pair with freq(u)^2 + freq(v)^2 <= 9216, 0 where it is >= 16384, either value between. `led_code`: pattern p always has LED p mod 2 switched on.
All inputs are finite; a program needn't handle non-finite values.
Results may differ from the reference program's by a relative error of at most 0.0003.
Values sent between devices are 32-bit elements; how exact they have to be, the bound alone decides.
A program may use at most 128 MiB of HBM per device.

```python
import math
import jax
import jax.numpy as jnp
from jax import lax

N = 1024
SLICES = 3
LEDS = 2
PATTERNS = 4
PUP_OUT = 128
PUP_IN = 96
LED_MAX = 32


def draw_pupil_mask(key, part):
    grid_index = jnp.arange(N, dtype=jnp.int32)
    frequency_index = (grid_index + N // 2) % N - N // 2
    radius = frequency_index[:, None] * frequency_index[:, None] + frequency_index[None, :] * frequency_index[None, :]
    coin_flip = jax.random.randint(key, (N, N), 0, 2, dtype=jnp.int32)
    opened = jnp.where(radius <= PUP_IN * PUP_IN, 1, coin_flip)
    return jnp.where(radius >= PUP_OUT * PUP_OUT, 0, opened).astype(jnp.int32)


def draw_led_code(key, part):
    coin_flip = jax.random.randint(key, (PATTERNS, LEDS), 0, 2, dtype=jnp.int32)
    pattern_index = jnp.arange(PATTERNS, dtype=jnp.int32)[:, None] % LEDS
    forced = (pattern_index == jnp.arange(LEDS, dtype=jnp.int32)[None, :]).astype(jnp.int32)
    return jnp.maximum(coin_flip, forced).astype(jnp.int32)


def draw_measured(key, part):
    level_key, count_key = jax.random.split(key)
    row_level = jnp.arange(N, dtype=jnp.int32) * 4 // N
    col_level = jax.random.randint(level_key, (N,), 0, 4, dtype=jnp.int32)
    ceiling = jnp.left_shift(jnp.int32(32), row_level[:, None] + col_level[None, :])
    return jax.random.randint(count_key, (PATTERNS, N, N), 1, ceiling[None, :, :] + 1, dtype=jnp.int32)


def set_ends(entries, stream_key, low, largest):
    spot = [jax.random.randint(jax.random.fold_in(stream_key, axis), (), 0, length) for axis, length in enumerate(entries.shape)]
    widest = entries.shape.index(max(entries.shape))
    beside = spot[:widest] + [(spot[widest] + 1) % entries.shape[widest]] + spot[widest + 1:]
    return entries.at[tuple(spot)].set(low).at[tuple(beside)].set(largest)


def block_scale(rng, extent, shards, smallest, top_value):
    factor_of, own = 1.0, jax.random.fold_in(rng, 6)
    for position, blocks in shards:
        heights = jnp.exp(jax.random.uniform(jax.random.fold_in(own, position), (blocks,), jnp.float32, smallest / len(shards), top_value / len(shards)))
        factor_of = factor_of * jnp.repeat(heights, extent[position] // blocks).reshape([-1 if axis == position else 1 for axis in range(len(extent))])
    return factor_of


def scatter_about(rng, shape, deviation, limit, shards=(), held_as=jnp.bfloat16):
    gain = block_scale(rng, shape, shards, -0.22, 0.18) if shards else 1.0
    entries = jax.random.normal(rng, shape, jnp.float32) * deviation * gain
    return jnp.minimum(jnp.maximum(entries, -limit), limit).astype(held_as)


def setup_inputs(seed: int = 0, part: int = 0) -> dict:
    arg_keys = jax.random.split(jax.random.key(seed), 7)
    own_keys = jax.random.split(jax.random.fold_in(arg_keys[6], part), 7)
    return {
        "slab_phase": jnp.clip(jax.random.uniform(own_keys[0], (SLICES, N, N), jnp.float32, -2.0, 2.0) * block_scale(own_keys[0], (SLICES, N, N), ((1, 16),), -0.4, 0.0), -2.0, 2.0),
        "pupil_phase": scatter_about(arg_keys[1], (N, N), 1.0, 5.0, ((0, 16),), jnp.float32),
        "pupil_mask": draw_pupil_mask(jax.random.fold_in(arg_keys[6], 71), part),
        "led_code": draw_led_code(jax.random.fold_in(arg_keys[6], 71), part),
        "led_freq": set_ends(jax.random.randint(arg_keys[4], (LEDS, 2), 0 - LED_MAX, LED_MAX + 1), jax.random.fold_in(arg_keys[4], 1), 0 - LED_MAX, LED_MAX).astype(jnp.int32),
        "measured": draw_measured(jax.random.fold_in(jax.random.fold_in(arg_keys[6], part), 71), part),
    }


spread_rate = 0.3
highest = lax.Precision.HIGHEST

def frequency(grid_index, grid_size):
    return (grid_index + grid_size // 2) % grid_size - grid_size // 2

def fourier(values):
    return jnp.fft.fft2(values, norm='ortho')

def inverse(values):
    return jnp.fft.ifft2(values, norm='ortho')

def reference(slab_phase, pupil_phase, pupil_mask, led_code, led_freq, measured):
    grid_index = jnp.arange(N, dtype=jnp.int32)
    spatial = frequency(grid_index, N)
    radius = spatial[:, None] * spatial[:, None] + spatial[None, :] * spatial[None, :]
    cutoff = N // 2 * (N // 2)
    inside = radius <= cutoff
    height = jnp.sqrt(jnp.maximum(cutoff - radius, 0).astype(jnp.float32))
    phase_shift = spread_rate * (height - N // 2)
    propagator = jnp.where(inside, jnp.cos(phase_shift), 0.0) + 1j * jnp.where(inside, jnp.sin(phase_shift), 0.0)
    opening = pupil_mask.T.astype(jnp.float32)
    pupil = opening * jnp.cos(pupil_phase.T) + 1j * (opening * jnp.sin(pupil_phase.T))
    tilt_index = (led_freq[:, 0][:, None, None] * grid_index[None, :, None] + led_freq[:, 1][:, None, None] * grid_index[None, None, :]) % N
    tilt_angle = tilt_index.astype(jnp.float32) * (2.0 * math.pi / N)
    wave_field = jnp.cos(tilt_angle) + 1j * jnp.sin(tilt_angle)
    transmission = jnp.cos(slab_phase) + 1j * jnp.sin(slab_phase)
    passed_list = []
    for slab_index in range(SLICES):
        passed = wave_field * transmission[slab_index][None]
        passed_list.append(passed)
        spectral_factor = propagator if slab_index < SLICES - 1 else pupil
        wave_field = inverse(spectral_factor[None] * fourier(passed))
    camera = wave_field
    led_power = jnp.real(camera) * jnp.real(camera) + jnp.imag(camera) * jnp.imag(camera)
    code_float = led_code.astype(jnp.float32)
    pattern_power = jnp.einsum('pl,lrc->prc', code_float, led_power, precision=highest)
    counts = measured.astype(jnp.float32)
    area = float(N * N)
    mean_power = lax.optimization_barrier(jnp.sum(pattern_power, axis=(1, 2))) / area
    mean_count = lax.optimization_barrier(jnp.sum(counts, axis=(1, 2))) / area
    relative = pattern_power / mean_power[:, None, None]
    misfit = relative - counts / mean_count[:, None, None]
    coupling = lax.optimization_barrier(jnp.sum(misfit * relative, axis=(1, 2))) / area
    pattern_weight = (misfit - coupling[:, None, None]) / mean_power[:, None, None]
    led_weight = jnp.einsum('pl,prc->lrc', code_float, pattern_weight, precision=highest)
    adjoint_field = 2.0 * led_weight * camera
    back_field = inverse(jnp.conj(pupil)[None] * fourier(adjoint_field))
    gradients = [None] * SLICES
    for slab_index in range(SLICES - 1, -1, -1):
        gradients[slab_index] = lax.optimization_barrier(jnp.sum(jnp.imag(jnp.conj(passed_list[slab_index]) * back_field), axis=0))
        if slab_index > 0:
            released = back_field * jnp.conj(transmission[slab_index])[None]
            back_field = inverse(jnp.conj(propagator)[None] * fourier(released))
    return jnp.stack(gradients)
```

```python
import functools
import math
import types

import jax
import jax.numpy as jnp
import numpy as np
from jax import lax
from jax.experimental import pallas as pl
from jax.experimental.pallas import tpu as pltpu
from jax.sharding import PartitionSpec as P

spread_rate = 0.3
highest = lax.Precision.HIGHEST


def frequency(grid_index, grid_size):
    return (grid_index + grid_size // 2) % grid_size - grid_size // 2


def complex_times(values, factor):
    real_part = values[0] * factor[0] - values[1] * factor[1]
    imag_part = values[0] * factor[1] + values[1] * factor[0]
    return jnp.stack([real_part, imag_part])


def dft_block(length, direction, norm_factor):
    grid_index = jnp.arange(length, dtype=jnp.int32)
    angles = (grid_index[:, None] * grid_index[None, :] % length).astype(jnp.float32) * (
        2.0 * math.pi / length
    )
    cosine = jnp.cos(angles) * norm_factor
    signed_sine = direction * jnp.sin(angles) * norm_factor
    real_rows = jnp.stack([cosine, signed_sine], 1)
    imag_rows = jnp.stack([-signed_sine, cosine], 1)
    return jnp.stack([real_rows, imag_rows], 0)


def twiddle_table(short_size, long_size, grid_size, direction):
    short_index = jnp.arange(short_size, dtype=jnp.int32)
    long_index = jnp.arange(long_size, dtype=jnp.int32)
    angles = (short_index[:, None] * long_index[None, :] % grid_size).astype(jnp.float32) * (
        2.0 * math.pi / grid_size
    )
    return jnp.stack([jnp.cos(angles), direction * jnp.sin(angles)])


def table_set(col_count, dev_count, grid_size, direction):
    short_table = dft_block(col_count, direction, 1.0)
    long_table = dft_block(dev_count, direction, 1.0 / math.sqrt(grid_size))
    return (short_table, long_table, twiddle_table(col_count, dev_count, grid_size, direction))


def to_fourier(wave_field, tables, dev_count):
    short_table, long_table, twiddles = tables
    led_count = wave_field.shape[1]
    row_count = wave_field.shape[2]
    grid_size = wave_field.shape[3]
    col_count = grid_size // dev_count
    shaped = wave_field.reshape(2, led_count, row_count, col_count, dev_count)
    sectioned = jnp.einsum("zlrmq,zmwc->wlrcq", shaped, short_table, precision=highest)
    sectioned = complex_times(sectioned, twiddles)
    outgoing = jnp.einsum("wlrcq,wqvd->dvlcr", sectioned, long_table, precision=highest)
    incoming = lax.all_to_all(
        outgoing.reshape(dev_count, -1), "pat", split_axis=0, concat_axis=0, tiled=True
    )
    incoming = incoming.reshape(dev_count, 2, led_count, col_count, row_count)
    sectioned = jnp.einsum("swlcr,wsvj->vlcrj", incoming, long_table, precision=highest)
    sectioned = complex_times(sectioned, twiddles)
    sectioned = jnp.einsum("wlcrj,wrvh->vlchj", sectioned, short_table, precision=highest)
    return sectioned.reshape(2, led_count, col_count, grid_size)


def to_space(spectrum, tables, dev_count):
    short_table, long_table, twiddles = tables
    led_count = spectrum.shape[1]
    col_count = spectrum.shape[2]
    grid_size = spectrum.shape[3]
    row_count = grid_size // dev_count
    shaped = spectrum.reshape(2, led_count, col_count, row_count, dev_count)
    sectioned = jnp.einsum("zlcmq,zmwr->wlcrq", shaped, short_table, precision=highest)
    sectioned = complex_times(sectioned, twiddles)
    outgoing = jnp.einsum("wlcrq,wqvd->dvlcr", sectioned, long_table, precision=highest)
    incoming = lax.all_to_all(
        outgoing.reshape(dev_count, -1), "pat", split_axis=0, concat_axis=0, tiled=True
    )
    incoming = incoming.reshape(dev_count, 2, led_count, col_count, row_count)
    sectioned = jnp.einsum("swlcr,wsvj->vlrcj", incoming, long_table, precision=highest)
    sectioned = complex_times(sectioned, twiddles)
    sectioned = jnp.einsum("wlrcj,wcvh->vlrhj", sectioned, short_table, precision=highest)
    return sectioned.reshape(2, led_count, row_count, grid_size)


def plain_body(slab_phase, pupil_phase, pupil_mask, led_code, led_freq, measured):
    dev_count = lax.axis_size("pat")
    position = lax.axis_index("pat")
    slab_count, row_count, grid_size = slab_phase.shape
    col_count = grid_size // dev_count
    pattern_count, led_count = led_code.shape
    area = float(grid_size * grid_size)
    forward_set = table_set(col_count, dev_count, grid_size, -1.0)
    inverse_set = table_set(col_count, dev_count, grid_size, 1.0)
    conjugate = jnp.array([1.0, -1.0], jnp.float32)[:, None, None]
    col_freq = frequency(position * col_count + jnp.arange(col_count, dtype=jnp.int32), grid_size)
    row_freq = frequency(jnp.arange(grid_size, dtype=jnp.int32), grid_size)
    radius = col_freq[:, None] * col_freq[:, None] + row_freq[None, :] * row_freq[None, :]
    cutoff = grid_size // 2 * (grid_size // 2)
    inside = radius <= cutoff
    height = jnp.sqrt(jnp.maximum(cutoff - radius, 0).astype(jnp.float32))
    phase_shift = spread_rate * (height - grid_size // 2)
    propagator = jnp.stack(
        [jnp.where(inside, jnp.cos(phase_shift), 0.0), jnp.where(inside, jnp.sin(phase_shift), 0.0)]
    )
    opening = pupil_mask.astype(jnp.float32)
    pupil = jnp.stack([opening * jnp.cos(pupil_phase), opening * jnp.sin(pupil_phase)])
    propagator_conj = propagator * conjugate
    pupil_conj = pupil * conjugate
    row_index = position * row_count + jnp.arange(row_count, dtype=jnp.int32)
    col_index = jnp.arange(grid_size, dtype=jnp.int32)
    tilt_index = (
        led_freq[:, 0][:, None, None] * row_index[None, :, None]
        + led_freq[:, 1][:, None, None] * col_index[None, None, :]
    ) % grid_size
    tilt_angle = tilt_index.astype(jnp.float32) * (2.0 * math.pi / grid_size)
    illumination = jnp.stack([jnp.cos(tilt_angle), jnp.sin(tilt_angle)])
    transmission = jnp.stack([jnp.cos(slab_phase), jnp.sin(slab_phase)])
    group_count = 1
    group_size = led_count // group_count
    wave_groups = [illumination]
    passed_groups = []
    for slab_index in range(slab_count):
        factor = transmission[:, slab_index]
        passed = [complex_times(wave_field, factor) for wave_field in wave_groups]
        passed_groups.append(passed)
        spectral_factor = propagator if slab_index < slab_count - 1 else pupil
        wave_groups = [
            to_space(
                complex_times(to_fourier(passed_field, forward_set, dev_count), spectral_factor),
                inverse_set,
                dev_count,
            )
            for passed_field in passed
        ]
    camera = wave_groups[0]
    led_power = camera[0] * camera[0] + camera[1] * camera[1]
    code_float = led_code.astype(jnp.float32)
    pattern_power = jnp.dot(
        code_float, led_power.reshape(led_count, -1), precision=highest
    ).reshape(pattern_count, row_count, grid_size)
    counts = measured.astype(jnp.float32)
    power_sum, count_sum = lax.psum(
        (jnp.sum(pattern_power, axis=(1, 2)), jnp.sum(counts, axis=(1, 2))), "pat"
    )
    mean_power = power_sum / area
    mean_count = count_sum / area
    relative = pattern_power / mean_power[:, None, None]
    misfit = relative - counts / mean_count[:, None, None]
    coupling = lax.psum(jnp.sum(misfit * relative, axis=(1, 2)), "pat") / area
    pattern_weight = (misfit - coupling[:, None, None]) / mean_power[:, None, None]
    led_weight = jnp.dot(
        code_float.T, pattern_weight.reshape(pattern_count, -1), precision=highest
    ).reshape(led_count, row_count, grid_size)
    camera_adjoint = 2.0 * led_weight[None] * camera
    adjoint_groups = [camera_adjoint]
    gradients = [None] * slab_count
    for slab_index in range(slab_count - 1, -1, -1):
        spectral_factor = pupil_conj if slab_index == slab_count - 1 else propagator_conj
        back_groups = [
            to_space(
                complex_times(to_fourier(adjoint_field, forward_set, dev_count), spectral_factor),
                inverse_set,
                dev_count,
            )
            for adjoint_field in adjoint_groups
        ]
        gradient = jnp.zeros((row_count, grid_size), jnp.float32)
        for passed_field, back_field in zip(passed_groups[slab_index], back_groups):
            gradient = jnp.sum(
                passed_field[0] * back_field[1] - passed_field[1] * back_field[0], axis=0
            )
        gradients[slab_index] = gradient
        if slab_index > 0:
            release = transmission[:, slab_index] * conjugate
            adjoint_groups = [complex_times(back_field, release) for back_field in back_groups]
    return jnp.stack(gradients)


class Names(types.SimpleNamespace):
    def __getitem__(self, name):
        return getattr(self, name)


pupil_radius = 128
lanes = 128
f32 = jnp.float32
bf16 = jnp.bfloat16


def halves(table):
    table32 = np.asarray(table, np.float32)
    high = table32.astype(bf16)
    low = (table32 - high.astype(np.float32)).astype(bf16)
    return np.stack([high, low])


def row_tables(size, block, band_block):
    quarter = size // 4
    pos = np.arange(quarter)
    angle = 2.0 * np.pi * ((pos[:, None] * pos[None, :]) % quarter) / quarter
    cosine = np.cos(angle) / math.sqrt(size)
    sine = np.sin(angle) / math.sqrt(size)

    def forward(freqs, width):
        parts = []
        for first in range(0, len(freqs), width):
            pick = freqs[first : first + width] % quarter
            left = np.concatenate([cosine[:, pick], sine[:, pick]], 0)
            right = np.concatenate([-sine[:, pick], cosine[:, pick]], 0)
            parts.append(np.concatenate([left, right], 1))
        return np.concatenate(parts, 1)

    full = forward(pos, block)
    reach = pupil_radius // 4
    band = forward(np.arange(-reach, reach), band_block)
    theta = 2.0 * np.pi * (np.arange(4)[:, None] * pos[None, :]) / size
    twiddle = np.concatenate([np.cos(theta), np.sin(theta)], 0).astype(np.float32)
    return Names(
        full=jnp.asarray(halves(full)),
        full_inv=jnp.asarray(halves(full.T)),
        band=jnp.asarray(halves(band)),
        band_inv=jnp.asarray(halves(band.T)),
        twiddle=jnp.asarray(twiddle),
    )


def col_tables(size):
    quarter = size // 4
    pos = np.arange(quarter)
    angle = 2.0 * np.pi * ((pos[:, None] * pos[None, :]) % quarter) / quarter
    both = np.concatenate([np.cos(angle), np.sin(angle)], 0) / math.sqrt(size)
    theta = 2.0 * np.pi * (np.arange(1, 4)[:, None] * pos[None, :]) / size
    twiddle = np.stack([np.cos(theta), np.sin(theta)]).astype(np.float32)
    twiddle = np.ascontiguousarray(np.broadcast_to(twiddle[..., None], twiddle.shape + (lanes,)))
    freqs = np.arange(-pupil_radius, pupil_radius)
    angle = 2.0 * np.pi * ((np.arange(size)[:, None] * freqs[None, :]) % size) / size
    cosine = np.cos(angle) / math.sqrt(size)
    sine = np.sin(angle) / math.sqrt(size)
    band = halves(np.concatenate([cosine, sine], 1))
    band_inv = halves(np.concatenate([cosine.T, sine.T], 1))
    return Names(both=halves(both), twiddle=twiddle, band=band, band_inv=band_inv)


def split(value):
    high = value.astype(bf16)
    return high, (value - high.astype(f32)).astype(bf16)


def dot3(left, right):
    def dot(a, b):
        return jnp.dot(a, b, preferred_element_type=f32)

    return dot(left[0], right[0]) + (dot(left[0], right[1]) + dot(left[1], right[0]))


def turn(value):
    rolled = pltpu.roll(value, lanes // 2, 1)
    lane = lax.broadcasted_iota(jnp.int32, value.shape, 1)
    return jnp.where(lane < lanes // 2, rolled, -rolled)


def row_spread(blocks, twiddle_ref):
    (r0, i0), (r1, i1), (r2, i2), (r3, i3) = blocks
    sr, si, tr, ti = r0 + r2, i0 + i2, r1 + r3, i1 + i3
    dr, di, er, ei = r0 - r2, i0 - i2, r1 - r3, i1 - i3
    mixed = [(sr + tr, si + ti), (dr + ei, di - er), (sr - tr, si - ti), (dr - ei, di + er)]
    out = [mixed[0]]
    for j in range(1, 4):
        cosine, sine = twiddle_ref[j : j + 1, :], twiddle_ref[4 + j : 5 + j, :]
        re, im = mixed[j]
        out.append((re * cosine + im * sine, im * cosine - re * sine))
    return out


def row_gather(parts, twiddle_ref):
    g = [parts[0]]
    for j in range(1, 4):
        cosine, sine = twiddle_ref[j : j + 1, :], twiddle_ref[4 + j : 5 + j, :]
        re, im = parts[j]
        g.append((re * cosine - im * sine, im * cosine + re * sine))
    (r0, i0), (r1, i1), (r2, i2), (r3, i3) = g
    sr, si, tr, ti = r0 + r2, i0 + i2, r1 + r3, i1 + i3
    dr, di, er, ei = r0 - r2, i0 - i2, r1 - r3, i1 - i3
    return [(sr + tr, si + ti), (dr - ei, di + er), (sr - tr, si - ti), (dr + ei, di - er)]


mesh_ids = pl.DeviceIdType.MESH
far_first = (14, 15, 6, 7, 10, 11, 12, 13, 2, 3, 4, 5, 8, 9, 1)
exit_order = (14, 15, 12, 13, 10, 11, 8, 9, 6, 7, 4, 5, 2, 3, 1, 0)


def flip(index, mask):
    out = index
    for bit in (1, 2, 4, 8):
        if mask & bit:
            out = out + bit - 2 * bit * lax.rem(index // bit, 2)
    return out


def whole_kernel(spec, *refs):
    ref = Names(**dict(zip(spec.names, refs)))
    count, rows, quarter, devs, patterns = spec.count, spec.rows, spec.quarter, spec.devs, spec.patterns
    size, per, half, step = 4 * quarter, devs // 4, devs // 2, 16
    tile, place = lax.axis_index("tiles"), lax.axis_index("pat")
    work = place // half
    me = half * tile + lax.rem(place, half)
    native = tile == work
    other = dict(tiles=1 - tile, pat=lax.rem(place + half, devs))

    def member(index):
        return dict(tiles=index // half, pat=work * half + lax.rem(index, half))

    barrier = pltpu.get_barrier_semaphore()
    everyone = spec.tiles * devs

    def signal(hop, carry):
        target = lax.rem(tile * devs + place + hop, everyone)
        pl.semaphore_signal(
            barrier, inc=1, device_id=dict(tiles=target // devs, pat=lax.rem(target, devs)),
            device_id_type=mesh_ids,
        )
        return carry

    lax.fori_loop(1, everyone, signal, 0)

    def local(source, target, sem):
        return pltpu.make_async_copy(source, target, sem)

    def away(source, target, sent, got, device):
        return pltpu.make_async_remote_copy(
            src_ref=source, dst_ref=target, send_sem=sent, recv_sem=got, device_id=device,
            device_id_type=mesh_ids,
        )

    def fetch(name):
        return local(ref[name + "_hbm"], ref[name], ref.loads.at[spec.loaded.index(name)])

    reach = pupil_radius
    spans = (slice(size - reach, size), slice(0, reach))

    def near(name, k):
        return local(ref[name + "_hbm"].at[:, spans[k]], ref[name].at[k], ref[name + "_sem"].at[k])

    for name in ("phase", "mask"):
        for k in range(2):
            near(name, k).start()
    for name in spec.loaded:
        fetch(name).start()

    def ready(name):
        fetch(name).wait()

    def trade(source, target, sent, got):
        @pl.when(native)
        def _():
            local(source, target, got).start()

        @pl.when(jnp.logical_not(native))
        def _():
            away(source, target, sent, got, other).start()

    def trade_slab(s):
        trade(ref.slab_hbm.at[s], ref.slab.at[s], ref.slab_sent.at[s], ref.slab_got.at[s])

    def trade_count(p):
        trade(ref.measured_hbm.at[p], ref.measured.at[p], ref.count_sent.at[p], ref.count_got.at[p])

    def port(name):
        return Names(
            stage=ref[name + "_stage"], y=ref[name + "_y"], sent=ref[name + "_sent"], got=ref[name + "_got"]
        )

    def push(x, slot):
        for mask in far_first:
            dest = flip(me, mask)
            away(
                x.stage.at[slot, dest], x.y.at[slot, me], x.sent.at[slot], x.got.at[slot], member(dest)
            ).start()
        local(x.stage.at[slot, me], x.y.at[slot, me], x.got.at[slot]).start()

    def land(x, slot):
        local(x.y.at[slot], x.y.at[slot], x.got.at[slot]).wait()

    def drain(x, slots):
        for slot in range(slots):
            part = x.stage.at[slot, pl.ds(0, devs - 1)]
            local(part, part, x.sent.at[slot]).wait()

    hi, lo, zs = ref.hi, ref.lo, ref.zs
    cut = [slice(a * quarter, (a + 1) * quarter) for a in range(4)]

    def spot(l, base):
        return pl.ds(pl.multiple_of(l * rows + base, step), step)

    def each_chunk(chunk, carry=0):
        def at_chunk(i, carry):
            base = pl.multiple_of(i * step, step)
            return chunk(base, pl.ds(base, step), carry)

        return lax.fori_loop(0, rows // step, at_chunk, carry)

    def gathered(l, base):
        at = spot(l, base)
        parts = [(zs[j, at, :quarter], zs[j, at, quarter:]) for j in range(4)]
        return row_gather(parts, ref.row_twiddle)

    def scattered(l, base, blocks):
        at = spot(l, base)
        for j, (re, im) in enumerate(row_spread(blocks, ref.row_twiddle)):
            high, low = split(re)
            hi[j, at, :quarter] = high
            lo[j, at, :quarter] = low
            high, low = split(im)
            hi[j, at, quarter:] = high
            lo[j, at, quarter:] = low

    def led_rows(l):
        return pl.ds(pl.multiple_of(l * rows, rows), rows)

    def inverse_full(y, slot, l):
        for j in range(4):
            for q in range(per):
                high, low = split(y[slot, per * j + q])
                ref.ghi[j * rows : (j + 1) * rows, q * lanes : (q + 1) * lanes] = high
                ref.glo[j * rows : (j + 1) * rows, q * lanes : (q + 1) * lanes] = low
        value = dot3((ref.ghi[...], ref.glo[...]), (ref.full_inv[0], ref.full_inv[1]))
        zs[:, led_rows(l), :] = value.reshape(4, rows, 2 * quarter)

    def emit_full(x, slot, l):
        left = [part[:, led_rows(l), :].reshape(4 * rows, 2 * quarter) for part in (hi, lo)]
        value = dot3(left, (ref.full[0], ref.full[1]))
        for j in range(4):
            for q in range(per):
                x.stage[slot, per * j + q] = value[j * rows : (j + 1) * rows, q * lanes : (q + 1) * lanes]
        push(x, slot)

    total = count * rows

    def inverse_band(x):
        for j in range(4):
            block = x.y[0, per * j : per * (j + 1)].reshape(-1, total)
            zs[j, :, :] = dot3(split(block.T), (ref.band_inv[0], ref.band_inv[1]))

    def emit_band(x):
        for j in range(4):
            value = dot3((hi[j], lo[j]), (ref.band[0], ref.band[1]))
            flipped = value.T
            deep = flipped.shape[0] // per
            for q in range(per):
                x.stage[0, per * j + q] = flipped[q * deep : (q + 1) * deep]
        push(x, 0)

    def tilt(l, here, a, value, sign):
        rc, rs = ref.tilt_r[2 * l, here, :], ref.tilt_r[2 * l + 1, here, :]
        cc, cs = ref.tilt_c[2 * l, :, cut[a]], ref.tilt_c[2 * l + 1, :, cut[a]]
        rc = jnp.concatenate([rc] * (quarter // lanes), 1)
        rs = jnp.concatenate([rs] * (quarter // lanes), 1)
        er = rc * cc - rs * cs
        ei = sign * (rc * cs + rs * cc)
        re, im = value
        return re * er - im * ei, re * ei + im * er

    def spread(x, slot):
        def at_part(i, carry):
            here = pl.ds(pl.multiple_of(i * rows, rows), rows)
            x0, x1, x2, x3 = [x.y[slot, per * a + i] for a in range(4)]
            s, t, d, e = x0 + x2, x1 + x3, x0 - x2, turn(x1 - x3)
            for j, value in enumerate((s + t, d + e, s - t, d - e)):
                if j:
                    value = value * ref.col_twiddle[0, j - 1, here, :] + turn(value) * ref.col_twiddle[1, j - 1, here, :]
                high, low = split(value)
                ref.chi[here, j * lanes : (j + 1) * lanes] = high
                ref.clo[here, j * lanes : (j + 1) * lanes] = low
            return carry

        lax.fori_loop(0, per, at_part, 0)

    def col_dot(high, low, take, sign):
        for pair in range(2):
            at = slice(2 * pair * lanes, 2 * (pair + 1) * lanes)
            y = dot3((ref.both[0], ref.both[1]), (high[:, at], low[:, at]))
            for k in range(2):
                at = slice(k * lanes, (k + 1) * lanes)
                take(2 * pair + k, y[:quarter, at] + sign * turn(y[quarter:, at]))

    def shaped(z, l, j, sign):
        return z * ref.prop[0, l, j] - sign * (turn(z) * ref.prop[1, l, j])

    def stow(j, value):
        high, low = split(value)
        ref.dhi[:, j * lanes : (j + 1) * lanes] = high
        ref.dlo[:, j * lanes : (j + 1) * lanes] = low

    def col_inverse(x, slot):
        def take(j, value):
            if j:
                value = value * ref.col_twiddle[0, j - 1] - turn(value) * ref.col_twiddle[1, j - 1]
            ref.cz[j] = value

        col_dot(ref.dhi, ref.dlo, take, -1.0)

        def at_part(i, carry):
            here = pl.ds(pl.multiple_of(i * rows, rows), rows)
            g0, g1, g2, g3 = [ref.cz[j, here, :] for j in range(4)]
            s, t, d, e = g0 + g2, g1 + g3, g0 - g2, turn(g1 - g3)
            for a, value in enumerate((s + t, d - e, s - t, d + e)):
                x.stage[slot, per * a + i] = value
            return carry

        lax.fori_loop(0, per, at_part, 0)

    def each_led(stage):
        def at_led(l, carry):
            stage(l)
            return carry

        lax.fori_loop(0, count, at_led, 0)

    def columns(x, out, sign):
        def stage(l):
            land(x, l)
            spread(x, l)
            col_dot(ref.chi, ref.clo, lambda j, z: stow(j, shaped(z, l, j, sign)), 1.0)
            col_inverse(out, l)
            push(out, l)

        each_led(stage)

    def pupil_columns(x, out, sign):
        land(x, 0)
        middle = lanes // 2
        lane = lax.broadcasted_iota(jnp.int32, x.y.shape[2:], 1)
        pieces = [[], []]
        for s in range(0, devs, 2):
            even, odd = x.y[0, s], x.y[0, s + 1]
            pieces[0].append(jnp.where(lane < middle, even, pltpu.roll(odd, middle, 1)))
            pieces[1].append(jnp.where(lane < middle, pltpu.roll(even, middle, 1), odd))
        field = jnp.concatenate([jnp.concatenate(p, 1) for p in pieces], 0)
        wide = ref.pupil_in.shape[2] // 2
        deep = ref.pupil_out.shape[2] // 2
        cols = x.y.shape[2] // 2
        both = dot3(split(field), (ref.pupil_in[0], ref.pupil_in[1]))
        scaled = []
        for l in range(count):
            re = slice(2 * l * cols, (2 * l + 1) * cols)
            im = slice((2 * l + 1) * cols, (2 * l + 2) * cols)
            yr = both[re, :wide] + both[im, wide:]
            yi = both[im, :wide] - both[re, wide:]
            pr, pi = ref.pupil[0], sign * ref.pupil[1]
            scaled += [yr * pr - yi * pi, yr * pi + yi * pr]
        both = dot3(split(jnp.concatenate(scaled, 0)), (ref.pupil_out[0], ref.pupil_out[1]))
        found = []
        for l in range(count):
            re = slice(2 * l * cols, (2 * l + 1) * cols)
            im = slice((2 * l + 1) * cols, (2 * l + 2) * cols)
            found.append(
                jnp.concatenate(
                    [both[re, :deep] - both[im, deep:], both[im, :deep] + both[re, deep:]], 0
                )
            )
        for s in range(0, devs, 2):
            at = slice(s * middle, s * middle + lanes)
            first, second = found[0][:, at], found[1][:, at]
            out.stage[0, s] = jnp.where(lane < middle, first, pltpu.roll(second, middle, 1))
            out.stage[0, s + 1] = jnp.where(lane < middle, pltpu.roll(first, middle, 1), second)
        push(out, 0)

    def phases(source, target):
        def chunk(base, here, carry):
            phase = source[here, :]
            target[0, here, :] = jnp.cos(phase)
            target[1, here, :] = jnp.sin(phase)
            return carry

        each_chunk(chunk)

    def slab_phases(s):
        local(ref.slab.at[s], ref.slab.at[s], ref.slab_got.at[s]).wait()
        phases(ref.slab.at[s], ref.tr.at[s])

    for name in ("phase", "mask"):
        for k in range(2):
            near(name, k).wait()
    for j in range(4):
        line = pl.ds(j, rows // 4, stride=4)
        for k in range(2):
            opening = ref.mask[k, line, :].astype(f32)
            angle = ref.phase[k, line, :]
            at = slice(k * reach, (k + 1) * reach)
            ref.own[j, 0, :, at] = opening * jnp.cos(angle)
            ref.own[j, 1, :, at] = opening * jnp.sin(angle)
    turn_size = 2.0 * math.pi / size
    col = lax.broadcasted_iota(jnp.int32, (8, size), 1)
    row = me * rows + lax.broadcasted_iota(jnp.int32, (rows, lanes), 0)
    for l in range(count):
        for index, freq, tilts in ((col, ref.freq[l, 1], ref.tilt_c), (row, ref.freq[l, 0], ref.tilt_r)):
            angle = jnp.bitwise_and(index * freq, size - 1).astype(f32) * turn_size
            deep = tilts.shape[1]
            tilts[2 * l] = jnp.cos(angle)[:deep]
            tilts[2 * l + 1] = jnp.sin(angle)[:deep]

    pl.semaphore_wait(barrier, everyone - 1)
    trade_slab(0)

    owners = spec.owners

    def pupil_copy(jj, w, q):
        return away(
            ref.own.at[2 * tile + jj], ref.pupil, ref.pupil_sent.at[2 * jj + w], ref.pupil_got,
            dict(tiles=tile, pat=w * half + jj * per + q),
        )

    for q in range(per):

        @pl.when(place == owners[q])
        def _():
            for jj in range(2):
                for w in range(2):
                    pupil_copy(jj, w, q).start()

    cutoff = size // 2 * (size // 2)

    def centred(index):
        return jnp.where(index >= size // 2, index - size, index)

    def spectrum(i, carry):
        here = pl.ds(pl.multiple_of(i * step, step), step)
        row = lax.broadcasted_iota(jnp.int32, (step, lanes), 0) + i * step
        lane = lax.broadcasted_iota(jnp.int32, (step, lanes), 1)
        lane = jnp.where(lane < lanes // 2, lane, lane - lanes // 2)
        col = 4 * (lax.rem(me, per) * (lanes // 2) + lane) + me // per
        for l in range(count):
            v = centred(col + ref.freq[l, 1])
            for j in range(4):
                u = centred(4 * row + j + ref.freq[l, 0])
                radius = u * u + v * v
                inside = radius <= cutoff
                height = jnp.sqrt(jnp.maximum(cutoff - radius, 0).astype(f32))
                shift = spread_rate * (height - float(size // 2))
                ref.prop[0, l, j, here, :] = jnp.where(inside, jnp.cos(shift), 0.0)
                ref.prop[1, l, j, here, :] = jnp.where(inside, jnp.sin(shift), 0.0)
        return carry

    lax.fori_loop(0, quarter // step, spectrum, 0)

    ready("row_twiddle")
    ready("full")
    local(ref.slab.at[0], ref.slab.at[0], ref.slab_got.at[0]).wait()

    def enter(base, here, carry):
        blocks = []
        for c in cut:
            phase = ref.slab[0, here, c]
            blocks.append((jnp.cos(phase), jnp.sin(phase)))
        scattered(0, base, blocks)
        return carry

    each_chunk(enter)
    x0, x1, x2, x3 = port("x0"), port("x1"), port("x2"), port("x3")
    emit_full(x0, 0, 0)
    trade_slab(1)
    ready("col_twiddle")
    ready("both")
    ready("full_inv")
    land(x0, 0)
    spread(x0, 0)

    def keep_spectrum(j, z):
        ref.cs[j] = z

    col_dot(ref.chi, ref.clo, keep_spectrum, 1.0)

    def first(l):
        for j in range(4):
            stow(j, shaped(ref.cs[j], l, j, 1.0))
        col_inverse(x1, l)
        push(x1, l)

    each_led(first)
    trade_slab(2)
    slab_phases(1)

    def forward(l):
        land(x1, l)
        inverse_full(x1.y, l, l)

        def chunk(base, here, carry):
            fields, at, blocks = gathered(l, base), spot(l, base), []
            for a, c in enumerate(cut):
                tr, ti = ref.tr[1, 0, here, c], ref.tr[1, 1, here, c]
                re, im = fields[a]
                re, im = re * tr - im * ti, re * ti + im * tr
                ref.passed1[0, at, c] = re
                ref.passed1[1, at, c] = im
                blocks.append((re, im))
            scattered(l, base, blocks)
            return carry

        each_chunk(chunk)
        emit_full(x2, l, l)

    each_led(forward)
    for p in range(patterns // 2):
        trade_count(p)
    columns(x2, x3, 1.0)
    for p in range(patterns // 2, patterns):
        trade_count(p)
    slab_phases(2)

    def forward_band(l):
        land(x3, l)
        inverse_full(x3.y, l, l)

        def chunk(base, here, carry):
            fields, at, blocks = gathered(l, base), spot(l, base), []
            for a, c in enumerate(cut):
                tr, ti = ref.tr[2, 0, here, c], ref.tr[2, 1, here, c]
                re, im = fields[a]
                re, im = re * tr - im * ti, re * ti + im * tr
                ref.passed2[0, at, c] = re
                ref.passed2[1, at, c] = im
                blocks.append(tilt(l, here, a, (re, im), 1.0))
            scattered(l, base, blocks)
            return carry

        each_chunk(chunk)

    each_led(forward_band)
    b0, b1, b2, b3, sums = port("b0"), port("b1"), port("b2"), port("b3"), port("sums")
    ready("band")
    emit_band(b0)
    ready("pupil_in")
    ready("pupil_out")
    local(ref.pupil, ref.pupil, ref.pupil_got).wait()
    pupil_columns(b0, b1, 1.0)
    for p in range(patterns):
        local(ref.measured.at[p], ref.measured.at[p], ref.count_got.at[p]).wait()
    ready("band_inv")
    land(b1, 0)
    inverse_band(b1)

    def fold(value):
        total_rows = value[:8]
        for k in range(1, value.shape[0] // 8):
            total_rows = total_rows + value[8 * k : 8 * k + 8]
        out = total_rows[:, :lanes]
        for k in range(1, value.shape[1] // lanes):
            out = out + total_rows[:, lanes * k : lanes * (k + 1)]
        return out

    def measure(base, here, carry):
        fields = [gathered(l, base) for l in range(count)]
        adds = [0.0] * spec.stat_rows
        for a, c in enumerate(cut):
            power = []
            for l in range(count):
                at = spot(l, base)
                re, im = fields[l][a]
                ref.camera[0, at, c] = re
                ref.camera[1, at, c] = im
                power.append(re * re + im * im)
            values = list(power)
            for l in range(count):
                for m in range(l, count):
                    values.append(power[l] * power[m])
            seen = [ref.measured[p, here, c].astype(f32) for p in range(patterns)]
            for p in range(patterns):
                for l in range(count):
                    values.append(seen[p] * power[l])
            values += seen
            for k, value in enumerate(values):
                adds[k] = adds[k] + fold(value)
        return tuple(x + y for x, y in zip(carry, adds))

    stats = each_chunk(measure, tuple(jnp.zeros((8, lanes), f32) for _ in range(spec.stat_rows)))
    packed = [jnp.sum(line, 0, keepdims=True) for line in stats]
    packed.append(jnp.zeros((sums.stage.shape[2] - len(packed), lanes), f32))
    packed = jnp.concatenate(packed, 0)
    for d in range(devs):
        sums.stage[0, d] = packed
    push(sums, 0)
    land(sums, 0)
    added = jnp.sum(jnp.sum(sums.y[0], 0), 1, keepdims=True)
    code = [[ref.code[p, l].astype(f32) for l in range(count)] for p in range(patterns)]
    area = spec.area
    power_mean, count_mean, couple = [], [], []
    base_row = count + count * (count + 1) // 2
    for p in range(patterns):
        mean = sum(added[l : l + 1] * code[p][l] for l in range(count)) / area
        mean_count = added[base_row + patterns * count + p :][:1] / area
        square = 0.0
        at = count
        for l in range(count):
            for m in range(l, count):
                factor = 1.0 if l == m else 2.0
                square = square + (factor * code[p][l] * code[p][m]) * added[at : at + 1]
                at += 1
        cross = sum(code[p][l] * added[base_row + p * count + l :][:1] for l in range(count))
        power_mean.append(mean)
        count_mean.append(mean_count)
        couple.append((square / mean / mean - cross / mean_count / mean) / area)

    def weigh(base, here, carry):
        outgoing = [[] for _ in range(count)]
        for a, c in enumerate(cut):
            camera, power = [], []
            for l in range(count):
                at = spot(l, base)
                re, im = ref.camera[0, at, c], ref.camera[1, at, c]
                camera.append((re, im))
                power.append(re * re + im * im)
            weight = [0.0] * count
            for p in range(patterns):
                lit = sum(code[p][l] * power[l] for l in range(count))
                seen = ref.measured[p, here, c].astype(f32)
                misfit = lit * (1.0 / power_mean[p]) - seen * (1.0 / count_mean[p])
                pull = (misfit - couple[p]) * (1.0 / power_mean[p])
                for l in range(count):
                    weight[l] = weight[l] + code[p][l] * pull
            for l in range(count):
                scale = 2.0 * weight[l]
                outgoing[l].append((scale * camera[l][0], scale * camera[l][1]))
        for l in range(count):
            scattered(l, base, outgoing[l])
        return carry

    each_chunk(weigh)
    emit_band(b2)
    pupil_columns(b2, b3, -1.0)
    land(b3, 0)
    inverse_band(b3)
    y2, y1, y0, out = port("y2"), port("y1"), port("y0"), port("out")
    y3 = port("y3")
    ref.grad[...] = jnp.zeros(ref.grad.shape, f32)

    def back_band(l):
        def chunk(base, here, carry):
            fields, at, blocks = gathered(l, base), spot(l, base), []
            for a, c in enumerate(cut):
                re, im = tilt(l, here, a, fields[a], -1.0)
                pr, pi = ref.passed2[0, at, c], ref.passed2[1, at, c]
                ref.grad[1, here, c] += pr * im - pi * re
                tr, ti = ref.tr[2, 0, here, c], ref.tr[2, 1, here, c]
                blocks.append((re * tr + im * ti, im * tr - re * ti))
            scattered(l, base, blocks)
            return carry

        each_chunk(chunk)
        emit_full(y3, l, l)

    each_led(back_band)
    trade(ref.grad.at[1], ref.result.at[2], ref.grad_sent.at[1], ref.grad_got.at[1])
    columns(y3, y2, -1.0)

    def back(l):
        land(y2, l)
        inverse_full(y2.y, l, l)

        def chunk(base, here, carry):
            fields, at, blocks = gathered(l, base), spot(l, base), []
            for a, c in enumerate(cut):
                re, im = fields[a]
                pr, pi = ref.passed1[0, at, c], ref.passed1[1, at, c]
                ref.grad[0, here, c] += pr * im - pi * re
                tr, ti = ref.tr[1, 0, here, c], ref.tr[1, 1, here, c]
                blocks.append((re * tr + im * ti, im * tr - re * ti))
            scattered(l, base, blocks)
            return carry

        each_chunk(chunk)
        emit_full(y1, l, l)

    each_led(back)
    trade(ref.grad.at[0], ref.result.at[1], ref.grad_sent.at[0], ref.grad_got.at[0])
    ready("slab_own")
    phases(ref.slab_own, ref.tr.at[0])
    ref.cs[...] = jnp.zeros(ref.cs.shape, f32)

    def last(l):
        land(y1, l)
        spread(y1, l)

        def add(j, z):
            ref.cs[j] += shaped(z, l, j, -1.0)

        col_dot(ref.chi, ref.clo, add, 1.0)

    each_led(last)
    for j in range(4):
        stow(j, ref.cs[j])
    col_inverse(y0, 0)
    for mask in exit_order:
        dest = flip(place, mask)
        if mask:
            away(
                y0.stage.at[0, dest], y0.y.at[0, me], y0.sent.at[0], y0.got.at[0],
                dict(tiles=work, pat=dest),
            ).start()
        else:

            @pl.when(native)
            def _():
                local(y0.stage.at[0, dest], y0.y.at[0, me], y0.got.at[0]).start()

            @pl.when(jnp.logical_not(native))
            def _():
                away(
                    y0.stage.at[0, dest], y0.y.at[0, me], y0.sent.at[0], y0.got.at[0],
                    dict(tiles=work, pat=dest),
                ).start()

    land(y0, 0)
    inverse_full(y0.y, 0, 0)

    def leave(base, here, carry):
        fields = gathered(0, base)
        for a, c in enumerate(cut):
            tr, ti = ref.tr[0, 0, here, c], ref.tr[0, 1, here, c]
            re, im = fields[a]
            ref.grad0[here, c] = tr * im - ti * re
        return carry

    each_chunk(leave)
    final = local(ref.grad0, ref.result.at[0], ref.loads.at[len(spec.loaded)])
    final.start()

    for x, slots in (
        (x0, 1), (x1, count), (x2, count), (x3, count), (b0, 1), (b1, 1), (b2, 1), (b3, 1),
        (sums, 1), (y3, count), (y2, count), (y1, count), (y0, 1),
    ):
        drain(x, slots)
    for q in range(per):

        @pl.when(place == owners[q])
        def _():
            for jj in range(2):
                for w in range(2):
                    pupil_copy(jj, w, q).wait_send()

    for k in range(2):
        local(ref.grad.at[k], ref.result.at[k + 1], ref.grad_got.at[k]).wait()

    @pl.when(jnp.logical_not(native))
    def _():
        part = y0.stage.at[0, 0]
        local(part, part, y0.sent.at[0]).wait()
        for s in range(3):
            local(ref.slab.at[s], ref.slab.at[s], ref.slab_sent.at[s]).wait()
        for p in range(patterns):
            local(ref.measured.at[p], ref.measured.at[p], ref.count_sent.at[p]).wait()
        for k in range(2):
            local(ref.grad.at[k], ref.grad.at[k], ref.grad_sent.at[k]).wait()

    final.wait()


def body(tiles, slab_phase, pupil_phase, pupil_mask, led_code, led_freq, measured):
    devs = lax.axis_size("pat")
    slab_count, rows, size = slab_phase.shape
    patterns, count = led_code.shape
    quarter, cols, per = size // 4, size // devs, devs // 4
    band = 2 * pupil_radius
    band_cols = band // devs
    rt = row_tables(size, cols, band_cols)
    ct = col_tables(size)
    stat_rows = count + count * (count + 1) // 2 + patterns * count + patterns
    owners = [(q - pupil_radius // cols) % devs for q in range(per)]
    loads = dict(
        row_twiddle=rt.twiddle, full=rt.full,
        col_twiddle=jnp.asarray(ct.twiddle), both=jnp.asarray(ct.both), full_inv=rt.full_inv, band=rt.band,
        pupil_in=jnp.asarray(ct.band), pupil_out=jnp.asarray(ct.band_inv), band_inv=rt.band_inv,
        slab_own=slab_phase[0],
    )
    inputs = {name + "_hbm": value for name, value in loads.items()}
    inputs |= dict(phase_hbm=pupil_phase, mask_hbm=pupil_mask, slab_hbm=slab_phase, measured_hbm=measured, freq=led_freq, code=led_code)
    wide = 2 * quarter
    total = count * rows
    vmem, dma = pltpu.VMEM, pltpu.SemaphoreType.DMA
    scratch = {name: vmem(value.shape, value.dtype) for name, value in loads.items()}
    scratch |= dict(
        slab=vmem(slab_phase.shape, f32), measured=vmem(measured.shape, jnp.int32),
        phase=vmem((2, rows, pupil_radius), f32), mask=vmem((2, rows, pupil_radius), jnp.int32),
        phase_sem=dma((2,)), mask_sem=dma((2,)), own=vmem((4, 2, rows // 4, band), f32), pupil=vmem((2, band_cols, band), f32),
        tilt_c=vmem((2 * count, 1, size), f32), tilt_r=vmem((2 * count, rows, lanes), f32),
        prop=vmem((2, count, 4, quarter, lanes), f32), tr=vmem((3, 2, rows, size), f32),
        passed1=vmem((2, total, size), f32), passed2=vmem((2, total, size), f32),
        camera=vmem((2, total, size), f32), grad=vmem((2, rows, size), f32), grad0=vmem((rows, size), f32),
        hi=vmem((4, total, wide), bf16), lo=vmem((4, total, wide), bf16), zs=vmem((4, total, wide), f32),
        ghi=vmem((4 * rows, wide), bf16), glo=vmem((4 * rows, wide), bf16),
        chi=vmem((quarter, 4 * lanes), bf16), clo=vmem((quarter, 4 * lanes), bf16),
        dhi=vmem((quarter, 4 * lanes), bf16), dlo=vmem((quarter, 4 * lanes), bf16),
        cz=vmem((4, quarter, lanes), f32), cs=vmem((4, quarter, lanes), f32),
        loads=dma((len(loads) + 1,)),
        slab_sent=dma((3,)), slab_got=dma((3,)), count_sent=dma((patterns,)), count_got=dma((patterns,)),
        pupil_sent=dma((4,)), pupil_got=dma, grad_sent=dma((2,)), grad_got=dma((2,)),
    )
    block, narrow = (devs, rows, lanes), (devs, 2 * band_cols, total)
    ports = dict(x0=(1, block), x1=(count, block), x2=(count, block), x3=(count, block))
    ports |= dict(b0=(1, narrow), b1=(1, narrow), b2=(1, narrow), b3=(1, narrow))
    ports |= dict(sums=(1, (devs, -(-stat_rows // 8) * 8, lanes)))
    ports |= dict(y3=(count, block), y2=(count, block), y1=(count, block), y0=(1, block), out=(1, (8, lanes)))
    for name, (slots, shape) in ports.items():
        scratch[name + "_stage"] = vmem((slots,) + shape, f32)
        scratch[name + "_y"] = vmem((slots,) + shape, f32)
        scratch[name + "_sent"] = dma((slots,))
        scratch[name + "_got"] = dma((slots,))
    spec = Names(
        count=count, rows=rows, quarter=quarter, devs=devs, tiles=tiles, patterns=patterns,
        area=float(size * size), stat_rows=stat_rows, owners=owners, loaded=list(loads),
        names=list(inputs) + ["result"] + list(scratch),
    )
    anywhere = pl.BlockSpec(memory_space=pl.ANY)
    smem = pl.BlockSpec(memory_space=pltpu.SMEM)
    return pl.pallas_call(
        functools.partial(whole_kernel, spec),
        out_shape=jax.ShapeDtypeStruct(slab_phase.shape, f32),
        in_specs=[smem if name in ("freq", "code") else anywhere for name in inputs],
        out_specs=anywhere,
        scratch_shapes=list(scratch.values()),
        compiler_params=pltpu.CompilerParams(
            collective_id=1, has_side_effects=True, vmem_limit_bytes=67043328
        ),
        name="whole",
    )(*inputs.values())


def solution(mesh):
    in_specs = (
        P("tiles", "pat", None),
        P("pat", None),
        P("pat", None),
        P(),
        P(),
        P("tiles", "pat", None),
    )
    out_specs = P("tiles", "pat", None)

    def run(slab_phase, *others):
        devs, tiles = mesh.shape["pat"], mesh.shape["tiles"]
        size, count = slab_phase.shape[-1], others[2].shape[1]
        fits = 2 * size == lanes * devs and count * size == lanes * devs and slab_phase.shape[0] == 3 * tiles
        fits = fits and tiles == 2 and devs == len(exit_order)
        inner = functools.partial(body, tiles) if fits else plain_body
        return jax.shard_map(inner, mesh=mesh, in_specs=in_specs, out_specs=out_specs, check_vma=False)(
            slab_phase, *others
        )

    return run
```

```python
import functools
import math
import types

import jax
import jax.numpy as jnp
import numpy as np
from jax import lax
from jax.experimental import pallas as pl
from jax.experimental.pallas import tpu as pltpu
from jax.sharding import PartitionSpec as P

spread_rate = 0.3
highest = lax.Precision.HIGHEST


def frequency(grid_index, grid_size):
    return (grid_index + grid_size // 2) % grid_size - grid_size // 2


def complex_times(values, factor):
    real_part = values[0] * factor[0] - values[1] * factor[1]
    imag_part = values[0] * factor[1] + values[1] * factor[0]
    return jnp.stack([real_part, imag_part])


def dft_block(length, direction, norm_factor):
    grid_index = jnp.arange(length, dtype=jnp.int32)
    angles = (grid_index[:, None] * grid_index[None, :] % length).astype(jnp.float32) * (
        2.0 * math.pi / length
    )
    cosine = jnp.cos(angles) * norm_factor
    signed_sine = direction * jnp.sin(angles) * norm_factor
    real_rows = jnp.stack([cosine, signed_sine], 1)
    imag_rows = jnp.stack([-signed_sine, cosine], 1)
    return jnp.stack([real_rows, imag_rows], 0)


def twiddle_table(short_size, long_size, grid_size, direction):
    short_index = jnp.arange(short_size, dtype=jnp.int32)
    long_index = jnp.arange(long_size, dtype=jnp.int32)
    angles = (short_index[:, None] * long_index[None, :] % grid_size).astype(jnp.float32) * (
        2.0 * math.pi / grid_size
    )
    return jnp.stack([jnp.cos(angles), direction * jnp.sin(angles)])


def table_set(col_count, dev_count, grid_size, direction):
    short_table = dft_block(col_count, direction, 1.0)
    long_table = dft_block(dev_count, direction, 1.0 / math.sqrt(grid_size))
    return (short_table, long_table, twiddle_table(col_count, dev_count, grid_size, direction))


def to_fourier(wave_field, tables, dev_count):
    short_table, long_table, twiddles = tables
    led_count = wave_field.shape[1]
    row_count = wave_field.shape[2]
    grid_size = wave_field.shape[3]
    col_count = grid_size // dev_count
    shaped = wave_field.reshape(2, led_count, row_count, col_count, dev_count)
    sectioned = jnp.einsum("zlrmq,zmwc->wlrcq", shaped, short_table, precision=highest)
    sectioned = complex_times(sectioned, twiddles)
    outgoing = jnp.einsum("wlrcq,wqvd->dvlcr", sectioned, long_table, precision=highest)
    incoming = lax.all_to_all(
        outgoing.reshape(dev_count, -1), "pat", split_axis=0, concat_axis=0, tiled=True
    )
    incoming = incoming.reshape(dev_count, 2, led_count, col_count, row_count)
    sectioned = jnp.einsum("swlcr,wsvj->vlcrj", incoming, long_table, precision=highest)
    sectioned = complex_times(sectioned, twiddles)
    sectioned = jnp.einsum("wlcrj,wrvh->vlchj", sectioned, short_table, precision=highest)
    return sectioned.reshape(2, led_count, col_count, grid_size)


def to_space(spectrum, tables, dev_count):
    short_table, long_table, twiddles = tables
    led_count = spectrum.shape[1]
    col_count = spectrum.shape[2]
    grid_size = spectrum.shape[3]
    row_count = grid_size // dev_count
    shaped = spectrum.reshape(2, led_count, col_count, row_count, dev_count)
    sectioned = jnp.einsum("zlcmq,zmwr->wlcrq", shaped, short_table, precision=highest)
    sectioned = complex_times(sectioned, twiddles)
    outgoing = jnp.einsum("wlcrq,wqvd->dvlcr", sectioned, long_table, precision=highest)
    incoming = lax.all_to_all(
        outgoing.reshape(dev_count, -1), "pat", split_axis=0, concat_axis=0, tiled=True
    )
    incoming = incoming.reshape(dev_count, 2, led_count, col_count, row_count)
    sectioned = jnp.einsum("swlcr,wsvj->vlrcj", incoming, long_table, precision=highest)
    sectioned = complex_times(sectioned, twiddles)
    sectioned = jnp.einsum("wlrcj,wcvh->vlrhj", sectioned, short_table, precision=highest)
    return sectioned.reshape(2, led_count, row_count, grid_size)


def plain_body(slab_phase, pupil_phase, pupil_mask, led_code, led_freq, measured):
    dev_count = lax.axis_size("pat")
    position = lax.axis_index("pat")
    slab_count, row_count, grid_size = slab_phase.shape
    col_count = grid_size // dev_count
    pattern_count, led_count = led_code.shape
    area = float(grid_size * grid_size)
    forward_set = table_set(col_count, dev_count, grid_size, -1.0)
    inverse_set = table_set(col_count, dev_count, grid_size, 1.0)
    conjugate = jnp.array([1.0, -1.0], jnp.float32)[:, None, None]
    col_freq = frequency(position * col_count + jnp.arange(col_count, dtype=jnp.int32), grid_size)
    row_freq = frequency(jnp.arange(grid_size, dtype=jnp.int32), grid_size)
    radius = col_freq[:, None] * col_freq[:, None] + row_freq[None, :] * row_freq[None, :]
    cutoff = grid_size // 2 * (grid_size // 2)
    inside = radius <= cutoff
    height = jnp.sqrt(jnp.maximum(cutoff - radius, 0).astype(jnp.float32))
    phase_shift = spread_rate * (height - grid_size // 2)
    propagator = jnp.stack(
        [jnp.where(inside, jnp.cos(phase_shift), 0.0), jnp.where(inside, jnp.sin(phase_shift), 0.0)]
    )
    opening = pupil_mask.astype(jnp.float32)
    pupil = jnp.stack([opening * jnp.cos(pupil_phase), opening * jnp.sin(pupil_phase)])
    propagator_conj = propagator * conjugate
    pupil_conj = pupil * conjugate
    row_index = position * row_count + jnp.arange(row_count, dtype=jnp.int32)
    col_index = jnp.arange(grid_size, dtype=jnp.int32)
    tilt_index = (
        led_freq[:, 0][:, None, None] * row_index[None, :, None]
        + led_freq[:, 1][:, None, None] * col_index[None, None, :]
    ) % grid_size
    tilt_angle = tilt_index.astype(jnp.float32) * (2.0 * math.pi / grid_size)
    illumination = jnp.stack([jnp.cos(tilt_angle), jnp.sin(tilt_angle)])
    transmission = jnp.stack([jnp.cos(slab_phase), jnp.sin(slab_phase)])
    group_count = 1
    group_size = led_count // group_count
    wave_groups = [illumination]
    passed_groups = []
    for slab_index in range(slab_count):
        factor = transmission[:, slab_index]
        passed = [complex_times(wave_field, factor) for wave_field in wave_groups]
        passed_groups.append(passed)
        spectral_factor = propagator if slab_index < slab_count - 1 else pupil
        wave_groups = [
            to_space(
                complex_times(to_fourier(passed_field, forward_set, dev_count), spectral_factor),
                inverse_set,
                dev_count,
            )
            for passed_field in passed
        ]
    camera = wave_groups[0]
    led_power = camera[0] * camera[0] + camera[1] * camera[1]
    code_float = led_code.astype(jnp.float32)
    pattern_power = jnp.dot(
        code_float, led_power.reshape(led_count, -1), precision=highest
    ).reshape(pattern_count, row_count, grid_size)
    counts = measured.astype(jnp.float32)
    power_sum, count_sum = lax.psum(
        (jnp.sum(pattern_power, axis=(1, 2)), jnp.sum(counts, axis=(1, 2))), "pat"
    )
    mean_power = power_sum / area
    mean_count = count_sum / area
    relative = pattern_power / mean_power[:, None, None]
    misfit = relative - counts / mean_count[:, None, None]
    coupling = lax.psum(jnp.sum(misfit * relative, axis=(1, 2)), "pat") / area
    pattern_weight = (misfit - coupling[:, None, None]) / mean_power[:, None, None]
    led_weight = jnp.dot(
        code_float.T, pattern_weight.reshape(pattern_count, -1), precision=highest
    ).reshape(led_count, row_count, grid_size)
    camera_adjoint = 2.0 * led_weight[None] * camera
    adjoint_groups = [camera_adjoint]
    gradients = [None] * slab_count
    for slab_index in range(slab_count - 1, -1, -1):
        spectral_factor = pupil_conj if slab_index == slab_count - 1 else propagator_conj
        back_groups = [
            to_space(
                complex_times(to_fourier(adjoint_field, forward_set, dev_count), spectral_factor),
                inverse_set,
                dev_count,
            )
            for adjoint_field in adjoint_groups
        ]
        gradient = jnp.zeros((row_count, grid_size), jnp.float32)
        for passed_field, back_field in zip(passed_groups[slab_index], back_groups):
            gradient = jnp.sum(
                passed_field[0] * back_field[1] - passed_field[1] * back_field[0], axis=0
            )
        gradients[slab_index] = gradient
        if slab_index > 0:
            release = transmission[:, slab_index] * conjugate
            adjoint_groups = [complex_times(back_field, release) for back_field in back_groups]
    return jnp.stack(gradients)


class Names(types.SimpleNamespace):
    def __getitem__(self, name):
        return getattr(self, name)


pupil_radius = 128
lanes = 128
f32 = jnp.float32
bf16 = jnp.bfloat16


def halves(table):
    table32 = np.asarray(table, np.float32)
    high = table32.astype(bf16)
    low = (table32 - high.astype(np.float32)).astype(bf16)
    return np.stack([high, low])


def row_tables(size, block, band_block):
    quarter = size // 4
    pos = np.arange(quarter)
    angle = 2.0 * np.pi * ((pos[:, None] * pos[None, :]) % quarter) / quarter
    cosine = np.cos(angle) / math.sqrt(size)
    sine = np.sin(angle) / math.sqrt(size)

    def forward(freqs, width):
        parts = []
        for first in range(0, len(freqs), width):
            pick = freqs[first : first + width] % quarter
            left = np.concatenate([cosine[:, pick], sine[:, pick]], 0)
            right = np.concatenate([-sine[:, pick], cosine[:, pick]], 0)
            parts.append(np.concatenate([left, right], 1))
        return np.concatenate(parts, 1)

    full = forward(pos, block)
    reach = pupil_radius // 4
    band = forward(np.arange(-reach, reach), band_block)
    theta = 2.0 * np.pi * (np.arange(4)[:, None] * pos[None, :]) / size
    twiddle = np.concatenate([np.cos(theta), np.sin(theta)], 0).astype(np.float32)
    return Names(
        full=jnp.asarray(halves(full)),
        full_inv=jnp.asarray(halves(full.T)),
        band=jnp.asarray(halves(band)),
        band_inv=jnp.asarray(halves(band.T)),
        twiddle=jnp.asarray(twiddle),
    )


def col_tables(size):
    quarter = size // 4
    pos = np.arange(quarter)
    angle = 2.0 * np.pi * ((pos[:, None] * pos[None, :]) % quarter) / quarter
    both = np.concatenate([np.cos(angle), np.sin(angle)], 0) / math.sqrt(size)
    theta = 2.0 * np.pi * (np.arange(1, 4)[:, None] * pos[None, :]) / size
    twiddle = np.stack([np.cos(theta), np.sin(theta)]).astype(np.float32)
    twiddle = np.ascontiguousarray(np.broadcast_to(twiddle[..., None], twiddle.shape + (lanes,)))
    freqs = np.arange(-pupil_radius, pupil_radius)
    angle = 2.0 * np.pi * ((np.arange(size)[:, None] * freqs[None, :]) % size) / size
    cosine = np.cos(angle) / math.sqrt(size)
    sine = np.sin(angle) / math.sqrt(size)
    band = halves(np.concatenate([cosine, sine], 1))
    band_inv = halves(np.concatenate([cosine.T, sine.T], 1))
    return Names(both=halves(both), twiddle=twiddle, band=band, band_inv=band_inv)


def split(value):
    high = value.astype(bf16)
    return high, (value - high.astype(f32)).astype(bf16)


def dot3(left, right):
    def dot(a, b):
        return jnp.dot(a, b, preferred_element_type=f32)

    return dot(left[0], right[0]) + (dot(left[0], right[1]) + dot(left[1], right[0]))


def turn(value):
    rolled = pltpu.roll(value, lanes // 2, 1)
    lane = lax.broadcasted_iota(jnp.int32, value.shape, 1)
    return jnp.where(lane < lanes // 2, rolled, -rolled)


def row_spread(blocks, twiddle_ref):
    (r0, i0), (r1, i1), (r2, i2), (r3, i3) = blocks
    sr, si, tr, ti = r0 + r2, i0 + i2, r1 + r3, i1 + i3
    dr, di, er, ei = r0 - r2, i0 - i2, r1 - r3, i1 - i3
    mixed = [(sr + tr, si + ti), (dr + ei, di - er), (sr - tr, si - ti), (dr - ei, di + er)]
    out = [mixed[0]]
    for j in range(1, 4):
        cosine, sine = twiddle_ref[j : j + 1, :], twiddle_ref[4 + j : 5 + j, :]
        re, im = mixed[j]
        out.append((re * cosine + im * sine, im * cosine - re * sine))
    return out


def row_gather(parts, twiddle_ref):
    g = [parts[0]]
    for j in range(1, 4):
        cosine, sine = twiddle_ref[j : j + 1, :], twiddle_ref[4 + j : 5 + j, :]
        re, im = parts[j]
        g.append((re * cosine - im * sine, im * cosine + re * sine))
    (r0, i0), (r1, i1), (r2, i2), (r3, i3) = g
    sr, si, tr, ti = r0 + r2, i0 + i2, r1 + r3, i1 + i3
    dr, di, er, ei = r0 - r2, i0 - i2, r1 - r3, i1 - i3
    return [(sr + tr, si + ti), (dr - ei, di + er), (sr - tr, si - ti), (dr + ei, di - er)]


mesh_ids = pl.DeviceIdType.MESH
far_first = (14, 15, 6, 7, 10, 11, 12, 13, 2, 3, 4, 5, 8, 9, 1, 0)


def flip(index, mask):
    out = index
    for bit in (1, 2, 4, 8):
        if mask & bit:
            out = out + bit - 2 * bit * lax.rem(index // bit, 2)
    return out


def whole_kernel(spec, *refs):
    ref = Names(**dict(zip(spec.names, refs)))
    count, rows, quarter, devs, patterns = spec.count, spec.rows, spec.quarter, spec.devs, spec.patterns
    size, per, half, step = 4 * quarter, devs // 4, devs // 2, 16
    tile, place = lax.axis_index("tiles"), lax.axis_index("pat")
    work = place // half
    me = half * tile + lax.rem(place, half)
    native = tile == work
    foreign = jnp.logical_not(native)
    other = dict(tiles=1 - tile, pat=lax.rem(place + half, devs))

    def member(index):
        return dict(tiles=index // half, pat=work * half + lax.rem(index, half))

    barrier = pltpu.get_barrier_semaphore()
    everyone = spec.tiles * devs

    def signal(hop, carry):
        target = lax.rem(tile * devs + place + hop, everyone)
        pl.semaphore_signal(
            barrier, inc=1, device_id=dict(tiles=target // devs, pat=lax.rem(target, devs)),
            device_id_type=mesh_ids,
        )
        return carry

    lax.fori_loop(1, everyone, signal, 0)

    def local(source, target, sem):
        return pltpu.make_async_copy(source, target, sem)

    def away(source, target, sent, got, device):
        return pltpu.make_async_remote_copy(
            src_ref=source, dst_ref=target, send_sem=sent, recv_sem=got, device_id=device,
            device_id_type=mesh_ids,
        )

    def fetch(name):
        source = ref.slab_hbm.at[0] if name == "slab_own" else ref[name + "_hbm"]
        return local(source, ref[name], ref.loads.at[spec.loaded.index(name)])

    reach = pupil_radius
    spans = (slice(size - reach, size), slice(0, reach))

    def near(name, k):
        return local(ref[name + "_hbm"].at[:, spans[k]], ref[name].at[k], ref[name + "_sem"].at[k])

    for name in ("phase", "mask"):
        for k in range(2):
            near(name, k).start()
    for name in spec.loaded:
        fetch(name).start()

    def ready(name):
        fetch(name).wait()

    share = rows // 2
    neighbour = dict(tiles=1 - tile, pat=place)
    across = dict(tiles=tile, pat=lax.rem(place + half, devs))

    sources = dict(slab=ref.slab_hbm, lit=ref.lit_own, grad=ref.grad)
    targets = dict(slab=ref.slab, lit=ref.lit, grad=ref.result.at[1:3])
    part = dict(slab=3, lit=spec.sets, grad=2)

    def semaphore(name, kind, k):
        return ref[name + kind].at[k]

    def direct(name, k):
        return away(
            sources[name].at[k, :share], targets[name].at[k, :share], semaphore(name, "_sent", k),
            semaphore(name, "_got", k), other,
        )

    def hop(name, k):
        return away(
            sources[name].at[k, share:], ref[name + "_relay"].at[k], semaphore(name, "_sent", k),
            semaphore(name, "_via", k), neighbour,
        )

    def onward(name, k):
        return away(
            ref[name + "_relay"].at[k], targets[name].at[k, share:], semaphore(name, "_sent", k),
            semaphore(name, "_late" if name == "slab" else "_got", k), across,
        )

    def trade_native(name, k):
        @pl.when(native)
        def _():
            if name == "slab":
                for span, kind in ((pl.ds(0, share), "_got"), (pl.ds(share, share), "_late")):
                    local(sources[name].at[k, span], targets[name].at[k, span], semaphore(name, kind, k)).start()
            else:
                local(sources[name].at[k], targets[name].at[k], semaphore(name, "_got", k)).start()

    def trade_foreign(name, *blocks):
        @pl.when(foreign)
        def _():
            for k in blocks:
                direct(name, k).start()
                hop(name, k).start()

    def forward_on(name, *blocks):
        @pl.when(native)
        def _():
            for k in blocks:
                hop(name, k).wait_recv()
                onward(name, k).start()

    def traded(name, k):
        whole = targets[name].at[k]
        if name == "slab":
            halves = (whole.at[:share], whole.at[share:])
            local(halves[0], halves[0], semaphore(name, "_got", k)).wait()
            local(halves[1], halves[1], semaphore(name, "_late", k)).wait()
        else:
            local(whole, whole, semaphore(name, "_got", k)).wait()

    def trade_ends(name):
        for k in range(part[name]):

            @pl.when(native)
            def _():
                onward(name, k).wait_send()

            @pl.when(foreign)
            def _():
                whole = sources[name].at[k]
                local(whole, whole, semaphore(name, "_sent", k)).wait()

    def port(name):
        return Names(
            stage=ref[name + "_stage"], y=ref[name + "_y"], sent=ref[name + "_sent"], got=ref[name + "_got"]
        )

    def push_one(x, slot, mask, span=None):
        dest = flip(me, mask)
        source = x.stage.at[slot, dest] if span is None else x.stage.at[slot, dest, span]
        target = x.y.at[slot, me] if span is None else x.y.at[slot, me, span]
        if mask:
            away(source, target, x.sent.at[slot], x.got.at[slot], member(dest)).start()
        else:
            local(source, target, x.got.at[slot]).start()

    def push(x, slot):
        for mask in far_first:
            push_one(x, slot, mask)

    def leave_one(x, slot, mask):
        dest = flip(place, mask)

        def start_away():
            away(
                x.stage.at[slot, dest], x.y.at[slot, me], x.sent.at[slot], x.got.at[slot],
                dict(tiles=work, pat=dest),
            ).start()

        if mask:
            start_away()
        else:

            @pl.when(native)
            def _():
                local(x.stage.at[slot, dest], x.y.at[slot, me], x.got.at[slot]).start()

            pl.when(foreign)(start_away)

    def land(x, slot):
        local(x.y.at[slot], x.y.at[slot], x.got.at[slot]).wait()

    def drain(x, slots):
        for slot in range(slots):
            part = x.stage.at[slot, pl.ds(0, devs - 1)]
            local(part, part, x.sent.at[slot]).wait()

    hi, lo, zs = ref.hi, ref.lo, ref.zs
    cut = [slice(a * quarter, (a + 1) * quarter) for a in range(4)]

    def spot(l, base):
        return pl.ds(pl.multiple_of(l * rows + base, step), step)

    def each_chunk(chunk, carry=0):
        def at_chunk(i, carry):
            base = pl.multiple_of(i * step, step)
            return chunk(base, pl.ds(base, step), carry)

        return lax.fori_loop(0, rows // step, at_chunk, carry)

    def gathered(l, base):
        at = spot(l, base)
        parts = [(zs[j, at, :quarter], zs[j, at, quarter:]) for j in range(4)]
        return row_gather(parts, ref.row_twiddle)

    def scattered(l, base, blocks):
        at = spot(l, base)
        for j, (re, im) in enumerate(row_spread(blocks, ref.row_twiddle)):
            high, low = split(re)
            hi[j, at, :quarter] = high
            lo[j, at, :quarter] = low
            high, low = split(im)
            hi[j, at, quarter:] = high
            lo[j, at, quarter:] = low

    def led_rows(l):
        return pl.ds(pl.multiple_of(l * rows, rows), rows)

    def inverse_full(y, slot, l):
        for j in range(4):
            for q in range(per):
                high, low = split(y[slot, per * j + q])
                ref.ghi[j * rows : (j + 1) * rows, q * lanes : (q + 1) * lanes] = high
                ref.glo[j * rows : (j + 1) * rows, q * lanes : (q + 1) * lanes] = low
        value = dot3((ref.ghi[...], ref.glo[...]), (ref.full_inv[0], ref.full_inv[1]))
        zs[:, led_rows(l), :] = value.reshape(4, rows, 2 * quarter)

    def emit_full(x, slot, l):
        left = [part[:, led_rows(l), :].reshape(4 * rows, 2 * quarter) for part in (hi, lo)]
        value = dot3(left, (ref.full[0], ref.full[1]))
        for j in range(4):
            for q in range(per):
                x.stage[slot, per * j + q] = value[j * rows : (j + 1) * rows, q * lanes : (q + 1) * lanes]
        push(x, slot)

    total = count * rows

    def inverse_band(x):
        for j in range(4):
            block = x.y[0, per * j : per * (j + 1)].reshape(-1, total)
            zs[j, :, :] = dot3(split(block.T), (ref.band_inv[0], ref.band_inv[1]))

    def emit_band(x):
        for j in range(4):
            value = dot3((hi[j], lo[j]), (ref.band[0], ref.band[1]))
            flipped = value.T
            deep = flipped.shape[0] // per
            for q in range(per):
                x.stage[0, per * j + q] = flipped[q * deep : (q + 1) * deep]
        push(x, 0)

    def tilt(l, here, a, value, sign):
        rc, rs = ref.tilt_r[2 * l, here, :], ref.tilt_r[2 * l + 1, here, :]
        cc, cs = ref.tilt_c[2 * l, :, cut[a]], ref.tilt_c[2 * l + 1, :, cut[a]]
        rc = jnp.concatenate([rc] * (quarter // lanes), 1)
        rs = jnp.concatenate([rs] * (quarter // lanes), 1)
        er = rc * cc - rs * cs
        ei = sign * (rc * cs + rs * cc)
        re, im = value
        return re * er - im * ei, re * ei + im * er

    def spread(x, slot):
        def at_part(i, carry):
            here = pl.ds(pl.multiple_of(i * rows, rows), rows)
            x0, x1, x2, x3 = [x.y[slot, per * a + i] for a in range(4)]
            s, t, d, e = x0 + x2, x1 + x3, x0 - x2, turn(x1 - x3)
            for j, value in enumerate((s + t, d + e, s - t, d - e)):
                if j:
                    value = value * ref.col_twiddle[0, j - 1, here, :] + turn(value) * ref.col_twiddle[1, j - 1, here, :]
                high, low = split(value)
                ref.chi[here, j * lanes : (j + 1) * lanes] = high
                ref.clo[here, j * lanes : (j + 1) * lanes] = low
            return carry

        lax.fori_loop(0, per, at_part, 0)

    def col_dot(high, low, take, sign):
        for pair in range(2):
            at = slice(2 * pair * lanes, 2 * (pair + 1) * lanes)
            y = dot3((ref.both[0], ref.both[1]), (high[:, at], low[:, at]))
            for k in range(2):
                at = slice(k * lanes, (k + 1) * lanes)
                take(2 * pair + k, y[:quarter, at] + sign * turn(y[quarter:, at]))

    def shaped(z, l, j, sign):
        return z * ref.prop[0, l, j] - sign * (turn(z) * ref.prop[1, l, j])

    def stow(j, value):
        high, low = split(value)
        ref.dhi[:, j * lanes : (j + 1) * lanes] = high
        ref.dlo[:, j * lanes : (j + 1) * lanes] = low

    def col_inverse(x, slot, send=push_one, far_parts=(3, 1, 2, 0)):
        def take(j, value):
            if j:
                value = value * ref.col_twiddle[0, j - 1] - turn(value) * ref.col_twiddle[1, j - 1]
            ref.cz[j] = value

        col_dot(ref.dhi, ref.dlo, take, -1.0)
        home = lax.rem(me, per)
        for bits in (3, 2, 1, 0):
            i = flip(home, bits)
            here = pl.ds(pl.multiple_of(i * rows, rows), rows)
            g0, g1, g2, g3 = [ref.cz[j, here, :] for j in range(4)]
            s, t, d, e = g0 + g2, g1 + g3, g0 - g2, turn(g1 - g3)
            for a, value in enumerate((s + t, d - e, s - t, d + e)):
                x.stage[slot, per * a + i] = value
            for far in far_parts:
                send(x, slot, per * far + bits)

    def each_led(stage):
        def at_led(l, carry):
            stage(l)
            return carry

        lax.fori_loop(0, count, at_led, 0)

    def columns(x, out, sign):
        def stage(l):
            land(x, l)
            spread(x, l)
            col_dot(ref.chi, ref.clo, lambda j, z: stow(j, shaped(z, l, j, sign)), 1.0)
            col_inverse(out, l)

        each_led(stage)

    def pupil_columns(x, out, sign):
        land(x, 0)
        middle = lanes // 2
        lane = lax.broadcasted_iota(jnp.int32, x.y.shape[2:], 1)
        pieces = [[], []]
        for s in range(0, devs, 2):
            even, odd = x.y[0, s], x.y[0, s + 1]
            pieces[0].append(jnp.where(lane < middle, even, pltpu.roll(odd, middle, 1)))
            pieces[1].append(jnp.where(lane < middle, pltpu.roll(even, middle, 1), odd))
        field = jnp.concatenate([jnp.concatenate(p, 1) for p in pieces], 0)
        wide = ref.pupil_in.shape[2] // 2
        deep = ref.pupil_out.shape[2] // 2
        cols = x.y.shape[2] // 2
        both = dot3(split(field), (ref.pupil_in[0], ref.pupil_in[1]))
        scaled = []
        for l in range(count):
            re = slice(2 * l * cols, (2 * l + 1) * cols)
            im = slice((2 * l + 1) * cols, (2 * l + 2) * cols)
            yr = both[re, :wide] + both[im, wide:]
            yi = both[im, :wide] - both[re, wide:]
            pr, pi = ref.pupil[0], sign * ref.pupil[1]
            scaled += [yr * pr - yi * pi, yr * pi + yi * pr]
        both = dot3(split(jnp.concatenate(scaled, 0)), (ref.pupil_out[0], ref.pupil_out[1]))
        found = []
        for l in range(count):
            re = slice(2 * l * cols, (2 * l + 1) * cols)
            im = slice((2 * l + 1) * cols, (2 * l + 2) * cols)
            found.append(
                jnp.concatenate(
                    [both[re, :deep] - both[im, deep:], both[im, :deep] + both[re, deep:]], 0
                )
            )
        for s in range(0, devs, 2):
            at = slice(s * middle, s * middle + lanes)
            first, second = found[0][:, at], found[1][:, at]
            out.stage[0, s] = jnp.where(lane < middle, first, pltpu.roll(second, middle, 1))
            out.stage[0, s + 1] = jnp.where(lane < middle, pltpu.roll(first, middle, 1), second)
        push(out, 0)

    def phases(source, target):
        def chunk(base, here, carry):
            phase = source[here, :]
            target[0, here, :] = jnp.cos(phase)
            target[1, here, :] = jnp.sin(phase)
            return carry

        each_chunk(chunk)

    def fold(value):
        total_rows = value[:8]
        for k in range(1, value.shape[0] // 8):
            total_rows = total_rows + value[8 * k : 8 * k + 8]
        out = total_rows[:, :lanes]
        for k in range(1, value.shape[1] // lanes):
            out = out + total_rows[:, lanes * k : lanes * (k + 1)]
        return out

    def fold_all(p):
        def chunk(base, here, carry):
            return carry + fold(ref.measured[p, here, :].astype(f32))

        return jnp.sum(each_chunk(chunk, jnp.zeros((8, lanes), f32)), 0, keepdims=True)

    def slab_phases(s):
        traded("slab", s)
        phases(ref.slab.at[s], ref.tr.at[s])

    for k in range(3):
        trade_native("slab", k)
    turn_size = 2.0 * math.pi / size
    col = lax.broadcasted_iota(jnp.int32, (8, size), 1)
    row = me * rows + lax.broadcasted_iota(jnp.int32, (rows, lanes), 0)
    for l in range(count):
        for index, freq, tilts in ((col, ref.freq[l, 1], ref.tilt_c), (row, ref.freq[l, 0], ref.tilt_r)):
            angle = jnp.bitwise_and(index * freq, size - 1).astype(f32) * turn_size
            deep = tilts.shape[1]
            tilts[2 * l] = jnp.cos(angle)[:deep]
            tilts[2 * l + 1] = jnp.sin(angle)[:deep]

    pl.semaphore_wait(barrier, everyone - 1)
    trade_foreign("slab", 0, 1, 2)
    ready("row_twiddle")
    ready("full")
    x0, x1, x2, x3 = port("x0"), port("x1"), port("x2"), port("x3")

    def enter(first, count_rows):
        def chunk(i, carry):
            base = pl.multiple_of(first + i * step, step)
            here = pl.ds(base, step)
            blocks = []
            for c in cut:
                phase = ref.slab[0, here, c]
                blocks.append((jnp.cos(phase), jnp.sin(phase)))
            scattered(0, base, blocks)
            return carry

        lax.fori_loop(0, count_rows // step, chunk, 0)
        span = pl.ds(first, count_rows)
        left = [part[:, span, :].reshape(4 * count_rows, 2 * quarter) for part in (hi, lo)]
        value = dot3(left, (ref.full[0], ref.full[1]))
        for j in range(4):
            for q in range(per):
                x0.stage[0, per * j + q, span] = value[
                    j * count_rows : (j + 1) * count_rows, q * lanes : (q + 1) * lanes
                ]
        for mask in far_first:
            push_one(x0, 0, mask, span)

    @pl.when(native)
    def _():
        traded("slab", 0)
        enter(0, rows)


    for name in ("phase", "mask"):
        for k in range(2):
            near(name, k).wait()
    for j in range(4):
        line = pl.ds(j, rows // 4, stride=4)
        for k in range(2):
            opening = ref.mask[k, line, :].astype(f32)
            angle = ref.phase[k, line, :]
            at = slice(k * reach, (k + 1) * reach)
            ref.own[j, 0, :, at] = opening * jnp.cos(angle)
            ref.own[j, 1, :, at] = opening * jnp.sin(angle)
    owners = spec.owners

    def pupil_copy(jj, w, q):
        return away(
            ref.own.at[2 * tile + jj], ref.pupil, ref.pupil_sent.at[2 * jj + w], ref.pupil_got,
            dict(tiles=tile, pat=w * half + jj * per + q),
        )

    for q in range(per):

        @pl.when(place == owners[q])
        def _():
            for jj in range(2):
                for w in range(2):
                    pupil_copy(jj, w, q).start()

    forward_on("slab", 0)
    cutoff = size // 2 * (size // 2)

    def centred(index):
        return jnp.where(index >= size // 2, index - size, index)

    def spectrum(i, carry):
        here = pl.ds(pl.multiple_of(i * step, step), step)
        row = lax.broadcasted_iota(jnp.int32, (step, lanes), 0) + i * step
        lane = lax.broadcasted_iota(jnp.int32, (step, lanes), 1)
        lane = jnp.where(lane < lanes // 2, lane, lane - lanes // 2)
        col = 4 * (lax.rem(me, per) * (lanes // 2) + lane) + me // per
        for l in range(count):
            v = centred(col + ref.freq[l, 1])
            for j in range(4):
                u = centred(4 * row + j + ref.freq[l, 0])
                radius = u * u + v * v
                inside = radius <= cutoff
                height = jnp.sqrt(jnp.maximum(cutoff - radius, 0).astype(f32))
                shift = spread_rate * (height - float(size // 2))
                ref.prop[0, l, j, here, :] = jnp.where(inside, jnp.cos(shift), 0.0)
                ref.prop[1, l, j, here, :] = jnp.where(inside, jnp.sin(shift), 0.0)
        return carry

    lax.fori_loop(0, quarter // step // 2, spectrum, 0)
    forward_on("slab", 1)
    lax.fori_loop(quarter // step // 2, quarter // step, spectrum, 0)

    @pl.when(foreign)
    def _():
        direct("slab", 0).wait_recv()
        enter(0, share)
        onward("slab", 0).wait_recv()
        enter(share, rows - share)


    ready("measured")
    counts = port("counts")
    lines = [fold_all(p) for p in range(patterns)]
    lines.append(jnp.zeros((counts.stage.shape[2] - patterns, lanes), f32))
    lines = jnp.concatenate(lines, 0)
    for d in range(devs):
        counts.stage[0, d] = lines
    for mask in far_first:
        dest = flip(place, mask)
        if mask:
            away(
                counts.stage.at[0, dest], counts.y.at[0, place], counts.sent.at[0], counts.got.at[0],
                dict(tiles=tile, pat=dest),
            ).start()
        else:
            local(counts.stage.at[0, dest], counts.y.at[0, place], counts.got.at[0]).start()
    forward_on("slab", 2)
    ready("col_twiddle")
    ready("both")
    ready("full_inv")
    land(x0, 0)
    spread(x0, 0)

    def keep_spectrum(j, z):
        ref.cs[j] = z

    col_dot(ref.chi, ref.clo, keep_spectrum, 1.0)

    def first(l):
        for j in range(4):
            stow(j, shaped(ref.cs[j], l, j, 1.0))
        col_inverse(x1, l)

    each_led(first)
    land(counts, 0)
    count_sum = jnp.sum(jnp.sum(counts.y[0], 0), 1, keepdims=True)
    area = spec.area
    code = [[ref.code[l, p].astype(f32) for l in range(count)] for p in range(patterns)]
    lit_sets = [[l for l in range(count) if (c + 1) >> l & 1] for c in range(spec.sets)]
    member_of = []
    for leds in lit_sets:
        member_of.append([])
        for p in range(patterns):
            is_in = 1.0
            for l in range(count):
                is_in = is_in * (code[p][l] if l in leds else 1.0 - code[p][l])
            member_of[-1].append(is_in)
    share_of = [[member_of[c][p] * (area / count_sum[p : p + 1]) for p in range(patterns)] for c in range(spec.sets)]

    def gather_counts(base, here, carry):
        for c in cut:
            seen = [ref.measured[p, here, c].astype(f32) for p in range(patterns)]
            for k in range(spec.sets):
                ref.lit_own[k, here, c] = sum(share_of[k][p] * seen[p] for p in range(patterns))
        return carry

    each_chunk(gather_counts)
    for k in range(spec.sets):
        trade_native("lit", k)
    slab_phases(1)

    def forward(l):
        land(x1, l)
        inverse_full(x1.y, l, l)

        def chunk(base, here, carry):
            fields, at, blocks = gathered(l, base), spot(l, base), []
            for a, c in enumerate(cut):
                tr, ti = ref.tr[1, 0, here, c], ref.tr[1, 1, here, c]
                re, im = fields[a]
                re, im = re * tr - im * ti, re * ti + im * tr
                ref.passed1[0, at, c] = re
                ref.passed1[1, at, c] = im
                blocks.append((re, im))
            scattered(l, base, blocks)
            return carry

        each_chunk(chunk)
        emit_full(x2, l, l)

    each_led(forward)
    trade_foreign("lit", 0)
    columns(x2, x3, 1.0)
    trade_foreign("lit", *range(1, spec.sets))
    forward_on("lit", 0)
    slab_phases(2)

    def forward_band(l):
        land(x3, l)
        inverse_full(x3.y, l, l)

        def chunk(base, here, carry):
            fields, at, blocks = gathered(l, base), spot(l, base), []
            for a, c in enumerate(cut):
                tr, ti = ref.tr[2, 0, here, c], ref.tr[2, 1, here, c]
                re, im = fields[a]
                re, im = re * tr - im * ti, re * ti + im * tr
                ref.passed2[0, at, c] = re
                ref.passed2[1, at, c] = im
                blocks.append(tilt(l, here, a, (re, im), 1.0))
            scattered(l, base, blocks)
            return carry

        each_chunk(chunk)

    each_led(forward_band)
    forward_on("lit", *range(1, spec.sets))
    b0, b1, b2, b3, sums = port("b0"), port("b1"), port("b2"), port("b3"), port("sums")
    ready("band")
    emit_band(b0)
    ready("pupil_in")
    ready("pupil_out")
    local(ref.pupil, ref.pupil, ref.pupil_got).wait()
    pupil_columns(b0, b1, 1.0)
    for k in range(spec.sets):
        traded("lit", k)
    ready("band_inv")
    land(b1, 0)
    inverse_band(b1)

    def measure(base, here, carry):
        fields = [gathered(l, base) for l in range(count)]
        adds = [0.0] * spec.stat_rows
        for a, c in enumerate(cut):
            power = []
            for l in range(count):
                at = spot(l, base)
                re, im = fields[l][a]
                ref.camera[0, at, c] = re
                ref.camera[1, at, c] = im
                power.append(re * re + im * im)
            values = list(power)
            for l in range(count):
                for m in range(l, count):
                    values.append(power[l] * power[m])
            for k, leds in enumerate(lit_sets):
                seen = ref.lit[k, here, c]
                values += [seen * power[l] for l in leds]
            for k, value in enumerate(values):
                adds[k] = adds[k] + fold(value)
        return tuple(x + y for x, y in zip(carry, adds))

    stats = each_chunk(measure, tuple(jnp.zeros((8, lanes), f32) for _ in range(spec.stat_rows)))
    packed = [jnp.sum(line, 0, keepdims=True) for line in stats]
    packed.append(jnp.zeros((sums.stage.shape[2] - len(packed), lanes), f32))
    packed = jnp.concatenate(packed, 0)
    for d in range(devs):
        sums.stage[0, d] = packed
    push(sums, 0)
    land(sums, 0)
    added = jnp.sum(jnp.sum(sums.y[0], 0), 1, keepdims=True)
    pairs = [(l, m) for l in range(count) for m in range(l, count)]
    cross_row = count + len(pairs)
    inverse_mean, number, couple = [], [], []
    for k, leds in enumerate(lit_sets):
        mean = sum(added[l : l + 1] for l in leds) / area
        members = sum(member_of[k])
        inverse = jnp.where(members > 0.0, 1.0 / mean, 0.0)
        square = 0.0
        for at, (l, m) in enumerate(pairs):
            if l in leds and m in leds:
                square = square + (1.0 if l == m else 2.0) * added[count + at : count + at + 1]
        cross = sum(added[cross_row + i : cross_row + i + 1] for i in range(len(leds)))
        cross_row += len(leds)
        inverse_mean.append(inverse)
        number.append(members * inverse)
        couple.append((members * square * inverse * inverse - cross * inverse) / area)

    def weigh(base, here, carry):
        outgoing = [[] for _ in range(count)]
        for a, c in enumerate(cut):
            camera, power = [], []
            for l in range(count):
                at = spot(l, base)
                re, im = ref.camera[0, at, c], ref.camera[1, at, c]
                camera.append((re, im))
                power.append(re * re + im * im)
            weight = [0.0] * count
            for k, leds in enumerate(lit_sets):
                lit = sum(power[l] for l in leds)
                pull = (lit * number[k] - ref.lit[k, here, c] - couple[k]) * inverse_mean[k]
                for l in leds:
                    weight[l] = weight[l] + pull
            for l in range(count):
                scale = 2.0 * weight[l]
                outgoing[l].append((scale * camera[l][0], scale * camera[l][1]))
        for l in range(count):
            scattered(l, base, outgoing[l])
        return carry

    each_chunk(weigh)
    emit_band(b2)
    pupil_columns(b2, b3, -1.0)
    land(b3, 0)
    inverse_band(b3)
    y3, y2, y1, y0 = port("y3"), port("y2"), port("y1"), port("y0")
    ref.grad[...] = jnp.zeros(ref.grad.shape, f32)

    def back_band(l):
        def chunk(base, here, carry):
            fields, at, blocks = gathered(l, base), spot(l, base), []
            for a, c in enumerate(cut):
                re, im = tilt(l, here, a, fields[a], -1.0)
                pr, pi = ref.passed2[0, at, c], ref.passed2[1, at, c]
                ref.grad[1, here, c] += pr * im - pi * re
                tr, ti = ref.tr[2, 0, here, c], ref.tr[2, 1, here, c]
                blocks.append((re * tr + im * ti, im * tr - re * ti))
            scattered(l, base, blocks)
            return carry

        each_chunk(chunk)

        @pl.when(l == count - 1)
        def _():
            trade_native("grad", 1)
            trade_foreign("grad", 1)

        emit_full(y3, l, l)

    each_led(back_band)
    columns(y3, y2, -1.0)
    forward_on("grad", 1)

    def back(l):
        land(y2, l)
        inverse_full(y2.y, l, l)

        def chunk(base, here, carry):
            fields, at, blocks = gathered(l, base), spot(l, base), []
            for a, c in enumerate(cut):
                re, im = fields[a]
                pr, pi = ref.passed1[0, at, c], ref.passed1[1, at, c]
                ref.grad[0, here, c] += pr * im - pi * re
                tr, ti = ref.tr[1, 0, here, c], ref.tr[1, 1, here, c]
                blocks.append((re * tr + im * ti, im * tr - re * ti))
            scattered(l, base, blocks)
            return carry

        each_chunk(chunk)

        @pl.when(l == count - 1)
        def _():
            trade_native("grad", 0)
            trade_foreign("grad", 0)

        emit_full(y1, l, l)

    each_led(back)
    ready("slab_own")
    phases(ref.slab_own, ref.tr.at[0])
    ref.cs[...] = jnp.zeros(ref.cs.shape, f32)

    def last(l):
        land(y1, l)
        spread(y1, l)

        def add(j, z):
            ref.cs[j] += shaped(z, l, j, -1.0)

        col_dot(ref.chi, ref.clo, add, 1.0)

    last(0)
    forward_on("grad", 0)
    lax.fori_loop(1, count, lambda l, carry: last(l) or carry, 0)
    for j in range(4):
        stow(j, ref.cs[j])
    col_inverse(y0, 0, leave_one, (3, 2, 1, 0))
    land(y0, 0)
    inverse_full(y0.y, 0, 0)

    def leave(base, here, carry):
        fields = gathered(0, base)
        for a, c in enumerate(cut):
            tr, ti = ref.tr[0, 0, here, c], ref.tr[0, 1, here, c]
            re, im = fields[a]
            ref.grad0[here, c] = tr * im - ti * re
        return carry

    each_chunk(leave)
    final = local(ref.grad0, ref.result.at[0], ref.loads.at[len(spec.loaded)])
    final.start()

    for x, slots in (
        (x0, 1), (x1, count), (x2, count), (x3, count), (b0, 1), (b1, 1), (b2, 1), (b3, 1),
        (sums, 1), (counts, 1), (y3, count), (y2, count), (y1, count), (y0, 1),
    ):
        drain(x, slots)
    for q in range(per):

        @pl.when(place == owners[q])
        def _():
            for jj in range(2):
                for w in range(2):
                    pupil_copy(jj, w, q).wait_send()

    for name in part:
        trade_ends(name)
    for k in range(2):
        traded("grad", k)

    @pl.when(foreign)
    def _():
        block = y0.stage.at[0, 0]
        local(block, block, y0.sent.at[0]).wait()

    final.wait()


def body(tiles, slab_phase, pupil_phase, pupil_mask, led_code, led_freq, measured):
    devs = lax.axis_size("pat")
    slab_count, rows, size = slab_phase.shape
    patterns, count = led_code.shape
    quarter, cols, per = size // 4, size // devs, devs // 4
    band = 2 * pupil_radius
    band_cols = band // devs
    rt = row_tables(size, cols, band_cols)
    ct = col_tables(size)
    sets = 2**count - 1
    stat_rows = count + count * (count + 1) // 2 + count * 2 ** (count - 1)
    owners = [(q - pupil_radius // cols) % devs for q in range(per)]
    loads = dict(
        row_twiddle=rt.twiddle, full=rt.full,
        col_twiddle=jnp.asarray(ct.twiddle), both=jnp.asarray(ct.both), full_inv=rt.full_inv, band=rt.band,
        pupil_in=jnp.asarray(ct.band), pupil_out=jnp.asarray(ct.band_inv), band_inv=rt.band_inv, measured=measured,
    )
    inputs = {name + "_hbm": value for name, value in loads.items()}
    inputs |= dict(phase_hbm=pupil_phase, mask_hbm=pupil_mask, slab_hbm=slab_phase, freq=led_freq, code=led_code.T)
    wide = 2 * quarter
    total = count * rows
    vmem, dma = pltpu.VMEM, pltpu.SemaphoreType.DMA
    scratch = {name: vmem(value.shape, value.dtype) for name, value in loads.items()}
    loads["slab_own"] = None
    scratch["slab_own"] = vmem((rows, size), f32)
    scratch |= dict(
        slab=vmem(slab_phase.shape, f32), lit=vmem((sets, rows, size), f32), lit_own=vmem((sets, rows, size), f32),
        phase=vmem((2, rows, pupil_radius), f32), mask=vmem((2, rows, pupil_radius), jnp.int32),
        phase_sem=dma((2,)), mask_sem=dma((2,)), own=vmem((4, 2, rows // 4, band), f32), pupil=vmem((2, band_cols, band), f32),
        tilt_c=vmem((2 * count, 1, size), f32), tilt_r=vmem((2 * count, rows, lanes), f32),
        prop=vmem((2, count, 4, quarter, lanes), f32), tr=vmem((3, 2, rows, size), f32),
        passed1=vmem((2, total, size), f32), passed2=vmem((2, total, size), f32),
        camera=vmem((2, total, size), f32), grad=vmem((2, rows, size), f32), grad0=vmem((rows, size), f32),
        hi=vmem((4, total, wide), bf16), lo=vmem((4, total, wide), bf16), zs=vmem((4, total, wide), f32),
        ghi=vmem((4 * rows, wide), bf16), glo=vmem((4 * rows, wide), bf16),
        chi=vmem((quarter, 4 * lanes), bf16), clo=vmem((quarter, 4 * lanes), bf16),
        dhi=vmem((quarter, 4 * lanes), bf16), dlo=vmem((quarter, 4 * lanes), bf16),
        cz=vmem((4, quarter, lanes), f32), cs=vmem((4, quarter, lanes), f32),
        loads=dma((len(loads) + 1,)),
        pupil_sent=dma((4,)), pupil_got=dma,
    )
    for name, blocks in (("slab", 3), ("lit", sets), ("grad", 2)):
        scratch[name + "_relay"] = vmem((blocks, rows // 2, size), f32)
        for kind in ("_sent", "_got", "_late", "_via"):
            scratch[name + kind] = dma((blocks,))
    block, narrow = (devs, rows, lanes), (devs, 2 * band_cols, total)
    ports = dict(x0=(1, block), x1=(count, block), x2=(count, block), x3=(count, block))
    ports |= dict(b0=(1, narrow), b1=(1, narrow), b2=(1, narrow), b3=(1, narrow))
    ports |= dict(sums=(1, (devs, -(-stat_rows // 8) * 8, lanes)))
    ports |= dict(counts=(1, (devs, -(-patterns // 8) * 8, lanes)))
    ports |= dict(y3=(count, block), y2=(count, block), y1=(count, block), y0=(1, block))
    for name, (slots, shape) in ports.items():
        scratch[name + "_stage"] = vmem((slots,) + shape, f32)
        scratch[name + "_y"] = vmem((slots,) + shape, f32)
        scratch[name + "_sent"] = dma((slots,))
        scratch[name + "_got"] = dma((slots,))
    spec = Names(
        count=count, rows=rows, quarter=quarter, devs=devs, tiles=tiles, patterns=patterns,
        area=float(size * size), stat_rows=stat_rows, sets=sets, owners=owners, loaded=list(loads),
        names=list(inputs) + ["result"] + list(scratch),
    )
    anywhere = pl.BlockSpec(memory_space=pl.ANY)
    smem = pl.BlockSpec(memory_space=pltpu.SMEM)
    return pl.pallas_call(
        functools.partial(whole_kernel, spec),
        out_shape=jax.ShapeDtypeStruct(slab_phase.shape, f32),
        in_specs=[smem if name in ("freq", "code") else anywhere for name in inputs],
        out_specs=anywhere,
        scratch_shapes=list(scratch.values()),
        compiler_params=pltpu.CompilerParams(
            collective_id=1, has_side_effects=True, vmem_limit_bytes=67043328
        ),
        name="whole",
    )(*inputs.values())


def solution(mesh):
    in_specs = (
        P("tiles", "pat", None),
        P("pat", None),
        P("pat", None),
        P(),
        P(),
        P("tiles", "pat", None),
    )
    out_specs = P("tiles", "pat", None)

    def run(slab_phase, *others):
        devs, tiles = mesh.shape["pat"], mesh.shape["tiles"]
        size, count = slab_phase.shape[-1], others[2].shape[1]
        fits = 2 * size == lanes * devs and count * size == lanes * devs and slab_phase.shape[0] == 3 * tiles
        fits = fits and tiles == 2 and devs == len(far_first)
        inner = functools.partial(body, tiles) if fits else plain_body
        return jax.shard_map(inner, mesh=mesh, in_specs=in_specs, out_specs=out_specs, check_vma=False)(
            slab_phase, *others
        )

    return run
```

```python
import functools
import math
import types

import jax
import jax.numpy as jnp
import numpy as np
from jax import lax
from jax.experimental import pallas as pl
from jax.experimental.pallas import tpu as pltpu
from jax.sharding import PartitionSpec as P

spread_rate = 0.3
highest = lax.Precision.HIGHEST


def frequency(grid_index, grid_size):
    return (grid_index + grid_size // 2) % grid_size - grid_size // 2


def complex_times(values, factor):
    real_part = values[0] * factor[0] - values[1] * factor[1]
    imag_part = values[0] * factor[1] + values[1] * factor[0]
    return jnp.stack([real_part, imag_part])


def dft_block(length, direction, norm_factor):
    grid_index = jnp.arange(length, dtype=jnp.int32)
    angles = (grid_index[:, None] * grid_index[None, :] % length).astype(jnp.float32) * (
        2.0 * math.pi / length
    )
    cosine = jnp.cos(angles) * norm_factor
    signed_sine = direction * jnp.sin(angles) * norm_factor
    real_rows = jnp.stack([cosine, signed_sine], 1)
    imag_rows = jnp.stack([-signed_sine, cosine], 1)
    return jnp.stack([real_rows, imag_rows], 0)


def twiddle_table(short_size, long_size, grid_size, direction):
    short_index = jnp.arange(short_size, dtype=jnp.int32)
    long_index = jnp.arange(long_size, dtype=jnp.int32)
    angles = (short_index[:, None] * long_index[None, :] % grid_size).astype(jnp.float32) * (
        2.0 * math.pi / grid_size
    )
    return jnp.stack([jnp.cos(angles), direction * jnp.sin(angles)])


def table_set(col_count, dev_count, grid_size, direction):
    short_table = dft_block(col_count, direction, 1.0)
    long_table = dft_block(dev_count, direction, 1.0 / math.sqrt(grid_size))
    return (short_table, long_table, twiddle_table(col_count, dev_count, grid_size, direction))


def to_fourier(wave_field, tables, dev_count):
    short_table, long_table, twiddles = tables
    led_count = wave_field.shape[1]
    row_count = wave_field.shape[2]
    grid_size = wave_field.shape[3]
    col_count = grid_size // dev_count
    shaped = wave_field.reshape(2, led_count, row_count, col_count, dev_count)
    sectioned = jnp.einsum("zlrmq,zmwc->wlrcq", shaped, short_table, precision=highest)
    sectioned = complex_times(sectioned, twiddles)
    outgoing = jnp.einsum("wlrcq,wqvd->dvlcr", sectioned, long_table, precision=highest)
    incoming = lax.all_to_all(
        outgoing.reshape(dev_count, -1), "pat", split_axis=0, concat_axis=0, tiled=True
    )
    incoming = incoming.reshape(dev_count, 2, led_count, col_count, row_count)
    sectioned = jnp.einsum("swlcr,wsvj->vlcrj", incoming, long_table, precision=highest)
    sectioned = complex_times(sectioned, twiddles)
    sectioned = jnp.einsum("wlcrj,wrvh->vlchj", sectioned, short_table, precision=highest)
    return sectioned.reshape(2, led_count, col_count, grid_size)


def to_space(spectrum, tables, dev_count):
    short_table, long_table, twiddles = tables
    led_count = spectrum.shape[1]
    col_count = spectrum.shape[2]
    grid_size = spectrum.shape[3]
    row_count = grid_size // dev_count
    shaped = spectrum.reshape(2, led_count, col_count, row_count, dev_count)
    sectioned = jnp.einsum("zlcmq,zmwr->wlcrq", shaped, short_table, precision=highest)
    sectioned = complex_times(sectioned, twiddles)
    outgoing = jnp.einsum("wlcrq,wqvd->dvlcr", sectioned, long_table, precision=highest)
    incoming = lax.all_to_all(
        outgoing.reshape(dev_count, -1), "pat", split_axis=0, concat_axis=0, tiled=True
    )
    incoming = incoming.reshape(dev_count, 2, led_count, col_count, row_count)
    sectioned = jnp.einsum("swlcr,wsvj->vlrcj", incoming, long_table, precision=highest)
    sectioned = complex_times(sectioned, twiddles)
    sectioned = jnp.einsum("wlrcj,wcvh->vlrhj", sectioned, short_table, precision=highest)
    return sectioned.reshape(2, led_count, row_count, grid_size)


def plain_body(slab_phase, pupil_phase, pupil_mask, led_code, led_freq, measured):
    dev_count = lax.axis_size("pat")
    position = lax.axis_index("pat")
    slab_count, row_count, grid_size = slab_phase.shape
    col_count = grid_size // dev_count
    pattern_count, led_count = led_code.shape
    area = float(grid_size * grid_size)
    forward_set = table_set(col_count, dev_count, grid_size, -1.0)
    inverse_set = table_set(col_count, dev_count, grid_size, 1.0)
    conjugate = jnp.array([1.0, -1.0], jnp.float32)[:, None, None]
    col_freq = frequency(position * col_count + jnp.arange(col_count, dtype=jnp.int32), grid_size)
    row_freq = frequency(jnp.arange(grid_size, dtype=jnp.int32), grid_size)
    radius = col_freq[:, None] * col_freq[:, None] + row_freq[None, :] * row_freq[None, :]
    cutoff = grid_size // 2 * (grid_size // 2)
    inside = radius <= cutoff
    height = jnp.sqrt(jnp.maximum(cutoff - radius, 0).astype(jnp.float32))
    phase_shift = spread_rate * (height - grid_size // 2)
    propagator = jnp.stack(
        [jnp.where(inside, jnp.cos(phase_shift), 0.0), jnp.where(inside, jnp.sin(phase_shift), 0.0)]
    )
    opening = pupil_mask.astype(jnp.float32)
    pupil = jnp.stack([opening * jnp.cos(pupil_phase), opening * jnp.sin(pupil_phase)])
    propagator_conj = propagator * conjugate
    pupil_conj = pupil * conjugate
    row_index = position * row_count + jnp.arange(row_count, dtype=jnp.int32)
    col_index = jnp.arange(grid_size, dtype=jnp.int32)
    tilt_index = (
        led_freq[:, 0][:, None, None] * row_index[None, :, None]
        + led_freq[:, 1][:, None, None] * col_index[None, None, :]
    ) % grid_size
    tilt_angle = tilt_index.astype(jnp.float32) * (2.0 * math.pi / grid_size)
    illumination = jnp.stack([jnp.cos(tilt_angle), jnp.sin(tilt_angle)])
    transmission = jnp.stack([jnp.cos(slab_phase), jnp.sin(slab_phase)])
    group_count = 1
    group_size = led_count // group_count
    wave_groups = [illumination]
    passed_groups = []
    for slab_index in range(slab_count):
        factor = transmission[:, slab_index]
        passed = [complex_times(wave_field, factor) for wave_field in wave_groups]
        passed_groups.append(passed)
        spectral_factor = propagator if slab_index < slab_count - 1 else pupil
        wave_groups = [
            to_space(
                complex_times(to_fourier(passed_field, forward_set, dev_count), spectral_factor),
                inverse_set,
                dev_count,
            )
            for passed_field in passed
        ]
    camera = wave_groups[0]
    led_power = camera[0] * camera[0] + camera[1] * camera[1]
    code_float = led_code.astype(jnp.float32)
    pattern_power = jnp.dot(
        code_float, led_power.reshape(led_count, -1), precision=highest
    ).reshape(pattern_count, row_count, grid_size)
    counts = measured.astype(jnp.float32)
    power_sum, count_sum = lax.psum(
        (jnp.sum(pattern_power, axis=(1, 2)), jnp.sum(counts, axis=(1, 2))), "pat"
    )
    mean_power = power_sum / area
    mean_count = count_sum / area
    relative = pattern_power / mean_power[:, None, None]
    misfit = relative - counts / mean_count[:, None, None]
    coupling = lax.psum(jnp.sum(misfit * relative, axis=(1, 2)), "pat") / area
    pattern_weight = (misfit - coupling[:, None, None]) / mean_power[:, None, None]
    led_weight = jnp.dot(
        code_float.T, pattern_weight.reshape(pattern_count, -1), precision=highest
    ).reshape(led_count, row_count, grid_size)
    camera_adjoint = 2.0 * led_weight[None] * camera
    adjoint_groups = [camera_adjoint]
    gradients = [None] * slab_count
    for slab_index in range(slab_count - 1, -1, -1):
        spectral_factor = pupil_conj if slab_index == slab_count - 1 else propagator_conj
        back_groups = [
            to_space(
                complex_times(to_fourier(adjoint_field, forward_set, dev_count), spectral_factor),
                inverse_set,
                dev_count,
            )
            for adjoint_field in adjoint_groups
        ]
        gradient = jnp.zeros((row_count, grid_size), jnp.float32)
        for passed_field, back_field in zip(passed_groups[slab_index], back_groups):
            gradient = jnp.sum(
                passed_field[0] * back_field[1] - passed_field[1] * back_field[0], axis=0
            )
        gradients[slab_index] = gradient
        if slab_index > 0:
            release = transmission[:, slab_index] * conjugate
            adjoint_groups = [complex_times(back_field, release) for back_field in back_groups]
    return jnp.stack(gradients)


class Names(types.SimpleNamespace):
    def __getitem__(self, name):
        return getattr(self, name)


pupil_radius = 128
lanes = 128
f32 = jnp.float32
bf16 = jnp.bfloat16


def halves(table):
    table32 = np.asarray(table, np.float32)
    high = table32.astype(bf16)
    low = (table32 - high.astype(np.float32)).astype(bf16)
    return np.stack([high, low])


def row_tables(size, block, band_block):
    quarter = size // 4
    pos = np.arange(quarter)
    angle = 2.0 * np.pi * ((pos[:, None] * pos[None, :]) % quarter) / quarter
    cosine = np.cos(angle) / math.sqrt(size)
    sine = np.sin(angle) / math.sqrt(size)

    def forward(freqs, width):
        parts = []
        for first in range(0, len(freqs), width):
            pick = freqs[first : first + width] % quarter
            left = np.concatenate([cosine[:, pick], sine[:, pick]], 0)
            right = np.concatenate([-sine[:, pick], cosine[:, pick]], 0)
            parts.append(np.concatenate([left, right], 1))
        return np.concatenate(parts, 1)

    full = forward(pos, block)
    reach = pupil_radius // 4
    band = forward(np.arange(-reach, reach), band_block)
    theta = 2.0 * np.pi * (np.arange(4)[:, None] * pos[None, :]) / size
    twiddle = np.concatenate([np.cos(theta), np.sin(theta)], 0).astype(np.float32)
    return Names(
        full=jnp.asarray(halves(full)),
        full_inv=jnp.asarray(halves(full.T)),
        band=jnp.asarray(halves(band)),
        band_inv=jnp.asarray(halves(band.T)),
        twiddle=jnp.asarray(twiddle),
    )


def col_tables(size):
    quarter = size // 4
    pos = np.arange(quarter)
    angle = 2.0 * np.pi * ((pos[:, None] * pos[None, :]) % quarter) / quarter
    both = np.concatenate([np.cos(angle), np.sin(angle)], 0) / math.sqrt(size)
    theta = 2.0 * np.pi * (np.arange(1, 4)[:, None] * pos[None, :]) / size
    twiddle = np.stack([np.cos(theta), np.sin(theta)]).astype(np.float32)
    twiddle = np.ascontiguousarray(np.broadcast_to(twiddle[..., None], twiddle.shape + (lanes,)))
    return Names(both=halves(both), twiddle=twiddle)


def split(value):
    high = value.astype(bf16)
    return high, (value - high.astype(f32)).astype(bf16)


def dot3(left, right):
    def dot(a, b):
        return jnp.dot(a, b, preferred_element_type=f32)

    return dot(left[0], right[0]) + (dot(left[0], right[1]) + dot(left[1], right[0]))


def turn(value):
    rolled = pltpu.roll(value, lanes // 2, 1)
    lane = lax.broadcasted_iota(jnp.int32, value.shape, 1)
    return jnp.where(lane < lanes // 2, rolled, -rolled)


def row_spread(blocks, twiddle_ref):
    (r0, i0), (r1, i1), (r2, i2), (r3, i3) = blocks
    sr, si, tr, ti = r0 + r2, i0 + i2, r1 + r3, i1 + i3
    dr, di, er, ei = r0 - r2, i0 - i2, r1 - r3, i1 - i3
    mixed = [(sr + tr, si + ti), (dr + ei, di - er), (sr - tr, si - ti), (dr - ei, di + er)]
    out = [mixed[0]]
    for j in range(1, 4):
        cosine, sine = twiddle_ref[j : j + 1, :], twiddle_ref[4 + j : 5 + j, :]
        re, im = mixed[j]
        out.append((re * cosine + im * sine, im * cosine - re * sine))
    return out


def row_gather(parts, twiddle_ref):
    g = [parts[0]]
    for j in range(1, 4):
        cosine, sine = twiddle_ref[j : j + 1, :], twiddle_ref[4 + j : 5 + j, :]
        re, im = parts[j]
        g.append((re * cosine - im * sine, im * cosine + re * sine))
    (r0, i0), (r1, i1), (r2, i2), (r3, i3) = g
    sr, si, tr, ti = r0 + r2, i0 + i2, r1 + r3, i1 + i3
    dr, di, er, ei = r0 - r2, i0 - i2, r1 - r3, i1 - i3
    return [(sr + tr, si + ti), (dr - ei, di + er), (sr - tr, si - ti), (dr + ei, di - er)]


mesh_ids = pl.DeviceIdType.MESH
far_first = (14, 15, 6, 7, 10, 11, 12, 13, 2, 3, 4, 5, 8, 9, 1, 0)


def flip(index, mask):
    out = index
    for bit in (1, 2, 4, 8):
        if mask & bit:
            out = out + bit - 2 * bit * lax.rem(index // bit, 2)
    return out


def whole_kernel(spec, *refs):
    ref = Names(**dict(zip(spec.names, refs)))
    count, rows, quarter, devs, patterns = spec.count, spec.rows, spec.quarter, spec.devs, spec.patterns
    size, per, half, step = 4 * quarter, devs // 4, devs // 2, 16
    tile, place = lax.axis_index("tiles"), lax.axis_index("pat")
    work = place // half
    me = half * tile + lax.rem(place, half)
    native = tile == work
    foreign = jnp.logical_not(native)
    other = dict(tiles=1 - tile, pat=lax.rem(place + half, devs))

    def member(index):
        return dict(tiles=index // half, pat=work * half + lax.rem(index, half))

    barrier = pltpu.get_barrier_semaphore()
    everyone = spec.tiles * devs

    def signal(hop, carry):
        target = lax.rem(tile * devs + place + hop, everyone)
        pl.semaphore_signal(
            barrier, inc=1, device_id=dict(tiles=target // devs, pat=lax.rem(target, devs)),
            device_id_type=mesh_ids,
        )
        return carry

    lax.fori_loop(1, everyone, signal, 0)

    def local(source, target, sem):
        return pltpu.make_async_copy(source, target, sem)

    def away(source, target, sent, got, device):
        return pltpu.make_async_remote_copy(
            src_ref=source, dst_ref=target, send_sem=sent, recv_sem=got, device_id=device,
            device_id_type=mesh_ids,
        )

    def fetch(name):
        source = ref.slab_hbm.at[0] if name == "slab_own" else ref[name + "_hbm"]
        return local(source, ref[name], ref.loads.at[spec.loaded.index(name)])

    reach = pupil_radius
    spans = (slice(size - reach, size), slice(0, reach))

    def near(name, k):
        return local(ref[name + "_hbm"].at[:, spans[k]], ref[name].at[k], ref[name + "_sem"].at[k])

    for name in ("phase", "mask"):
        for k in range(2):
            near(name, k).start()
    for name in spec.loaded:
        fetch(name).start()

    def ready(name):
        fetch(name).wait()

    share = rows // 2
    neighbour = dict(tiles=1 - tile, pat=place)
    across = dict(tiles=tile, pat=lax.rem(place + half, devs))

    sources = dict(slab=ref.slab_hbm, lit=ref.lit_own, grad=ref.grad)
    targets = dict(slab=ref.slab, lit=ref.lit, grad=ref.result.at[1:3])
    part = dict(slab=3, lit=spec.sets, grad=2)

    def semaphore(name, kind, k):
        return ref[name + kind].at[k]

    def direct(name, k):
        return away(
            sources[name].at[k, :share], targets[name].at[k, :share], semaphore(name, "_sent", k),
            semaphore(name, "_got", k), other,
        )

    def hop(name, k):
        return away(
            sources[name].at[k, share:], ref[name + "_relay"].at[k], semaphore(name, "_sent", k),
            semaphore(name, "_via", k), neighbour,
        )

    def onward(name, k):
        return away(
            ref[name + "_relay"].at[k], targets[name].at[k, share:], semaphore(name, "_sent", k),
            semaphore(name, "_late" if name == "slab" else "_got", k), across,
        )

    def trade_native(name, k):
        @pl.when(native)
        def _():
            if name == "slab":
                for span, kind in ((pl.ds(0, share), "_got"), (pl.ds(share, share), "_late")):
                    local(sources[name].at[k, span], targets[name].at[k, span], semaphore(name, kind, k)).start()
            else:
                local(sources[name].at[k], targets[name].at[k], semaphore(name, "_got", k)).start()

    def trade_foreign(name, *blocks):
        @pl.when(foreign)
        def _():
            for k in blocks:
                direct(name, k).start()
                hop(name, k).start()

    def forward_on(name, *blocks):
        @pl.when(native)
        def _():
            for k in blocks:
                hop(name, k).wait_recv()
                onward(name, k).start()

    def traded(name, k):
        whole = targets[name].at[k]
        if name == "slab":
            halves = (whole.at[:share], whole.at[share:])
            local(halves[0], halves[0], semaphore(name, "_got", k)).wait()
            local(halves[1], halves[1], semaphore(name, "_late", k)).wait()
        else:
            local(whole, whole, semaphore(name, "_got", k)).wait()

    def trade_ends(name):
        for k in range(part[name]):

            @pl.when(native)
            def _():
                onward(name, k).wait_send()

            @pl.when(foreign)
            def _():
                whole = sources[name].at[k]
                local(whole, whole, semaphore(name, "_sent", k)).wait()

    def port(name):
        return Names(
            stage=ref[name + "_stage"], y=ref[name + "_y"], sent=ref[name + "_sent"], got=ref[name + "_got"]
        )

    def push_one(x, slot, mask, span=None):
        dest = flip(me, mask)
        source = x.stage.at[slot, dest] if span is None else x.stage.at[slot, dest, span]
        target = x.y.at[slot, me] if span is None else x.y.at[slot, me, span]
        if mask:
            away(source, target, x.sent.at[slot], x.got.at[slot], member(dest)).start()
        else:
            local(source, target, x.got.at[slot]).start()

    def push(x, slot):
        for mask in far_first:
            push_one(x, slot, mask)

    def leave_one(x, slot, mask):
        dest = flip(place, mask)

        def start_away():
            away(
                x.stage.at[slot, dest], x.y.at[slot, me], x.sent.at[slot], x.got.at[slot],
                dict(tiles=work, pat=dest),
            ).start()

        if mask:
            start_away()
        else:

            @pl.when(native)
            def _():
                local(x.stage.at[slot, dest], x.y.at[slot, me], x.got.at[slot]).start()

            pl.when(foreign)(start_away)

    def land(x, slot):
        local(x.y.at[slot], x.y.at[slot], x.got.at[slot]).wait()

    def drain(x, slots):
        for slot in range(slots):
            part = x.stage.at[slot, pl.ds(0, devs - 1)]
            local(part, part, x.sent.at[slot]).wait()

    hi, lo, zs = ref.hi, ref.lo, ref.zs
    cut = [slice(a * quarter, (a + 1) * quarter) for a in range(4)]

    def spot(l, base):
        return pl.ds(pl.multiple_of(l * rows + base, step), step)

    def each_chunk(chunk, carry=0):
        def at_chunk(i, carry):
            base = pl.multiple_of(i * step, step)
            return chunk(base, pl.ds(base, step), carry)

        return lax.fori_loop(0, rows // step, at_chunk, carry)

    def gathered(l, base):
        at = spot(l, base)
        parts = [(zs[j, at, :quarter], zs[j, at, quarter:]) for j in range(4)]
        return row_gather(parts, ref.row_twiddle)

    def scattered(l, base, blocks):
        at = spot(l, base)
        for j, (re, im) in enumerate(row_spread(blocks, ref.row_twiddle)):
            high, low = split(re)
            hi[j, at, :quarter] = high
            lo[j, at, :quarter] = low
            high, low = split(im)
            hi[j, at, quarter:] = high
            lo[j, at, quarter:] = low

    def led_rows(l):
        return pl.ds(pl.multiple_of(l * rows, rows), rows)

    def inverse_full(y, slot, l):
        for j in range(4):
            for q in range(per):
                high, low = split(y[slot, per * j + q])
                ref.ghi[j * rows : (j + 1) * rows, q * lanes : (q + 1) * lanes] = high
                ref.glo[j * rows : (j + 1) * rows, q * lanes : (q + 1) * lanes] = low
        value = dot3((ref.ghi[...], ref.glo[...]), (ref.full_inv[0], ref.full_inv[1]))
        zs[:, led_rows(l), :] = value.reshape(4, rows, 2 * quarter)

    def emit_full(x, slot, l):
        left = [part[:, led_rows(l), :].reshape(4 * rows, 2 * quarter) for part in (hi, lo)]
        value = dot3(left, (ref.full[0], ref.full[1]))
        for j in range(4):
            for q in range(per):
                x.stage[slot, per * j + q] = value[j * rows : (j + 1) * rows, q * lanes : (q + 1) * lanes]
        push(x, slot)

    def braid(first, second):
        middle = lanes // 2
        lane = lax.broadcasted_iota(jnp.int32, first.shape, 1)
        return (
            jnp.where(lane < middle, first, pltpu.roll(second, middle, 1)),
            jnp.where(lane < middle, pltpu.roll(first, middle, 1), second),
        )

    def inverse_band(x, l):
        for pair in range(2):
            turned = x.y[l, 2 * per * pair : 2 * per * (pair + 1)].reshape(lanes, lanes).T
            for k, block in enumerate(braid(turned[:rows], turned[rows:])):
                at = slice((2 * pair + k) * rows, (2 * pair + k + 1) * rows)
                high, low = split(block)
                ref.ghi[at, :lanes] = high
                ref.glo[at, :lanes] = low
        value = dot3((ref.ghi[:, :lanes], ref.glo[:, :lanes]), (ref.band_inv[0], ref.band_inv[1]))
        zs[:, led_rows(l), :] = value.reshape(4, rows, 2 * quarter)

    def emit_band(x, l):
        left = [part[:, led_rows(l), :].reshape(4 * rows, 2 * quarter) for part in (hi, lo)]
        flipped = dot3(left, (ref.band[0], ref.band[1])).T
        deep = x.y.shape[2]
        for pair in range(2):
            at = slice(pair * lanes, (pair + 1) * lanes)
            for k, block in enumerate(braid(flipped[:rows, at], flipped[rows:, at])):
                for q in range(per):
                    x.stage[l, per * (2 * pair + k) + q] = block[q * deep : (q + 1) * deep]
        push(x, l)

    def tilt(l, here, a, value, sign):
        rc, rs = ref.tilt_r[2 * l, here, :], ref.tilt_r[2 * l + 1, here, :]
        cc, cs = ref.tilt_c[2 * l, :, cut[a]], ref.tilt_c[2 * l + 1, :, cut[a]]
        rc = jnp.concatenate([rc] * (quarter // lanes), 1)
        rs = jnp.concatenate([rs] * (quarter // lanes), 1)
        er = rc * cc - rs * cs
        ei = sign * (rc * cs + rs * cc)
        re, im = value
        return re * er - im * ei, re * ei + im * er

    def spread(x, slot):
        def at_part(i, carry):
            here = pl.ds(pl.multiple_of(i * rows, rows), rows)
            x0, x1, x2, x3 = [x.y[slot, per * a + i] for a in range(4)]
            s, t, d, e = x0 + x2, x1 + x3, x0 - x2, turn(x1 - x3)
            for j, value in enumerate((s + t, d + e, s - t, d - e)):
                if j:
                    value = value * ref.col_twiddle[0, j - 1, here, :] + turn(value) * ref.col_twiddle[1, j - 1, here, :]
                high, low = split(value)
                ref.chi[here, j * lanes : (j + 1) * lanes] = high
                ref.clo[here, j * lanes : (j + 1) * lanes] = low
            return carry

        lax.fori_loop(0, per, at_part, 0)

    def col_dot(high, low, take, sign):
        for pair in range(2):
            at = slice(2 * pair * lanes, 2 * (pair + 1) * lanes)
            y = dot3((ref.both[0], ref.both[1]), (high[:, at], low[:, at]))
            for k in range(2):
                at = slice(k * lanes, (k + 1) * lanes)
                take(2 * pair + k, y[:quarter, at] + sign * turn(y[quarter:, at]))

    def shaped(z, l, j, sign):
        return z * ref.prop[0, l, j] - sign * (turn(z) * ref.prop[1, l, j])

    def stow(j, value):
        high, low = split(value)
        ref.dhi[:, j * lanes : (j + 1) * lanes] = high
        ref.dlo[:, j * lanes : (j + 1) * lanes] = low

    def col_inverse(x, slot, send=push_one, far_parts=(3, 1, 2, 0)):
        def take(j, value):
            if j:
                value = value * ref.col_twiddle[0, j - 1] - turn(value) * ref.col_twiddle[1, j - 1]
            ref.cz[j] = value

        col_dot(ref.dhi, ref.dlo, take, -1.0)
        home = lax.rem(me, per)
        for bits in (3, 2, 1, 0):
            i = flip(home, bits)
            here = pl.ds(pl.multiple_of(i * rows, rows), rows)
            g0, g1, g2, g3 = [ref.cz[j, here, :] for j in range(4)]
            s, t, d, e = g0 + g2, g1 + g3, g0 - g2, turn(g1 - g3)
            for a, value in enumerate((s + t, d - e, s - t, d + e)):
                x.stage[slot, per * a + i] = value
            for far in far_parts:
                send(x, slot, per * far + bits)

    def each_led(stage):
        def at_led(l, carry):
            stage(l)
            return carry

        lax.fori_loop(0, count, at_led, 0)

    def columns(x, out, sign):
        def stage(l):
            land(x, l)
            spread(x, l)
            col_dot(ref.chi, ref.clo, lambda j, z: stow(j, shaped(z, l, j, sign)), 1.0)
            col_inverse(out, l)

        each_led(stage)

    def pupil_columns(x, out, sign):
        deep = x.y.shape[2]

        def stage(l):
            land(x, l)
            blocks = []
            for a in range(4):
                pairs = [braid(x.y[l, s], x.y[l, s + 1]) for s in range(per * a, per * (a + 1), 2)]
                blocks.append(tuple(jnp.concatenate([pair[k] for pair in pairs], 1) for k in range(2)))
            mixed = [jnp.concatenate(part, 1) for part in row_spread(blocks, ref.row_twiddle)]
            z = dot3(split(jnp.concatenate(mixed, 0)), (ref.band[0], ref.band[1]))
            z = z * ref.shape[0] + sign * (pltpu.roll(z, lanes // 2, 1) * ref.shape[1])
            y = dot3(split(z), (ref.band_inv[0], ref.band_inv[1]))
            parts = [(y[j * deep : (j + 1) * deep, :quarter], y[j * deep : (j + 1) * deep, quarter:]) for j in range(4)]
            for a, (re, im) in enumerate(row_gather(parts, ref.row_twiddle)):
                for k in range(quarter // lanes):
                    at = slice(k * lanes, (k + 1) * lanes)
                    first, second = braid(re[:, at], im[:, at])
                    out.stage[l, per * a + 2 * k] = first
                    out.stage[l, per * a + 2 * k + 1] = second
            push(out, l)

        each_led(stage)

    def shape_pupil():
        local(ref.pupil, ref.pupil, ref.pupil_got).wait()
        band, deep = ref.pupil.shape[2], ref.pupil.shape[1]
        freq = lax.broadcasted_iota(jnp.int32, (band, 4 * lanes), 0)
        slot = lax.broadcasted_iota(jnp.int32, (band, 4 * lanes), 1)
        wanted = 4 * lax.rem(slot, lanes // 2) + slot // lanes
        pick = jnp.where(freq == wanted, 1.0, 0.0).astype(bf16)
        value, out = ref.pupil[...].reshape(2 * deep, band), 0.0
        for k in range(3):
            high = value.astype(bf16)
            out = out + jnp.dot(high, pick, preferred_element_type=f32)
            value = value - high.astype(f32)
        lane = lax.broadcasted_iota(jnp.int32, (deep, lanes), 1)
        for j in range(4):
            at = slice(j * lanes, (j + 1) * lanes)
            ref.shape[0, j * deep : (j + 1) * deep] = out[:deep, at]
            ref.shape[1, j * deep : (j + 1) * deep] = jnp.where(lane < lanes // 2, -out[deep:, at], out[deep:, at])

    def phases(source, target):
        def chunk(base, here, carry):
            phase = source[here, :]
            target[0, here, :] = jnp.cos(phase)
            target[1, here, :] = jnp.sin(phase)
            return carry

        each_chunk(chunk)

    def fold(value):
        total_rows = value[:8]
        for k in range(1, value.shape[0] // 8):
            total_rows = total_rows + value[8 * k : 8 * k + 8]
        out = total_rows[:, :lanes]
        for k in range(1, value.shape[1] // lanes):
            out = out + total_rows[:, lanes * k : lanes * (k + 1)]
        return out

    def fold_all(p):
        def chunk(base, here, carry):
            return carry + fold(ref.measured[p, here, :].astype(f32))

        return jnp.sum(each_chunk(chunk, jnp.zeros((8, lanes), f32)), 0, keepdims=True)

    def slab_phases(s):
        traded("slab", s)
        phases(ref.slab.at[s], ref.tr.at[s])

    for k in range(3):
        trade_native("slab", k)
    turn_size = 2.0 * math.pi / size
    col = lax.broadcasted_iota(jnp.int32, (8, size), 1)
    row = me * rows + lax.broadcasted_iota(jnp.int32, (rows, lanes), 0)
    for l in range(count):
        for index, freq, tilts in ((col, ref.freq[l, 1], ref.tilt_c), (row, ref.freq[l, 0], ref.tilt_r)):
            angle = jnp.bitwise_and(index * freq, size - 1).astype(f32) * turn_size
            deep = tilts.shape[1]
            tilts[2 * l] = jnp.cos(angle)[:deep]
            tilts[2 * l + 1] = jnp.sin(angle)[:deep]

    pl.semaphore_wait(barrier, everyone - 1)
    pieces = (pl.ds(0, share // 2), pl.ds(share // 2, share // 2))

    def piece(source, target, sent, k, device):
        return away(source, target, sent, ref.piece_got.at[k], device)

    def first_hop(k):
        at = pieces[k]
        return piece(
            sources["slab"].at[0, share:].at[at], ref.slab_relay.at[0, at], semaphore("slab", "_sent", 0), k, neighbour
        )

    def first_onward(k):
        at = pieces[k]
        return away(
            ref.slab_relay.at[0, at], targets["slab"].at[0, share:].at[at], semaphore("slab", "_sent", 0),
            semaphore("slab", "_late", 0), across,
        )

    @pl.when(foreign)
    def _():
        direct("slab", 0).start()
        for k in range(2):
            first_hop(k).start()

    ready("row_twiddle")
    ready("full")
    x0, x1, x2, x3 = port("x0"), port("x1"), port("x2"), port("x3")

    def enter(first, count_rows):
        def chunk(i, carry):
            base = pl.multiple_of(first + i * step, step)
            here = pl.ds(base, step)
            blocks = []
            for c in cut:
                phase = ref.slab[0, here, c]
                blocks.append((jnp.cos(phase), jnp.sin(phase)))
            scattered(0, base, blocks)
            return carry

        lax.fori_loop(0, count_rows // step, chunk, 0)
        span = pl.ds(first, count_rows)
        left = [part[:, span, :].reshape(4 * count_rows, 2 * quarter) for part in (hi, lo)]
        value = dot3(left, (ref.full[0], ref.full[1]))
        for j in range(4):
            for q in range(per):
                x0.stage[0, per * j + q, span] = value[
                    j * count_rows : (j + 1) * count_rows, q * lanes : (q + 1) * lanes
                ]
        for mask in far_first:
            push_one(x0, 0, mask, span)


    for name in ("phase", "mask"):
        for k in range(2):
            near(name, k).wait()
    for j in range(4):
        line = pl.ds(j, rows // 4, stride=4)
        for k in range(2):
            opening = ref.mask[k, line, :].astype(f32)
            angle = ref.phase[k, line, :]
            at = slice(k * reach, (k + 1) * reach)
            ref.own[j, 0, :, at] = opening * jnp.cos(angle)
            ref.own[j, 1, :, at] = opening * jnp.sin(angle)
    owners = spec.owners

    def pupil_copy(jj, w, q):
        return away(
            ref.own.at[2 * tile + jj], ref.pupil, ref.pupil_sent.at[2 * jj + w], ref.pupil_got,
            dict(tiles=tile, pat=w * half + jj * per + q),
        )

    for q in range(per):

        @pl.when(place == owners[q])
        def _():
            for jj in range(2):
                for w in range(2):
                    pupil_copy(jj, w, q).start()


    @pl.when(native)
    def _():
        for k in range(2):
            first_hop(k).wait_recv()
            first_onward(k).start()
        traded("slab", 0)
        enter(0, rows)

    cutoff = size // 2 * (size // 2)

    def centred(index):
        return jnp.where(index >= size // 2, index - size, index)

    def spectrum(i, carry):
        here = pl.ds(pl.multiple_of(i * step, step), step)
        row = lax.broadcasted_iota(jnp.int32, (step, lanes), 0) + i * step
        lane = lax.broadcasted_iota(jnp.int32, (step, lanes), 1)
        lane = jnp.where(lane < lanes // 2, lane, lane - lanes // 2)
        col = 4 * (lax.rem(me, per) * (lanes // 2) + lane) + me // per
        for l in range(count):
            v = centred(col + ref.freq[l, 1])
            for j in range(4):
                u = centred(4 * row + j + ref.freq[l, 0])
                radius = u * u + v * v
                inside = radius <= cutoff
                height = jnp.sqrt(jnp.maximum(cutoff - radius, 0).astype(f32))
                shift = spread_rate * (height - float(size // 2))
                ref.prop[0, l, j, here, :] = jnp.where(inside, jnp.cos(shift), 0.0)
                ref.prop[1, l, j, here, :] = jnp.where(inside, jnp.sin(shift), 0.0)
        return carry

    lax.fori_loop(0, quarter // step, spectrum, 0)

    @pl.when(foreign)
    def _():
        direct("slab", 0).wait_recv()
        enter(0, share)
        onward("slab", 0).wait_recv()
        enter(share, rows - share)


    ready("measured")
    counts = port("counts")
    lines = [fold_all(p) for p in range(patterns)]
    lines.append(jnp.zeros((counts.stage.shape[2] - patterns, lanes), f32))
    lines = jnp.concatenate(lines, 0)
    for d in range(devs):
        counts.stage[0, d] = lines
    for mask in far_first:
        dest = flip(place, mask)
        if mask:
            away(
                counts.stage.at[0, dest], counts.y.at[0, place], counts.sent.at[0], counts.got.at[0],
                dict(tiles=tile, pat=dest),
            ).start()
        else:
            local(counts.stage.at[0, dest], counts.y.at[0, place], counts.got.at[0]).start()
    ready("col_twiddle")
    ready("both")
    ready("full_inv")
    trade_foreign("slab", 1)
    land(x0, 0)
    forward_on("slab", 1)
    spread(x0, 0)

    def keep_spectrum(j, z):
        ref.cs[j] = z

    col_dot(ref.chi, ref.clo, keep_spectrum, 1.0)

    def first(l):
        for j in range(4):
            stow(j, shaped(ref.cs[j], l, j, 1.0))
        col_inverse(x1, l)

    each_led(first)
    trade_foreign("slab", 2)
    land(counts, 0)
    count_sum = jnp.sum(jnp.sum(counts.y[0], 0), 1, keepdims=True)
    area = spec.area
    code = [[ref.code[l, p].astype(f32) for l in range(count)] for p in range(patterns)]
    lit_sets = [[l for l in range(count) if (c + 1) >> l & 1] for c in range(spec.sets)]
    member_of = []
    for leds in lit_sets:
        member_of.append([])
        for p in range(patterns):
            is_in = 1.0
            for l in range(count):
                is_in = is_in * (code[p][l] if l in leds else 1.0 - code[p][l])
            member_of[-1].append(is_in)
    share_of = [[member_of[c][p] * (area / count_sum[p : p + 1]) for p in range(patterns)] for c in range(spec.sets)]

    def gather_counts(base, here, carry):
        for c in cut:
            seen = [ref.measured[p, here, c].astype(f32) for p in range(patterns)]
            for k in range(spec.sets):
                ref.lit_own[k, here, c] = sum(share_of[k][p] * seen[p] for p in range(patterns))
        return carry

    each_chunk(gather_counts)
    for k in range(spec.sets):
        trade_native("lit", k)
    trade_foreign("lit", 0)
    slab_phases(1)

    def forward(l):
        land(x1, l)
        inverse_full(x1.y, l, l)

        def chunk(base, here, carry):
            fields, at, blocks = gathered(l, base), spot(l, base), []
            for a, c in enumerate(cut):
                tr, ti = ref.tr[1, 0, here, c], ref.tr[1, 1, here, c]
                re, im = fields[a]
                re, im = re * tr - im * ti, re * ti + im * tr
                ref.passed1[0, at, c] = re
                ref.passed1[1, at, c] = im
                blocks.append((re, im))
            scattered(l, base, blocks)
            return carry

        each_chunk(chunk)
        emit_full(x2, l, l)

    each_led(forward)
    forward_on("slab", 2)
    forward_on("lit", 0)
    trade_foreign("lit", 1)
    columns(x2, x3, 1.0)
    trade_foreign("lit", *range(2, spec.sets))
    forward_on("lit", 1)
    slab_phases(2)
    b0, b1, b2, b3, sums = port("b0"), port("b1"), port("b2"), port("b3"), port("sums")
    ready("band")
    ready("band_inv")
    shape_pupil()

    def forward_band(l):
        land(x3, l)
        inverse_full(x3.y, l, l)

        def chunk(base, here, carry):
            fields, at, blocks = gathered(l, base), spot(l, base), []
            for a, c in enumerate(cut):
                tr, ti = ref.tr[2, 0, here, c], ref.tr[2, 1, here, c]
                re, im = fields[a]
                re, im = re * tr - im * ti, re * ti + im * tr
                ref.passed2[0, at, c] = re
                ref.passed2[1, at, c] = im
                blocks.append(tilt(l, here, a, (re, im), 1.0))
            scattered(l, base, blocks)
            return carry

        each_chunk(chunk)
        emit_band(b0, l)

    each_led(forward_band)
    forward_on("lit", *range(2, spec.sets))
    pupil_columns(b0, b1, 1.0)

    def camera(l):
        land(b1, l)
        inverse_band(b1, l)

    each_led(camera)
    for k in range(spec.sets):
        traded("lit", k)

    def measure(base, here, carry):
        fields = [gathered(l, base) for l in range(count)]
        adds = [0.0] * spec.stat_rows
        for a, c in enumerate(cut):
            power = []
            for l in range(count):
                at = spot(l, base)
                re, im = fields[l][a]
                ref.camera[0, at, c] = re
                ref.camera[1, at, c] = im
                power.append(re * re + im * im)
            values = list(power)
            for l in range(count):
                for m in range(l, count):
                    values.append(power[l] * power[m])
            for k, leds in enumerate(lit_sets):
                seen = ref.lit[k, here, c]
                values += [seen * power[l] for l in leds]
            for k, value in enumerate(values):
                adds[k] = adds[k] + fold(value)
        return tuple(x + y for x, y in zip(carry, adds))

    stats = each_chunk(measure, tuple(jnp.zeros((8, lanes), f32) for _ in range(spec.stat_rows)))
    packed = [jnp.sum(line, 0, keepdims=True) for line in stats]
    packed.append(jnp.zeros((sums.stage.shape[2] - len(packed), lanes), f32))
    packed = jnp.concatenate(packed, 0)
    for d in range(devs):
        sums.stage[0, d] = packed
    push(sums, 0)
    land(sums, 0)
    added = jnp.sum(jnp.sum(sums.y[0], 0), 1, keepdims=True)
    pairs = [(l, m) for l in range(count) for m in range(l, count)]
    cross_row = count + len(pairs)
    inverse_mean, number, couple = [], [], []
    for k, leds in enumerate(lit_sets):
        mean = sum(added[l : l + 1] for l in leds) / area
        members = sum(member_of[k])
        inverse = jnp.where(members > 0.0, 1.0 / mean, 0.0)
        square = 0.0
        for at, (l, m) in enumerate(pairs):
            if l in leds and m in leds:
                square = square + (1.0 if l == m else 2.0) * added[count + at : count + at + 1]
        cross = sum(added[cross_row + i : cross_row + i + 1] for i in range(len(leds)))
        cross_row += len(leds)
        inverse_mean.append(inverse)
        number.append(members * inverse)
        couple.append((members * square * inverse * inverse - cross * inverse) / area)

    def weigh(base, here, carry):
        outgoing = [[] for _ in range(count)]
        for a, c in enumerate(cut):
            camera, power = [], []
            for l in range(count):
                at = spot(l, base)
                re, im = ref.camera[0, at, c], ref.camera[1, at, c]
                camera.append((re, im))
                power.append(re * re + im * im)
            weight = [0.0] * count
            for k, leds in enumerate(lit_sets):
                lit = sum(power[l] for l in leds)
                pull = (lit * number[k] - ref.lit[k, here, c] - couple[k]) * inverse_mean[k]
                for l in leds:
                    weight[l] = weight[l] + pull
            for l in range(count):
                scale = 2.0 * weight[l]
                outgoing[l].append((scale * camera[l][0], scale * camera[l][1]))
        for l in range(count):
            scattered(l, base, outgoing[l])
        return carry

    each_chunk(weigh)
    each_led(lambda l: emit_band(b2, l))
    pupil_columns(b2, b3, -1.0)
    y3, y2, y1, y0 = port("y3"), port("y2"), port("y1"), port("y0")
    ref.grad[...] = jnp.zeros(ref.grad.shape, f32)

    def back_band(l):
        land(b3, l)
        inverse_band(b3, l)

        def chunk(base, here, carry):
            fields, at, blocks = gathered(l, base), spot(l, base), []
            for a, c in enumerate(cut):
                re, im = tilt(l, here, a, fields[a], -1.0)
                pr, pi = ref.passed2[0, at, c], ref.passed2[1, at, c]
                ref.grad[1, here, c] += pr * im - pi * re
                tr, ti = ref.tr[2, 0, here, c], ref.tr[2, 1, here, c]
                blocks.append((re * tr + im * ti, im * tr - re * ti))
            scattered(l, base, blocks)
            return carry

        each_chunk(chunk)

        @pl.when(l == count - 1)
        def _():
            trade_native("grad", 1)
            trade_foreign("grad", 1)

        emit_full(y3, l, l)

    each_led(back_band)
    columns(y3, y2, -1.0)
    forward_on("grad", 1)

    def back(l):
        land(y2, l)
        inverse_full(y2.y, l, l)

        def chunk(base, here, carry):
            fields, at, blocks = gathered(l, base), spot(l, base), []
            for a, c in enumerate(cut):
                re, im = fields[a]
                pr, pi = ref.passed1[0, at, c], ref.passed1[1, at, c]
                ref.grad[0, here, c] += pr * im - pi * re
                tr, ti = ref.tr[1, 0, here, c], ref.tr[1, 1, here, c]
                blocks.append((re * tr + im * ti, im * tr - re * ti))
            scattered(l, base, blocks)
            return carry

        each_chunk(chunk)

        @pl.when(l == count - 1)
        def _():
            trade_native("grad", 0)
            trade_foreign("grad", 0)

        emit_full(y1, l, l)

    each_led(back)
    ready("slab_own")
    phases(ref.slab_own, ref.tr.at[0])
    ref.cs[...] = jnp.zeros(ref.cs.shape, f32)

    def last(l):
        land(y1, l)
        spread(y1, l)

        def add(j, z):
            ref.cs[j] += shaped(z, l, j, -1.0)

        col_dot(ref.chi, ref.clo, add, 1.0)

    last(0)
    forward_on("grad", 0)
    lax.fori_loop(1, count, lambda l, carry: last(l) or carry, 0)
    for j in range(4):
        stow(j, ref.cs[j])
    col_inverse(y0, 0, leave_one, (3, 2, 1, 0))
    land(y0, 0)
    inverse_full(y0.y, 0, 0)

    def leave(base, here, carry):
        fields = gathered(0, base)
        for a, c in enumerate(cut):
            tr, ti = ref.tr[0, 0, here, c], ref.tr[0, 1, here, c]
            re, im = fields[a]
            ref.grad0[here, c] = tr * im - ti * re
        return carry

    each_chunk(leave)
    final = local(ref.grad0, ref.result.at[0], ref.loads.at[len(spec.loaded)])
    final.start()

    for x, slots in (
        (x0, 1), (x1, count), (x2, count), (x3, count), (b0, count), (b1, count), (b2, count), (b3, count),
        (sums, 1), (counts, 1), (y3, count), (y2, count), (y1, count), (y0, 1),
    ):
        drain(x, slots)
    for q in range(per):

        @pl.when(place == owners[q])
        def _():
            for jj in range(2):
                for w in range(2):
                    pupil_copy(jj, w, q).wait_send()

    for name in part:
        trade_ends(name)
    for k in range(2):
        traded("grad", k)

    @pl.when(foreign)
    def _():
        block = y0.stage.at[0, 0]
        local(block, block, y0.sent.at[0]).wait()

    final.wait()


def body(tiles, slab_phase, pupil_phase, pupil_mask, led_code, led_freq, measured):
    devs = lax.axis_size("pat")
    slab_count, rows, size = slab_phase.shape
    patterns, count = led_code.shape
    quarter, cols, per = size // 4, size // devs, devs // 4
    band = 2 * pupil_radius
    band_cols = band // devs
    rt = row_tables(size, cols, band // 4)
    ct = col_tables(size)
    sets = 2**count - 1
    stat_rows = count + count * (count + 1) // 2 + count * 2 ** (count - 1)
    owners = [(q - pupil_radius // cols) % devs for q in range(per)]
    loads = dict(
        row_twiddle=rt.twiddle, full=rt.full,
        col_twiddle=jnp.asarray(ct.twiddle), both=jnp.asarray(ct.both), full_inv=rt.full_inv, band=rt.band,
        band_inv=rt.band_inv, measured=measured,
    )
    inputs = {name + "_hbm": value for name, value in loads.items()}
    inputs |= dict(phase_hbm=pupil_phase, mask_hbm=pupil_mask, slab_hbm=slab_phase, freq=led_freq, code=led_code.T)
    wide = 2 * quarter
    total = count * rows
    vmem, dma = pltpu.VMEM, pltpu.SemaphoreType.DMA
    scratch = {name: vmem(value.shape, value.dtype) for name, value in loads.items()}
    loads["slab_own"] = None
    scratch["slab_own"] = vmem((rows, size), f32)
    scratch |= dict(
        slab=vmem(slab_phase.shape, f32), lit=vmem((sets, rows, size), f32), lit_own=vmem((sets, rows, size), f32),
        phase=vmem((2, rows, pupil_radius), f32), mask=vmem((2, rows, pupil_radius), jnp.int32),
        phase_sem=dma((2,)), mask_sem=dma((2,)), own=vmem((4, 2, rows // 4, band), f32), pupil=vmem((2, band_cols, band), f32), shape=vmem((2, 4 * band_cols, lanes), f32),
        tilt_c=vmem((2 * count, 1, size), f32), tilt_r=vmem((2 * count, rows, lanes), f32),
        prop=vmem((2, count, 4, quarter, lanes), f32), tr=vmem((3, 2, rows, size), f32),
        passed1=vmem((2, total, size), f32), passed2=vmem((2, total, size), f32),
        camera=vmem((2, total, size), f32), grad=vmem((2, rows, size), f32), grad0=vmem((rows, size), f32),
        hi=vmem((4, total, wide), bf16), lo=vmem((4, total, wide), bf16), zs=vmem((4, total, wide), f32),
        ghi=vmem((4 * rows, wide), bf16), glo=vmem((4 * rows, wide), bf16),
        chi=vmem((quarter, 4 * lanes), bf16), clo=vmem((quarter, 4 * lanes), bf16),
        dhi=vmem((quarter, 4 * lanes), bf16), dlo=vmem((quarter, 4 * lanes), bf16),
        cz=vmem((4, quarter, lanes), f32), cs=vmem((4, quarter, lanes), f32),
        loads=dma((len(loads) + 1,)),
        pupil_sent=dma((4,)), pupil_got=dma, piece_got=dma((2,)),
    )
    for name, blocks in (("slab", 3), ("lit", sets), ("grad", 2)):
        scratch[name + "_relay"] = vmem((blocks, rows // 2, size), f32)
        for kind in ("_sent", "_got", "_late", "_via"):
            scratch[name + kind] = dma((blocks,))
    block, narrow = (devs, rows, lanes), (devs, band_cols, lanes)
    ports = dict(x0=(1, block), x1=(count, block), x2=(count, block), x3=(count, block))
    ports |= dict(b0=(count, narrow), b1=(count, narrow), b2=(count, narrow), b3=(count, narrow))
    ports |= dict(sums=(1, (devs, -(-stat_rows // 8) * 8, lanes)))
    ports |= dict(counts=(1, (devs, -(-patterns // 8) * 8, lanes)))
    ports |= dict(y3=(count, block), y2=(count, block), y1=(count, block), y0=(1, block))
    for name, (slots, shape) in ports.items():
        scratch[name + "_stage"] = vmem((slots,) + shape, f32)
        scratch[name + "_y"] = vmem((slots,) + shape, f32)
        scratch[name + "_sent"] = dma((slots,))
        scratch[name + "_got"] = dma((slots,))
    spec = Names(
        count=count, rows=rows, quarter=quarter, devs=devs, tiles=tiles, patterns=patterns,
        area=float(size * size), stat_rows=stat_rows, sets=sets, owners=owners, loaded=list(loads),
        names=list(inputs) + ["result"] + list(scratch),
    )
    anywhere = pl.BlockSpec(memory_space=pl.ANY)
    smem = pl.BlockSpec(memory_space=pltpu.SMEM)
    return pl.pallas_call(
        functools.partial(whole_kernel, spec),
        out_shape=jax.ShapeDtypeStruct(slab_phase.shape, f32),
        in_specs=[smem if name in ("freq", "code") else anywhere for name in inputs],
        out_specs=anywhere,
        scratch_shapes=list(scratch.values()),
        compiler_params=pltpu.CompilerParams(
            collective_id=1, has_side_effects=True, vmem_limit_bytes=67043328
        ),
        name="whole",
    )(*inputs.values())


def solution(mesh):
    in_specs = (
        P("tiles", "pat", None),
        P("pat", None),
        P("pat", None),
        P(),
        P(),
        P("tiles", "pat", None),
    )
    out_specs = P("tiles", "pat", None)

    def run(slab_phase, *others):
        devs, tiles = mesh.shape["pat"], mesh.shape["tiles"]
        size, count = slab_phase.shape[-1], others[2].shape[1]
        fits = 2 * size == lanes * devs and count * size == lanes * devs and slab_phase.shape[0] == 3 * tiles
        fits = fits and tiles == 2 and devs == len(far_first)
        inner = functools.partial(body, tiles) if fits else plain_body
        return jax.shard_map(inner, mesh=mesh, in_specs=in_specs, out_specs=out_specs, check_vma=False)(
            slab_phase, *others
        )

    return run
```

```python
import functools
import math
import types

import jax
import jax.numpy as jnp
import numpy as np
from jax import lax
from jax.experimental import pallas as pl
from jax.experimental.pallas import tpu as pltpu
from jax.sharding import PartitionSpec as P

spread_rate = 0.3
highest = lax.Precision.HIGHEST


def frequency(grid_index, grid_size):
    return (grid_index + grid_size // 2) % grid_size - grid_size // 2


def complex_times(values, factor):
    real_part = values[0] * factor[0] - values[1] * factor[1]
    imag_part = values[0] * factor[1] + values[1] * factor[0]
    return jnp.stack([real_part, imag_part])


def dft_block(length, direction, norm_factor):
    grid_index = jnp.arange(length, dtype=jnp.int32)
    angles = (grid_index[:, None] * grid_index[None, :] % length).astype(jnp.float32) * (
        2.0 * math.pi / length
    )
    cosine = jnp.cos(angles) * norm_factor
    signed_sine = direction * jnp.sin(angles) * norm_factor
    real_rows = jnp.stack([cosine, signed_sine], 1)
    imag_rows = jnp.stack([-signed_sine, cosine], 1)
    return jnp.stack([real_rows, imag_rows], 0)


def twiddle_table(short_size, long_size, grid_size, direction):
    short_index = jnp.arange(short_size, dtype=jnp.int32)
    long_index = jnp.arange(long_size, dtype=jnp.int32)
    angles = (short_index[:, None] * long_index[None, :] % grid_size).astype(jnp.float32) * (
        2.0 * math.pi / grid_size
    )
    return jnp.stack([jnp.cos(angles), direction * jnp.sin(angles)])


def table_set(col_count, dev_count, grid_size, direction):
    short_table = dft_block(col_count, direction, 1.0)
    long_table = dft_block(dev_count, direction, 1.0 / math.sqrt(grid_size))
    return (short_table, long_table, twiddle_table(col_count, dev_count, grid_size, direction))


def to_fourier(wave_field, tables, dev_count):
    short_table, long_table, twiddles = tables
    led_count = wave_field.shape[1]
    row_count = wave_field.shape[2]
    grid_size = wave_field.shape[3]
    col_count = grid_size // dev_count
    shaped = wave_field.reshape(2, led_count, row_count, col_count, dev_count)
    sectioned = jnp.einsum("zlrmq,zmwc->wlrcq", shaped, short_table, precision=highest)
    sectioned = complex_times(sectioned, twiddles)
    outgoing = jnp.einsum("wlrcq,wqvd->dvlcr", sectioned, long_table, precision=highest)
    incoming = lax.all_to_all(
        outgoing.reshape(dev_count, -1), "pat", split_axis=0, concat_axis=0, tiled=True
    )
    incoming = incoming.reshape(dev_count, 2, led_count, col_count, row_count)
    sectioned = jnp.einsum("swlcr,wsvj->vlcrj", incoming, long_table, precision=highest)
    sectioned = complex_times(sectioned, twiddles)
    sectioned = jnp.einsum("wlcrj,wrvh->vlchj", sectioned, short_table, precision=highest)
    return sectioned.reshape(2, led_count, col_count, grid_size)


def to_space(spectrum, tables, dev_count):
    short_table, long_table, twiddles = tables
    led_count = spectrum.shape[1]
    col_count = spectrum.shape[2]
    grid_size = spectrum.shape[3]
    row_count = grid_size // dev_count
    shaped = spectrum.reshape(2, led_count, col_count, row_count, dev_count)
    sectioned = jnp.einsum("zlcmq,zmwr->wlcrq", shaped, short_table, precision=highest)
    sectioned = complex_times(sectioned, twiddles)
    outgoing = jnp.einsum("wlcrq,wqvd->dvlcr", sectioned, long_table, precision=highest)
    incoming = lax.all_to_all(
        outgoing.reshape(dev_count, -1), "pat", split_axis=0, concat_axis=0, tiled=True
    )
    incoming = incoming.reshape(dev_count, 2, led_count, col_count, row_count)
    sectioned = jnp.einsum("swlcr,wsvj->vlrcj", incoming, long_table, precision=highest)
    sectioned = complex_times(sectioned, twiddles)
    sectioned = jnp.einsum("wlrcj,wcvh->vlrhj", sectioned, short_table, precision=highest)
    return sectioned.reshape(2, led_count, row_count, grid_size)


def plain_body(slab_phase, pupil_phase, pupil_mask, led_code, led_freq, measured):
    dev_count = lax.axis_size("pat")
    position = lax.axis_index("pat")
    slab_count, row_count, grid_size = slab_phase.shape
    col_count = grid_size // dev_count
    pattern_count, led_count = led_code.shape
    area = float(grid_size * grid_size)
    forward_set = table_set(col_count, dev_count, grid_size, -1.0)
    inverse_set = table_set(col_count, dev_count, grid_size, 1.0)
    conjugate = jnp.array([1.0, -1.0], jnp.float32)[:, None, None]
    col_freq = frequency(position * col_count + jnp.arange(col_count, dtype=jnp.int32), grid_size)
    row_freq = frequency(jnp.arange(grid_size, dtype=jnp.int32), grid_size)
    radius = col_freq[:, None] * col_freq[:, None] + row_freq[None, :] * row_freq[None, :]
    cutoff = grid_size // 2 * (grid_size // 2)
    inside = radius <= cutoff
    height = jnp.sqrt(jnp.maximum(cutoff - radius, 0).astype(jnp.float32))
    phase_shift = spread_rate * (height - grid_size // 2)
    propagator = jnp.stack(
        [jnp.where(inside, jnp.cos(phase_shift), 0.0), jnp.where(inside, jnp.sin(phase_shift), 0.0)]
    )
    opening = pupil_mask.astype(jnp.float32)
    pupil = jnp.stack([opening * jnp.cos(pupil_phase), opening * jnp.sin(pupil_phase)])
    propagator_conj = propagator * conjugate
    pupil_conj = pupil * conjugate
    row_index = position * row_count + jnp.arange(row_count, dtype=jnp.int32)
    col_index = jnp.arange(grid_size, dtype=jnp.int32)
    tilt_index = (
        led_freq[:, 0][:, None, None] * row_index[None, :, None]
        + led_freq[:, 1][:, None, None] * col_index[None, None, :]
    ) % grid_size
    tilt_angle = tilt_index.astype(jnp.float32) * (2.0 * math.pi / grid_size)
    illumination = jnp.stack([jnp.cos(tilt_angle), jnp.sin(tilt_angle)])
    transmission = jnp.stack([jnp.cos(slab_phase), jnp.sin(slab_phase)])
    group_count = 1
    group_size = led_count // group_count
    wave_groups = [illumination]
    passed_groups = []
    for slab_index in range(slab_count):
        factor = transmission[:, slab_index]
        passed = [complex_times(wave_field, factor) for wave_field in wave_groups]
        passed_groups.append(passed)
        spectral_factor = propagator if slab_index < slab_count - 1 else pupil
        wave_groups = [
            to_space(
                complex_times(to_fourier(passed_field, forward_set, dev_count), spectral_factor),
                inverse_set,
                dev_count,
            )
            for passed_field in passed
        ]
    camera = wave_groups[0]
    led_power = camera[0] * camera[0] + camera[1] * camera[1]
    code_float = led_code.astype(jnp.float32)
    pattern_power = jnp.dot(
        code_float, led_power.reshape(led_count, -1), precision=highest
    ).reshape(pattern_count, row_count, grid_size)
    counts = measured.astype(jnp.float32)
    power_sum, count_sum = lax.psum(
        (jnp.sum(pattern_power, axis=(1, 2)), jnp.sum(counts, axis=(1, 2))), "pat"
    )
    mean_power = power_sum / area
    mean_count = count_sum / area
    relative = pattern_power / mean_power[:, None, None]
    misfit = relative - counts / mean_count[:, None, None]
    coupling = lax.psum(jnp.sum(misfit * relative, axis=(1, 2)), "pat") / area
    pattern_weight = (misfit - coupling[:, None, None]) / mean_power[:, None, None]
    led_weight = jnp.dot(
        code_float.T, pattern_weight.reshape(pattern_count, -1), precision=highest
    ).reshape(led_count, row_count, grid_size)
    camera_adjoint = 2.0 * led_weight[None] * camera
    adjoint_groups = [camera_adjoint]
    gradients = [None] * slab_count
    for slab_index in range(slab_count - 1, -1, -1):
        spectral_factor = pupil_conj if slab_index == slab_count - 1 else propagator_conj
        back_groups = [
            to_space(
                complex_times(to_fourier(adjoint_field, forward_set, dev_count), spectral_factor),
                inverse_set,
                dev_count,
            )
            for adjoint_field in adjoint_groups
        ]
        gradient = jnp.zeros((row_count, grid_size), jnp.float32)
        for passed_field, back_field in zip(passed_groups[slab_index], back_groups):
            gradient = jnp.sum(
                passed_field[0] * back_field[1] - passed_field[1] * back_field[0], axis=0
            )
        gradients[slab_index] = gradient
        if slab_index > 0:
            release = transmission[:, slab_index] * conjugate
            adjoint_groups = [complex_times(back_field, release) for back_field in back_groups]
    return jnp.stack(gradients)


class Names(types.SimpleNamespace):
    def __getitem__(self, name):
        return getattr(self, name)


pupil_radius = 128
lanes = 128
f32 = jnp.float32
bf16 = jnp.bfloat16


def halves(table):
    table32 = np.asarray(table, np.float32)
    high = table32.astype(bf16)
    low = (table32 - high.astype(np.float32)).astype(bf16)
    return np.stack([high, low])


def row_tables(size, block, band_block):
    quarter = size // 4
    pos = np.arange(quarter)
    angle = 2.0 * np.pi * ((pos[:, None] * pos[None, :]) % quarter) / quarter
    cosine = np.cos(angle) / math.sqrt(size)
    sine = np.sin(angle) / math.sqrt(size)

    def forward(freqs, width):
        parts = []
        for first in range(0, len(freqs), width):
            pick = freqs[first : first + width] % quarter
            left = np.concatenate([cosine[:, pick], sine[:, pick]], 0)
            right = np.concatenate([-sine[:, pick], cosine[:, pick]], 0)
            parts.append(np.concatenate([left, right], 1))
        return np.concatenate(parts, 1)

    full = forward(pos, block)
    reach = pupil_radius // 4
    band = forward(np.arange(-reach, reach), band_block)
    theta = 2.0 * np.pi * (np.arange(4)[:, None] * pos[None, :]) / size
    twiddle = np.concatenate([np.cos(theta), np.sin(theta)], 0).astype(np.float32)
    return Names(
        full=jnp.asarray(halves(full)),
        full_inv=jnp.asarray(halves(full.T)),
        band=jnp.asarray(halves(band)),
        band_inv=jnp.asarray(halves(band.T)),
        twiddle=jnp.asarray(twiddle),
    )


def col_tables(size):
    quarter = size // 4
    pos = np.arange(quarter)
    angle = 2.0 * np.pi * ((pos[:, None] * pos[None, :]) % quarter) / quarter
    both = np.concatenate([np.cos(angle), np.sin(angle)], 0) / math.sqrt(size)
    theta = 2.0 * np.pi * (np.arange(1, 4)[:, None] * pos[None, :]) / size
    twiddle = np.stack([np.cos(theta), np.sin(theta)]).astype(np.float32)
    twiddle = np.ascontiguousarray(np.broadcast_to(twiddle[..., None], twiddle.shape + (lanes,)))
    return Names(both=halves(both), twiddle=twiddle)


def split(value):
    high = value.astype(bf16)
    return high, (value - high.astype(f32)).astype(bf16)


def dot3(left, right):
    def dot(a, b):
        return jnp.dot(a, b, preferred_element_type=f32)

    return dot(left[0], right[0]) + (dot(left[0], right[1]) + dot(left[1], right[0]))


def turn(value):
    rolled = pltpu.roll(value, lanes // 2, 1)
    lane = lax.broadcasted_iota(jnp.int32, value.shape, 1)
    return jnp.where(lane < lanes // 2, rolled, -rolled)


def row_spread(blocks, twiddle_ref):
    (r0, i0), (r1, i1), (r2, i2), (r3, i3) = blocks
    sr, si, tr, ti = r0 + r2, i0 + i2, r1 + r3, i1 + i3
    dr, di, er, ei = r0 - r2, i0 - i2, r1 - r3, i1 - i3
    mixed = [(sr + tr, si + ti), (dr + ei, di - er), (sr - tr, si - ti), (dr - ei, di + er)]
    out = [mixed[0]]
    for j in range(1, 4):
        cosine, sine = twiddle_ref[j : j + 1, :], twiddle_ref[4 + j : 5 + j, :]
        re, im = mixed[j]
        out.append((re * cosine + im * sine, im * cosine - re * sine))
    return out


def row_gather(parts, twiddle_ref):
    g = [parts[0]]
    for j in range(1, 4):
        cosine, sine = twiddle_ref[j : j + 1, :], twiddle_ref[4 + j : 5 + j, :]
        re, im = parts[j]
        g.append((re * cosine - im * sine, im * cosine + re * sine))
    (r0, i0), (r1, i1), (r2, i2), (r3, i3) = g
    sr, si, tr, ti = r0 + r2, i0 + i2, r1 + r3, i1 + i3
    dr, di, er, ei = r0 - r2, i0 - i2, r1 - r3, i1 - i3
    return [(sr + tr, si + ti), (dr - ei, di + er), (sr - tr, si - ti), (dr + ei, di - er)]


mesh_ids = pl.DeviceIdType.MESH
far_first = (14, 15, 6, 7, 10, 11, 12, 13, 2, 3, 4, 5, 8, 9, 1, 0)


def flip(index, mask):
    out = index
    for bit in (1, 2, 4, 8):
        if mask & bit:
            out = out + bit - 2 * bit * lax.rem(index // bit, 2)
    return out


def whole_kernel(spec, *refs):
    ref = Names(**dict(zip(spec.names, refs)))
    count, rows, quarter, devs, patterns = spec.count, spec.rows, spec.quarter, spec.devs, spec.patterns
    size, per, half, step = 4 * quarter, devs // 4, devs // 2, 16
    tile, place = lax.axis_index("tiles"), lax.axis_index("pat")
    work = place // half
    me = half * tile + lax.rem(place, half)
    native = tile == work
    foreign = jnp.logical_not(native)
    other = dict(tiles=1 - tile, pat=lax.rem(place + half, devs))

    def member(index):
        return dict(tiles=index // half, pat=work * half + lax.rem(index, half))

    barrier = pltpu.get_barrier_semaphore()
    everyone = spec.tiles * devs

    def signal(hop, carry):
        target = lax.rem(tile * devs + place + hop, everyone)
        pl.semaphore_signal(
            barrier, inc=1, device_id=dict(tiles=target // devs, pat=lax.rem(target, devs)),
            device_id_type=mesh_ids,
        )
        return carry

    lax.fori_loop(1, everyone, signal, 0)

    def local(source, target, sem):
        return pltpu.make_async_copy(source, target, sem)

    def away(source, target, sent, got, device):
        return pltpu.make_async_remote_copy(
            src_ref=source, dst_ref=target, send_sem=sent, recv_sem=got, device_id=device,
            device_id_type=mesh_ids,
        )

    def fetch(name):
        source = ref.slab_hbm.at[0] if name == "slab_own" else ref[name + "_hbm"]
        return local(source, ref[name], ref.loads.at[spec.loaded.index(name)])

    reach = pupil_radius
    spans = (slice(size - reach, size), slice(0, reach))

    def near(name, k):
        return local(ref[name + "_hbm"].at[:, spans[k]], ref[name].at[k], ref[name + "_sem"].at[k])

    for name in ("phase", "mask"):
        for k in range(2):
            near(name, k).start()
    for name in spec.loaded:
        fetch(name).start()

    def ready(name):
        fetch(name).wait()

    share = rows // 2
    neighbour = dict(tiles=1 - tile, pat=place)
    across = dict(tiles=tile, pat=lax.rem(place + half, devs))

    sources = dict(slab=ref.slab_hbm, lit=ref.lit_own, grad=ref.grad)
    targets = dict(slab=ref.slab, lit=ref.lit, grad=ref.result.at[1:3])
    part = dict(slab=3, lit=spec.sets, grad=2)

    def semaphore(name, kind, k):
        return ref[name + kind].at[k]

    def direct(name, k):
        return away(
            sources[name].at[k, :share], targets[name].at[k, :share], semaphore(name, "_sent", k),
            semaphore(name, "_got", k), other,
        )

    def hop(name, k):
        return away(
            sources[name].at[k, share:], ref[name + "_relay"].at[k], semaphore(name, "_sent", k),
            semaphore(name, "_via", k), neighbour,
        )

    def onward(name, k):
        return away(
            ref[name + "_relay"].at[k], targets[name].at[k, share:], semaphore(name, "_sent", k),
            semaphore(name, "_late" if name == "slab" else "_got", k), across,
        )

    def trade_native(name, k):
        @pl.when(native)
        def _():
            if name == "slab":
                for span, kind in ((pl.ds(0, share), "_got"), (pl.ds(share, share), "_late")):
                    local(sources[name].at[k, span], targets[name].at[k, span], semaphore(name, kind, k)).start()
            else:
                local(sources[name].at[k], targets[name].at[k], semaphore(name, "_got", k)).start()

    def trade_foreign(name, *blocks):
        @pl.when(foreign)
        def _():
            for k in blocks:
                direct(name, k).start()
                hop(name, k).start()

    def forward_on(name, *blocks):
        @pl.when(native)
        def _():
            for k in blocks:
                hop(name, k).wait_recv()
                onward(name, k).start()

    def traded(name, k):
        whole = targets[name].at[k]
        if name == "slab":
            halves = (whole.at[:share], whole.at[share:])
            local(halves[0], halves[0], semaphore(name, "_got", k)).wait()
            local(halves[1], halves[1], semaphore(name, "_late", k)).wait()
        else:
            local(whole, whole, semaphore(name, "_got", k)).wait()

    def trade_ends(name):
        for k in range(part[name]):

            @pl.when(native)
            def _():
                onward(name, k).wait_send()

            @pl.when(foreign)
            def _():
                whole = sources[name].at[k]
                local(whole, whole, semaphore(name, "_sent", k)).wait()

    def port(name):
        return Names(
            stage=ref[name + "_stage"], y=ref[name + "_y"], sent=ref[name + "_sent"], got=ref[name + "_got"]
        )

    def push_one(x, slot, mask, span=None):
        dest = flip(me, mask)
        source = x.stage.at[slot, dest] if span is None else x.stage.at[slot, dest, span]
        target = x.y.at[slot, me] if span is None else x.y.at[slot, me, span]
        if mask:
            away(source, target, x.sent.at[slot], x.got.at[slot], member(dest)).start()
        else:
            local(source, target, x.got.at[slot]).start()

    def push(x, slot):
        for mask in far_first:
            push_one(x, slot, mask)

    def leave_one(x, slot, mask):
        dest = flip(place, mask)

        def start_away():
            away(
                x.stage.at[slot, dest], x.y.at[slot, me], x.sent.at[slot], x.got.at[slot],
                dict(tiles=work, pat=dest),
            ).start()

        if mask:
            start_away()
        else:

            @pl.when(native)
            def _():
                local(x.stage.at[slot, dest], x.y.at[slot, me], x.got.at[slot]).start()

            pl.when(foreign)(start_away)

    def land(x, slot):
        local(x.y.at[slot], x.y.at[slot], x.got.at[slot]).wait()

    def drain(x, slots):
        for slot in range(slots):
            part = x.stage.at[slot, pl.ds(0, devs - 1)]
            local(part, part, x.sent.at[slot]).wait()

    hi, lo, zs = ref.hi, ref.lo, ref.zs
    cut = [slice(a * quarter, (a + 1) * quarter) for a in range(4)]

    def spot(l, base):
        return pl.ds(pl.multiple_of(l * rows + base, step), step)

    def each_chunk(chunk, carry=0):
        def at_chunk(i, carry):
            base = pl.multiple_of(i * step, step)
            return chunk(base, pl.ds(base, step), carry)

        return lax.fori_loop(0, rows // step, at_chunk, carry)

    def gathered(l, base):
        at = spot(l, base)
        parts = [(zs[j, at, :quarter], zs[j, at, quarter:]) for j in range(4)]
        return row_gather(parts, ref.row_twiddle)

    def scattered(l, base, blocks):
        at = spot(l, base)
        for j, (re, im) in enumerate(row_spread(blocks, ref.row_twiddle)):
            high, low = split(re)
            hi[j, at, :quarter] = high
            lo[j, at, :quarter] = low
            high, low = split(im)
            hi[j, at, quarter:] = high
            lo[j, at, quarter:] = low

    def led_rows(l):
        return pl.ds(pl.multiple_of(l * rows, rows), rows)

    def inverse_full(y, slot, l):
        for j in range(4):
            for q in range(per):
                high, low = split(y[slot, per * j + q])
                ref.ghi[j * rows : (j + 1) * rows, q * lanes : (q + 1) * lanes] = high
                ref.glo[j * rows : (j + 1) * rows, q * lanes : (q + 1) * lanes] = low
        value = dot3((ref.ghi[...], ref.glo[...]), (ref.full_inv[0], ref.full_inv[1]))
        zs[:, led_rows(l), :] = value.reshape(4, rows, 2 * quarter)

    def emit_full(x, slot, l):
        left = [part[:, led_rows(l), :].reshape(4 * rows, 2 * quarter) for part in (hi, lo)]
        value = dot3(left, (ref.full[0], ref.full[1]))
        for j in range(4):
            for q in range(per):
                x.stage[slot, per * j + q] = value[j * rows : (j + 1) * rows, q * lanes : (q + 1) * lanes]
        push(x, slot)

    def braid(first, second):
        middle = lanes // 2
        lane = lax.broadcasted_iota(jnp.int32, first.shape, 1)
        return (
            jnp.where(lane < middle, first, pltpu.roll(second, middle, 1)),
            jnp.where(lane < middle, pltpu.roll(first, middle, 1), second),
        )

    def inverse_band(x, l):
        for pair in range(2):
            turned = x.y[l, 2 * per * pair : 2 * per * (pair + 1)].reshape(lanes, lanes).T
            for k, block in enumerate(braid(turned[:rows], turned[rows:])):
                at = slice((2 * pair + k) * rows, (2 * pair + k + 1) * rows)
                high, low = split(block)
                ref.ghi[at, :lanes] = high
                ref.glo[at, :lanes] = low
        value = dot3((ref.ghi[:, :lanes], ref.glo[:, :lanes]), (ref.band_inv[0], ref.band_inv[1]))
        zs[:, led_rows(l), :] = value.reshape(4, rows, 2 * quarter)

    def emit_band(x, l):
        left = [part[:, led_rows(l), :].reshape(4 * rows, 2 * quarter) for part in (hi, lo)]
        flipped = dot3(left, (ref.band[0], ref.band[1])).T
        deep = x.y.shape[2]
        for pair in range(2):
            at = slice(pair * lanes, (pair + 1) * lanes)
            for k, block in enumerate(braid(flipped[:rows, at], flipped[rows:, at])):
                for q in range(per):
                    x.stage[l, per * (2 * pair + k) + q] = block[q * deep : (q + 1) * deep]
        push(x, l)

    def tilt(l, here, a, value, sign):
        rc, rs = ref.tilt_r[2 * l, here, :], ref.tilt_r[2 * l + 1, here, :]
        cc, cs = ref.tilt_c[2 * l, :, cut[a]], ref.tilt_c[2 * l + 1, :, cut[a]]
        rc = jnp.concatenate([rc] * (quarter // lanes), 1)
        rs = jnp.concatenate([rs] * (quarter // lanes), 1)
        er = rc * cc - rs * cs
        ei = sign * (rc * cs + rs * cc)
        re, im = value
        return re * er - im * ei, re * ei + im * er

    def spread(x, slot):
        def at_part(i, carry):
            here = pl.ds(pl.multiple_of(i * rows, rows), rows)
            x0, x1, x2, x3 = [x.y[slot, per * a + i] for a in range(4)]
            s, t, d, e = x0 + x2, x1 + x3, x0 - x2, turn(x1 - x3)
            for j, value in enumerate((s + t, d + e, s - t, d - e)):
                if j:
                    value = value * ref.col_twiddle[0, j - 1, here, :] + turn(value) * ref.col_twiddle[1, j - 1, here, :]
                high, low = split(value)
                ref.chi[here, j * lanes : (j + 1) * lanes] = high
                ref.clo[here, j * lanes : (j + 1) * lanes] = low
            return carry

        lax.fori_loop(0, per, at_part, 0)

    def col_dot(high, low, take, sign):
        for pair in range(2):
            at = slice(2 * pair * lanes, 2 * (pair + 1) * lanes)
            y = dot3((ref.both[0], ref.both[1]), (high[:, at], low[:, at]))
            for k in range(2):
                at = slice(k * lanes, (k + 1) * lanes)
                take(2 * pair + k, y[:quarter, at] + sign * turn(y[quarter:, at]))

    def shaped(z, l, j, sign):
        return z * ref.prop[0, l, j] - sign * (turn(z) * ref.prop[1, l, j])

    def stow(j, value):
        high, low = split(value)
        ref.dhi[:, j * lanes : (j + 1) * lanes] = high
        ref.dlo[:, j * lanes : (j + 1) * lanes] = low

    def col_inverse(x, slot, send=push_one, far_parts=(3, 1, 2, 0)):
        def take(j, value):
            if j:
                value = value * ref.col_twiddle[0, j - 1] - turn(value) * ref.col_twiddle[1, j - 1]
            ref.cz[j] = value

        col_dot(ref.dhi, ref.dlo, take, -1.0)
        home = lax.rem(me, per)
        for bits in (3, 2, 1, 0):
            i = flip(home, bits)
            here = pl.ds(pl.multiple_of(i * rows, rows), rows)
            g0, g1, g2, g3 = [ref.cz[j, here, :] for j in range(4)]
            s, t, d, e = g0 + g2, g1 + g3, g0 - g2, turn(g1 - g3)
            for a, value in enumerate((s + t, d - e, s - t, d + e)):
                x.stage[slot, per * a + i] = value
            for far in far_parts:
                send(x, slot, per * far + bits)

    def each_led(stage):
        def at_led(l, carry):
            stage(l)
            return carry

        lax.fori_loop(0, count, at_led, 0)

    def columns(x, out, sign):
        def stage(l):
            land(x, l)
            spread(x, l)
            col_dot(ref.chi, ref.clo, lambda j, z: stow(j, shaped(z, l, j, sign)), 1.0)
            col_inverse(out, l)

        each_led(stage)

    def pupil_columns(x, out, sign):
        deep = x.y.shape[2]

        def stage(l):
            land(x, l)
            blocks = []
            for a in range(4):
                pairs = [braid(x.y[l, s], x.y[l, s + 1]) for s in range(per * a, per * (a + 1), 2)]
                blocks.append(tuple(jnp.concatenate([pair[k] for pair in pairs], 1) for k in range(2)))
            mixed = [jnp.concatenate(part, 1) for part in row_spread(blocks, ref.row_twiddle)]
            z = dot3(split(jnp.concatenate(mixed, 0)), (ref.band[0], ref.band[1]))
            if sign < 0.0:
                z = z - ref.pulled[l] * ref.spectrum[l]
            z = z * ref.shape[0] + sign * (pltpu.roll(z, lanes // 2, 1) * ref.shape[1])
            if sign > 0.0:
                ref.spectrum[l] = z
                ref.energy[l] = jnp.sum(z * z, 0, keepdims=True)
            y = dot3(split(z), (ref.band_inv[0], ref.band_inv[1]))
            parts = [(y[j * deep : (j + 1) * deep, :quarter], y[j * deep : (j + 1) * deep, quarter:]) for j in range(4)]
            for a, (re, im) in enumerate(row_gather(parts, ref.row_twiddle)):
                for k in range(quarter // lanes):
                    at = slice(k * lanes, (k + 1) * lanes)
                    first, second = braid(re[:, at], im[:, at])
                    out.stage[l, per * a + 2 * k] = first
                    out.stage[l, per * a + 2 * k + 1] = second
            push(out, l)

        each_led(stage)

    def shape_pupil():
        local(ref.pupil, ref.pupil, ref.pupil_got).wait()
        band, deep = ref.pupil.shape[2], ref.pupil.shape[1]
        freq = lax.broadcasted_iota(jnp.int32, (band, 4 * lanes), 0)
        slot = lax.broadcasted_iota(jnp.int32, (band, 4 * lanes), 1)
        wanted = 4 * lax.rem(slot, lanes // 2) + slot // lanes
        pick = jnp.where(freq == wanted, 1.0, 0.0).astype(bf16)
        value, out = ref.pupil[...].reshape(2 * deep, band), 0.0
        for k in range(3):
            high = value.astype(bf16)
            out = out + jnp.dot(high, pick, preferred_element_type=f32)
            value = value - high.astype(f32)
        lane = lax.broadcasted_iota(jnp.int32, (deep, lanes), 1)
        for j in range(4):
            at = slice(j * lanes, (j + 1) * lanes)
            ref.shape[0, j * deep : (j + 1) * deep] = out[:deep, at]
            ref.shape[1, j * deep : (j + 1) * deep] = jnp.where(lane < lanes // 2, -out[deep:, at], out[deep:, at])

    def phases(source, target):
        def chunk(base, here, carry):
            phase = source[here, :]
            target[0, here, :] = jnp.cos(phase)
            target[1, here, :] = jnp.sin(phase)
            return carry

        each_chunk(chunk)

    def fold(value):
        total_rows = value[:8]
        for k in range(1, value.shape[0] // 8):
            total_rows = total_rows + value[8 * k : 8 * k + 8]
        out = total_rows[:, :lanes]
        for k in range(1, value.shape[1] // lanes):
            out = out + total_rows[:, lanes * k : lanes * (k + 1)]
        return out

    def fold_all(p):
        def chunk(base, here, carry):
            return carry + fold(ref.measured[p, here, :].astype(f32))

        return jnp.sum(each_chunk(chunk, jnp.zeros((8, lanes), f32)), 0, keepdims=True)

    def slab_phases(s):
        traded("slab", s)
        phases(ref.slab.at[s], ref.tr.at[s])

    for k in range(3):
        trade_native("slab", k)
    turn_size = 2.0 * math.pi / size
    col = lax.broadcasted_iota(jnp.int32, (8, size), 1)
    row = me * rows + lax.broadcasted_iota(jnp.int32, (rows, lanes), 0)
    for l in range(count):
        for index, freq, tilts in ((col, ref.freq[l, 1], ref.tilt_c), (row, ref.freq[l, 0], ref.tilt_r)):
            angle = jnp.bitwise_and(index * freq, size - 1).astype(f32) * turn_size
            deep = tilts.shape[1]
            tilts[2 * l] = jnp.cos(angle)[:deep]
            tilts[2 * l + 1] = jnp.sin(angle)[:deep]

    pl.semaphore_wait(barrier, everyone - 1)
    pieces = (pl.ds(0, share // 2), pl.ds(share // 2, share // 2))

    def piece(source, target, sent, k, device):
        return away(source, target, sent, ref.piece_got.at[k], device)

    def first_hop(k):
        at = pieces[k]
        return piece(
            sources["slab"].at[0, share:].at[at], ref.slab_relay.at[0, at], semaphore("slab", "_sent", 0), k, neighbour
        )

    def first_onward(k):
        at = pieces[k]
        return away(
            ref.slab_relay.at[0, at], targets["slab"].at[0, share:].at[at], semaphore("slab", "_sent", 0),
            semaphore("slab", "_late", 0), across,
        )

    @pl.when(foreign)
    def _():
        direct("slab", 0).start()
        for k in range(2):
            first_hop(k).start()

    ready("row_twiddle")
    ready("full")
    x0, x1, x2, x3 = port("x0"), port("x1"), port("x2"), port("x3")

    def enter(first, count_rows):
        def chunk(i, carry):
            base = pl.multiple_of(first + i * step, step)
            here = pl.ds(base, step)
            blocks = []
            for c in cut:
                phase = ref.slab[0, here, c]
                blocks.append((jnp.cos(phase), jnp.sin(phase)))
            scattered(0, base, blocks)
            return carry

        lax.fori_loop(0, count_rows // step, chunk, 0)
        span = pl.ds(first, count_rows)
        left = [part[:, span, :].reshape(4 * count_rows, 2 * quarter) for part in (hi, lo)]
        value = dot3(left, (ref.full[0], ref.full[1]))
        for j in range(4):
            for q in range(per):
                x0.stage[0, per * j + q, span] = value[
                    j * count_rows : (j + 1) * count_rows, q * lanes : (q + 1) * lanes
                ]
        for mask in far_first:
            push_one(x0, 0, mask, span)


    for name in ("phase", "mask"):
        for k in range(2):
            near(name, k).wait()
    for j in range(4):
        line = pl.ds(j, rows // 4, stride=4)
        for k in range(2):
            opening = ref.mask[k, line, :].astype(f32)
            angle = ref.phase[k, line, :]
            at = slice(k * reach, (k + 1) * reach)
            ref.own[j, 0, :, at] = opening * jnp.cos(angle)
            ref.own[j, 1, :, at] = opening * jnp.sin(angle)
    owners = spec.owners

    def pupil_copy(jj, w, q):
        return away(
            ref.own.at[2 * tile + jj], ref.pupil, ref.pupil_sent.at[2 * jj + w], ref.pupil_got,
            dict(tiles=tile, pat=w * half + jj * per + q),
        )

    for q in range(per):

        @pl.when(place == owners[q])
        def _():
            for jj in range(2):
                for w in range(2):
                    pupil_copy(jj, w, q).start()


    @pl.when(native)
    def _():
        for k in range(2):
            first_hop(k).wait_recv()
            first_onward(k).start()
        traded("slab", 0)
        enter(0, rows)

    cutoff = size // 2 * (size // 2)

    def centred(index):
        return jnp.where(index >= size // 2, index - size, index)

    def spectrum(i, carry):
        here = pl.ds(pl.multiple_of(i * step, step), step)
        row = lax.broadcasted_iota(jnp.int32, (step, lanes), 0) + i * step
        lane = lax.broadcasted_iota(jnp.int32, (step, lanes), 1)
        lane = jnp.where(lane < lanes // 2, lane, lane - lanes // 2)
        col = 4 * (lax.rem(me, per) * (lanes // 2) + lane) + me // per
        for l in range(count):
            v = centred(col + ref.freq[l, 1])
            for j in range(4):
                u = centred(4 * row + j + ref.freq[l, 0])
                radius = u * u + v * v
                inside = radius <= cutoff
                height = jnp.sqrt(jnp.maximum(cutoff - radius, 0).astype(f32))
                shift = spread_rate * (height - float(size // 2))
                ref.prop[0, l, j, here, :] = jnp.where(inside, jnp.cos(shift), 0.0)
                ref.prop[1, l, j, here, :] = jnp.where(inside, jnp.sin(shift), 0.0)
        return carry

    lax.fori_loop(0, quarter // step, spectrum, 0)

    @pl.when(foreign)
    def _():
        direct("slab", 0).wait_recv()
        enter(0, share)
        onward("slab", 0).wait_recv()
        enter(share, rows - share)


    ready("measured")
    counts = port("counts")
    lines = [fold_all(p) for p in range(patterns)]
    lines.append(jnp.zeros((counts.stage.shape[2] - patterns, lanes), f32))
    lines = jnp.concatenate(lines, 0)
    for d in range(devs):
        counts.stage[0, d] = lines
    for mask in far_first:
        dest = flip(place, mask)
        if mask:
            away(
                counts.stage.at[0, dest], counts.y.at[0, place], counts.sent.at[0], counts.got.at[0],
                dict(tiles=tile, pat=dest),
            ).start()
        else:
            local(counts.stage.at[0, dest], counts.y.at[0, place], counts.got.at[0]).start()
    ready("col_twiddle")
    ready("both")
    ready("full_inv")
    trade_foreign("slab", 1)
    land(x0, 0)
    forward_on("slab", 1)
    spread(x0, 0)

    def keep_spectrum(j, z):
        ref.cs[j] = z

    col_dot(ref.chi, ref.clo, keep_spectrum, 1.0)

    def first(l):
        for j in range(4):
            stow(j, shaped(ref.cs[j], l, j, 1.0))
        col_inverse(x1, l)

    each_led(first)
    trade_foreign("slab", 2)
    land(counts, 0)
    count_sum = jnp.sum(jnp.sum(counts.y[0], 0), 1, keepdims=True)
    area = spec.area
    code = [[ref.code[l, p].astype(f32) for l in range(count)] for p in range(patterns)]
    lit_sets = [[l for l in range(count) if (c + 1) >> l & 1] for c in range(spec.sets)]
    member_of = []
    for leds in lit_sets:
        member_of.append([])
        for p in range(patterns):
            is_in = 1.0
            for l in range(count):
                is_in = is_in * (code[p][l] if l in leds else 1.0 - code[p][l])
            member_of[-1].append(is_in)
    share_of = [[member_of[c][p] * (area / count_sum[p : p + 1]) for p in range(patterns)] for c in range(spec.sets)]

    def gather_counts(base, here, carry):
        for c in cut:
            seen = [ref.measured[p, here, c].astype(f32) for p in range(patterns)]
            for k in range(spec.sets):
                ref.lit_own[k, here, c] = sum(share_of[k][p] * seen[p] for p in range(patterns))
        return carry

    each_chunk(gather_counts)
    for k in range(spec.sets):
        trade_native("lit", k)
    trade_foreign("lit", 0)
    slab_phases(1)

    def forward(l):
        land(x1, l)
        inverse_full(x1.y, l, l)

        def chunk(base, here, carry):
            fields, at, blocks = gathered(l, base), spot(l, base), []
            for a, c in enumerate(cut):
                tr, ti = ref.tr[1, 0, here, c], ref.tr[1, 1, here, c]
                re, im = fields[a]
                re, im = re * tr - im * ti, re * ti + im * tr
                ref.passed1[0, at, c] = re
                ref.passed1[1, at, c] = im
                blocks.append((re, im))
            scattered(l, base, blocks)
            return carry

        each_chunk(chunk)
        emit_full(x2, l, l)

    each_led(forward)
    forward_on("slab", 2)
    forward_on("lit", 0)
    trade_foreign("lit", 1)
    columns(x2, x3, 1.0)
    trade_foreign("lit", *range(2, spec.sets))
    forward_on("lit", 1)
    slab_phases(2)
    b0, b1, b2, b3, sums = port("b0"), port("b1"), port("b2"), port("b3"), port("sums")
    ready("band")
    ready("band_inv")
    shape_pupil()

    def forward_band(l):
        land(x3, l)
        inverse_full(x3.y, l, l)

        def chunk(base, here, carry):
            fields, at, blocks = gathered(l, base), spot(l, base), []
            for a, c in enumerate(cut):
                tr, ti = ref.tr[2, 0, here, c], ref.tr[2, 1, here, c]
                re, im = fields[a]
                re, im = re * tr - im * ti, re * ti + im * tr
                ref.passed2[0, at, c] = re
                ref.passed2[1, at, c] = im
                blocks.append(tilt(l, here, a, (re, im), 1.0))
            scattered(l, base, blocks)
            return carry

        each_chunk(chunk)
        emit_band(b0, l)

    each_led(forward_band)
    forward_on("lit", *range(2, spec.sets))
    pupil_columns(b0, b1, 1.0)
    means = port("means")

    def announce(x, lines):
        lines = jnp.concatenate(lines + [jnp.zeros((x.stage.shape[2] - len(lines), lanes), f32)], 0)
        for d in range(devs):
            x.stage[0, d] = lines
        push(x, 0)

    def heard(x):
        land(x, 0)
        return jnp.sum(jnp.sum(x.y[0], 0), 1, keepdims=True)

    announce(means, [ref.energy[l] for l in range(count)])

    def camera(l):
        land(b1, l)
        inverse_band(b1, l)

    each_led(camera)
    for k in range(spec.sets):
        traded("lit", k)

    added = heard(means)
    pairs = [(l, m) for l in range(count) for m in range(l, count)]
    inverse_mean, number = [], []
    for k, leds in enumerate(lit_sets):
        members = sum(member_of[k])
        inverse = jnp.where(members > 0.0, area / sum(added[l : l + 1] for l in leds), 0.0)
        inverse_mean.append(inverse)
        number.append(members * inverse)

    def weigh(base, here, carry):
        fields = [gathered(l, base) for l in range(count)]
        adds, outgoing = [0.0] * spec.stat_rows, [[] for _ in range(count)]
        for a, c in enumerate(cut):
            power = [fields[l][a][0] * fields[l][a][0] + fields[l][a][1] * fields[l][a][1] for l in range(count)]
            values = [power[l] * power[m] for l, m in pairs]
            weight = [0.0] * count
            for k, leds in enumerate(lit_sets):
                seen = ref.lit[k, here, c]
                values += [seen * power[l] for l in leds]
                pull = (sum(power[l] for l in leds) * number[k] - seen) * inverse_mean[k]
                for l in leds:
                    weight[l] = weight[l] + pull
            for l in range(count):
                scale = 2.0 * weight[l]
                outgoing[l].append((scale * fields[l][a][0], scale * fields[l][a][1]))
            for k, value in enumerate(values):
                adds[k] = adds[k] + fold(value)
        for l in range(count):
            scattered(l, base, outgoing[l])
        return tuple(x + y for x, y in zip(carry, adds))

    stats = each_chunk(weigh, tuple(jnp.zeros((8, lanes), f32) for _ in range(spec.stat_rows)))
    announce(sums, [jnp.sum(line, 0, keepdims=True) for line in stats])
    each_led(lambda l: emit_band(b2, l))
    added = heard(sums)
    pulls = [0.0] * count
    cross_row = len(pairs)
    for k, leds in enumerate(lit_sets):
        square = 0.0
        for at, (l, m) in enumerate(pairs):
            if l in leds and m in leds:
                square = square + (1.0 if l == m else 2.0) * added[at : at + 1]
        cross = sum(added[cross_row + i : cross_row + i + 1] for i in range(len(leds)))
        cross_row += len(leds)
        couple = (number[k] * square * inverse_mean[k] - cross * inverse_mean[k]) / area
        for l in leds:
            pulls[l] = pulls[l] + couple * inverse_mean[k]
    for l in range(count):
        ref.pulled[l] = jnp.broadcast_to(2.0 * pulls[l], (1, lanes))
    pupil_columns(b2, b3, -1.0)
    y3, y2, y1, y0 = port("y3"), port("y2"), port("y1"), port("y0")
    ref.grad[...] = jnp.zeros(ref.grad.shape, f32)

    def back_band(l):
        land(b3, l)
        inverse_band(b3, l)

        def chunk(base, here, carry):
            fields, at, blocks = gathered(l, base), spot(l, base), []
            for a, c in enumerate(cut):
                re, im = tilt(l, here, a, fields[a], -1.0)
                pr, pi = ref.passed2[0, at, c], ref.passed2[1, at, c]
                ref.grad[1, here, c] += pr * im - pi * re
                tr, ti = ref.tr[2, 0, here, c], ref.tr[2, 1, here, c]
                blocks.append((re * tr + im * ti, im * tr - re * ti))
            scattered(l, base, blocks)
            return carry

        each_chunk(chunk)

        @pl.when(l == count - 1)
        def _():
            trade_native("grad", 1)
            trade_foreign("grad", 1)

        emit_full(y3, l, l)

    each_led(back_band)
    columns(y3, y2, -1.0)
    forward_on("grad", 1)

    def back(l):
        land(y2, l)
        inverse_full(y2.y, l, l)

        def chunk(base, here, carry):
            fields, at, blocks = gathered(l, base), spot(l, base), []
            for a, c in enumerate(cut):
                re, im = fields[a]
                pr, pi = ref.passed1[0, at, c], ref.passed1[1, at, c]
                ref.grad[0, here, c] += pr * im - pi * re
                tr, ti = ref.tr[1, 0, here, c], ref.tr[1, 1, here, c]
                blocks.append((re * tr + im * ti, im * tr - re * ti))
            scattered(l, base, blocks)
            return carry

        each_chunk(chunk)

        @pl.when(l == count - 1)
        def _():
            trade_native("grad", 0)
            trade_foreign("grad", 0)

        emit_full(y1, l, l)

    each_led(back)
    ready("slab_own")
    phases(ref.slab_own, ref.tr.at[0])
    ref.cs[...] = jnp.zeros(ref.cs.shape, f32)

    def last(l):
        land(y1, l)
        spread(y1, l)

        def add(j, z):
            ref.cs[j] += shaped(z, l, j, -1.0)

        col_dot(ref.chi, ref.clo, add, 1.0)

    last(0)
    forward_on("grad", 0)
    lax.fori_loop(1, count, lambda l, carry: last(l) or carry, 0)
    for j in range(4):
        stow(j, ref.cs[j])
    col_inverse(y0, 0, leave_one, (3, 2, 1, 0))
    land(y0, 0)
    inverse_full(y0.y, 0, 0)

    def leave(base, here, carry):
        fields = gathered(0, base)
        for a, c in enumerate(cut):
            tr, ti = ref.tr[0, 0, here, c], ref.tr[0, 1, here, c]
            re, im = fields[a]
            ref.grad0[here, c] = tr * im - ti * re
        return carry

    each_chunk(leave)
    final = local(ref.grad0, ref.result.at[0], ref.loads.at[len(spec.loaded)])
    final.start()

    for x, slots in (
        (x0, 1), (x1, count), (x2, count), (x3, count), (b0, count), (b1, count), (b2, count), (b3, count),
        (sums, 1), (means, 1), (counts, 1), (y3, count), (y2, count), (y1, count), (y0, 1),
    ):
        drain(x, slots)
    for q in range(per):

        @pl.when(place == owners[q])
        def _():
            for jj in range(2):
                for w in range(2):
                    pupil_copy(jj, w, q).wait_send()

    for name in part:
        trade_ends(name)
    for k in range(2):
        traded("grad", k)

    @pl.when(foreign)
    def _():
        block = y0.stage.at[0, 0]
        local(block, block, y0.sent.at[0]).wait()

    final.wait()


def body(tiles, slab_phase, pupil_phase, pupil_mask, led_code, led_freq, measured):
    devs = lax.axis_size("pat")
    slab_count, rows, size = slab_phase.shape
    patterns, count = led_code.shape
    quarter, cols, per = size // 4, size // devs, devs // 4
    band = 2 * pupil_radius
    band_cols = band // devs
    rt = row_tables(size, cols, band // 4)
    ct = col_tables(size)
    sets = 2**count - 1
    stat_rows = count * (count + 1) // 2 + count * 2 ** (count - 1)
    owners = [(q - pupil_radius // cols) % devs for q in range(per)]
    loads = dict(
        row_twiddle=rt.twiddle, full=rt.full,
        col_twiddle=jnp.asarray(ct.twiddle), both=jnp.asarray(ct.both), full_inv=rt.full_inv, band=rt.band,
        band_inv=rt.band_inv, measured=measured,
    )
    inputs = {name + "_hbm": value for name, value in loads.items()}
    inputs |= dict(phase_hbm=pupil_phase, mask_hbm=pupil_mask, slab_hbm=slab_phase, freq=led_freq, code=led_code.T)
    wide = 2 * quarter
    total = count * rows
    vmem, dma = pltpu.VMEM, pltpu.SemaphoreType.DMA
    scratch = {name: vmem(value.shape, value.dtype) for name, value in loads.items()}
    loads["slab_own"] = None
    scratch["slab_own"] = vmem((rows, size), f32)
    scratch |= dict(
        slab=vmem(slab_phase.shape, f32), lit=vmem((sets, rows, size), f32), lit_own=vmem((sets, rows, size), f32),
        phase=vmem((2, rows, pupil_radius), f32), mask=vmem((2, rows, pupil_radius), jnp.int32),
        phase_sem=dma((2,)), mask_sem=dma((2,)), own=vmem((4, 2, rows // 4, band), f32), pupil=vmem((2, band_cols, band), f32), shape=vmem((2, 4 * band_cols, lanes), f32),
        tilt_c=vmem((2 * count, 1, size), f32), tilt_r=vmem((2 * count, rows, lanes), f32),
        prop=vmem((2, count, 4, quarter, lanes), f32), tr=vmem((3, 2, rows, size), f32),
        passed1=vmem((2, total, size), f32), passed2=vmem((2, total, size), f32),
        spectrum=vmem((count, 4 * band_cols, lanes), f32), energy=vmem((count, 1, lanes), f32),
        pulled=vmem((count, 1, lanes), f32), grad=vmem((2, rows, size), f32), grad0=vmem((rows, size), f32),
        hi=vmem((4, total, wide), bf16), lo=vmem((4, total, wide), bf16), zs=vmem((4, total, wide), f32),
        ghi=vmem((4 * rows, wide), bf16), glo=vmem((4 * rows, wide), bf16),
        chi=vmem((quarter, 4 * lanes), bf16), clo=vmem((quarter, 4 * lanes), bf16),
        dhi=vmem((quarter, 4 * lanes), bf16), dlo=vmem((quarter, 4 * lanes), bf16),
        cz=vmem((4, quarter, lanes), f32), cs=vmem((4, quarter, lanes), f32),
        loads=dma((len(loads) + 1,)),
        pupil_sent=dma((4,)), pupil_got=dma, piece_got=dma((2,)),
    )
    for name, blocks in (("slab", 3), ("lit", sets), ("grad", 2)):
        scratch[name + "_relay"] = vmem((blocks, rows // 2, size), f32)
        for kind in ("_sent", "_got", "_late", "_via"):
            scratch[name + kind] = dma((blocks,))
    block, narrow = (devs, rows, lanes), (devs, band_cols, lanes)
    ports = dict(x0=(1, block), x1=(count, block), x2=(count, block), x3=(count, block))
    ports |= dict(b0=(count, narrow), b1=(count, narrow), b2=(count, narrow), b3=(count, narrow))
    ports |= dict(sums=(1, (devs, -(-stat_rows // 8) * 8, lanes)))
    ports |= dict(means=(1, (devs, -(-count // 8) * 8, lanes)))
    ports |= dict(counts=(1, (devs, -(-patterns // 8) * 8, lanes)))
    ports |= dict(y3=(count, block), y2=(count, block), y1=(count, block), y0=(1, block))
    for name, (slots, shape) in ports.items():
        scratch[name + "_stage"] = vmem((slots,) + shape, f32)
        scratch[name + "_y"] = vmem((slots,) + shape, f32)
        scratch[name + "_sent"] = dma((slots,))
        scratch[name + "_got"] = dma((slots,))
    spec = Names(
        count=count, rows=rows, quarter=quarter, devs=devs, tiles=tiles, patterns=patterns,
        area=float(size * size), stat_rows=stat_rows, sets=sets, owners=owners, loaded=list(loads),
        names=list(inputs) + ["result"] + list(scratch),
    )
    anywhere = pl.BlockSpec(memory_space=pl.ANY)
    smem = pl.BlockSpec(memory_space=pltpu.SMEM)
    return pl.pallas_call(
        functools.partial(whole_kernel, spec),
        out_shape=jax.ShapeDtypeStruct(slab_phase.shape, f32),
        in_specs=[smem if name in ("freq", "code") else anywhere for name in inputs],
        out_specs=anywhere,
        scratch_shapes=list(scratch.values()),
        compiler_params=pltpu.CompilerParams(
            collective_id=1, has_side_effects=True, vmem_limit_bytes=67043328
        ),
        name="whole",
    )(*inputs.values())


def solution(mesh):
    in_specs = (
        P("tiles", "pat", None),
        P("pat", None),
        P("pat", None),
        P(),
        P(),
        P("tiles", "pat", None),
    )
    out_specs = P("tiles", "pat", None)

    def run(slab_phase, *others):
        devs, tiles = mesh.shape["pat"], mesh.shape["tiles"]
        size, count = slab_phase.shape[-1], others[2].shape[1]
        fits = 2 * size == lanes * devs and count * size == lanes * devs and slab_phase.shape[0] == 3 * tiles
        fits = fits and tiles == 2 and devs == len(far_first)
        inner = functools.partial(body, tiles) if fits else plain_body
        return jax.shard_map(inner, mesh=mesh, in_specs=in_specs, out_specs=out_specs, check_vma=False)(
            slab_phase, *others
        )

    return run
```

```python
import functools
import math
import types

import jax
import jax.numpy as jnp
import numpy as np
from jax import lax
from jax.experimental import pallas as pl
from jax.experimental.pallas import tpu as pltpu
from jax.sharding import PartitionSpec as P

spread_rate = 0.3
highest = lax.Precision.HIGHEST


def frequency(grid_index, grid_size):
    return (grid_index + grid_size // 2) % grid_size - grid_size // 2


def complex_times(values, factor):
    real_part = values[0] * factor[0] - values[1] * factor[1]
    imag_part = values[0] * factor[1] + values[1] * factor[0]
    return jnp.stack([real_part, imag_part])


def dft_block(length, direction, norm_factor):
    grid_index = jnp.arange(length, dtype=jnp.int32)
    angles = (grid_index[:, None] * grid_index[None, :] % length).astype(jnp.float32) * (
        2.0 * math.pi / length
    )
    cosine = jnp.cos(angles) * norm_factor
    signed_sine = direction * jnp.sin(angles) * norm_factor
    real_rows = jnp.stack([cosine, signed_sine], 1)
    imag_rows = jnp.stack([-signed_sine, cosine], 1)
    return jnp.stack([real_rows, imag_rows], 0)


def twiddle_table(short_size, long_size, grid_size, direction):
    short_index = jnp.arange(short_size, dtype=jnp.int32)
    long_index = jnp.arange(long_size, dtype=jnp.int32)
    angles = (short_index[:, None] * long_index[None, :] % grid_size).astype(jnp.float32) * (
        2.0 * math.pi / grid_size
    )
    return jnp.stack([jnp.cos(angles), direction * jnp.sin(angles)])


def table_set(col_count, dev_count, grid_size, direction):
    short_table = dft_block(col_count, direction, 1.0)
    long_table = dft_block(dev_count, direction, 1.0 / math.sqrt(grid_size))
    return (short_table, long_table, twiddle_table(col_count, dev_count, grid_size, direction))


def to_fourier(wave_field, tables, dev_count):
    short_table, long_table, twiddles = tables
    led_count = wave_field.shape[1]
    row_count = wave_field.shape[2]
    grid_size = wave_field.shape[3]
    col_count = grid_size // dev_count
    shaped = wave_field.reshape(2, led_count, row_count, col_count, dev_count)
    sectioned = jnp.einsum("zlrmq,zmwc->wlrcq", shaped, short_table, precision=highest)
    sectioned = complex_times(sectioned, twiddles)
    outgoing = jnp.einsum("wlrcq,wqvd->dvlcr", sectioned, long_table, precision=highest)
    incoming = lax.all_to_all(
        outgoing.reshape(dev_count, -1), "pat", split_axis=0, concat_axis=0, tiled=True
    )
    incoming = incoming.reshape(dev_count, 2, led_count, col_count, row_count)
    sectioned = jnp.einsum("swlcr,wsvj->vlcrj", incoming, long_table, precision=highest)
    sectioned = complex_times(sectioned, twiddles)
    sectioned = jnp.einsum("wlcrj,wrvh->vlchj", sectioned, short_table, precision=highest)
    return sectioned.reshape(2, led_count, col_count, grid_size)


def to_space(spectrum, tables, dev_count):
    short_table, long_table, twiddles = tables
    led_count = spectrum.shape[1]
    col_count = spectrum.shape[2]
    grid_size = spectrum.shape[3]
    row_count = grid_size // dev_count
    shaped = spectrum.reshape(2, led_count, col_count, row_count, dev_count)
    sectioned = jnp.einsum("zlcmq,zmwr->wlcrq", shaped, short_table, precision=highest)
    sectioned = complex_times(sectioned, twiddles)
    outgoing = jnp.einsum("wlcrq,wqvd->dvlcr", sectioned, long_table, precision=highest)
    incoming = lax.all_to_all(
        outgoing.reshape(dev_count, -1), "pat", split_axis=0, concat_axis=0, tiled=True
    )
    incoming = incoming.reshape(dev_count, 2, led_count, col_count, row_count)
    sectioned = jnp.einsum("swlcr,wsvj->vlrcj", incoming, long_table, precision=highest)
    sectioned = complex_times(sectioned, twiddles)
    sectioned = jnp.einsum("wlrcj,wcvh->vlrhj", sectioned, short_table, precision=highest)
    return sectioned.reshape(2, led_count, row_count, grid_size)


def plain_body(slab_phase, pupil_phase, pupil_mask, led_code, led_freq, measured):
    dev_count = lax.axis_size("pat")
    position = lax.axis_index("pat")
    slab_count, row_count, grid_size = slab_phase.shape
    col_count = grid_size // dev_count
    pattern_count, led_count = led_code.shape
    area = float(grid_size * grid_size)
    forward_set = table_set(col_count, dev_count, grid_size, -1.0)
    inverse_set = table_set(col_count, dev_count, grid_size, 1.0)
    conjugate = jnp.array([1.0, -1.0], jnp.float32)[:, None, None]
    col_freq = frequency(position * col_count + jnp.arange(col_count, dtype=jnp.int32), grid_size)
    row_freq = frequency(jnp.arange(grid_size, dtype=jnp.int32), grid_size)
    radius = col_freq[:, None] * col_freq[:, None] + row_freq[None, :] * row_freq[None, :]
    cutoff = grid_size // 2 * (grid_size // 2)
    inside = radius <= cutoff
    height = jnp.sqrt(jnp.maximum(cutoff - radius, 0).astype(jnp.float32))
    phase_shift = spread_rate * (height - grid_size // 2)
    propagator = jnp.stack(
        [jnp.where(inside, jnp.cos(phase_shift), 0.0), jnp.where(inside, jnp.sin(phase_shift), 0.0)]
    )
    opening = pupil_mask.astype(jnp.float32)
    pupil = jnp.stack([opening * jnp.cos(pupil_phase), opening * jnp.sin(pupil_phase)])
    propagator_conj = propagator * conjugate
    pupil_conj = pupil * conjugate
    row_index = position * row_count + jnp.arange(row_count, dtype=jnp.int32)
    col_index = jnp.arange(grid_size, dtype=jnp.int32)
    tilt_index = (
        led_freq[:, 0][:, None, None] * row_index[None, :, None]
        + led_freq[:, 1][:, None, None] * col_index[None, None, :]
    ) % grid_size
    tilt_angle = tilt_index.astype(jnp.float32) * (2.0 * math.pi / grid_size)
    illumination = jnp.stack([jnp.cos(tilt_angle), jnp.sin(tilt_angle)])
    transmission = jnp.stack([jnp.cos(slab_phase), jnp.sin(slab_phase)])
    group_count = 1
    group_size = led_count // group_count
    wave_groups = [illumination]
    passed_groups = []
    for slab_index in range(slab_count):
        factor = transmission[:, slab_index]
        passed = [complex_times(wave_field, factor) for wave_field in wave_groups]
        passed_groups.append(passed)
        spectral_factor = propagator if slab_index < slab_count - 1 else pupil
        wave_groups = [
            to_space(
                complex_times(to_fourier(passed_field, forward_set, dev_count), spectral_factor),
                inverse_set,
                dev_count,
            )
            for passed_field in passed
        ]
    camera = wave_groups[0]
    led_power = camera[0] * camera[0] + camera[1] * camera[1]
    code_float = led_code.astype(jnp.float32)
    pattern_power = jnp.dot(
        code_float, led_power.reshape(led_count, -1), precision=highest
    ).reshape(pattern_count, row_count, grid_size)
    counts = measured.astype(jnp.float32)
    power_sum, count_sum = lax.psum(
        (jnp.sum(pattern_power, axis=(1, 2)), jnp.sum(counts, axis=(1, 2))), "pat"
    )
    mean_power = power_sum / area
    mean_count = count_sum / area
    relative = pattern_power / mean_power[:, None, None]
    misfit = relative - counts / mean_count[:, None, None]
    coupling = lax.psum(jnp.sum(misfit * relative, axis=(1, 2)), "pat") / area
    pattern_weight = (misfit - coupling[:, None, None]) / mean_power[:, None, None]
    led_weight = jnp.dot(
        code_float.T, pattern_weight.reshape(pattern_count, -1), precision=highest
    ).reshape(led_count, row_count, grid_size)
    camera_adjoint = 2.0 * led_weight[None] * camera
    adjoint_groups = [camera_adjoint]
    gradients = [None] * slab_count
    for slab_index in range(slab_count - 1, -1, -1):
        spectral_factor = pupil_conj if slab_index == slab_count - 1 else propagator_conj
        back_groups = [
            to_space(
                complex_times(to_fourier(adjoint_field, forward_set, dev_count), spectral_factor),
                inverse_set,
                dev_count,
            )
            for adjoint_field in adjoint_groups
        ]
        gradient = jnp.zeros((row_count, grid_size), jnp.float32)
        for passed_field, back_field in zip(passed_groups[slab_index], back_groups):
            gradient = jnp.sum(
                passed_field[0] * back_field[1] - passed_field[1] * back_field[0], axis=0
            )
        gradients[slab_index] = gradient
        if slab_index > 0:
            release = transmission[:, slab_index] * conjugate
            adjoint_groups = [complex_times(back_field, release) for back_field in back_groups]
    return jnp.stack(gradients)


class Names(types.SimpleNamespace):
    def __getitem__(self, name):
        return getattr(self, name)


pupil_radius = 128
lanes = 128
f32 = jnp.float32
bf16 = jnp.bfloat16


def halves(table):
    table32 = np.asarray(table, np.float32)
    high = table32.astype(bf16)
    low = (table32 - high.astype(np.float32)).astype(bf16)
    return np.stack([high, low])


def row_tables(size, block, band_block):
    quarter = size // 4
    pos = np.arange(quarter)
    angle = 2.0 * np.pi * ((pos[:, None] * pos[None, :]) % quarter) / quarter
    cosine = np.cos(angle) / math.sqrt(size)
    sine = np.sin(angle) / math.sqrt(size)

    def forward(freqs, width):
        parts = []
        for first in range(0, len(freqs), width):
            pick = freqs[first : first + width] % quarter
            left = np.concatenate([cosine[:, pick], sine[:, pick]], 0)
            right = np.concatenate([-sine[:, pick], cosine[:, pick]], 0)
            parts.append(np.concatenate([left, right], 1))
        return np.concatenate(parts, 1)

    full = forward(pos, block)
    reach = pupil_radius // 4
    band = forward(np.arange(-reach, reach), band_block)
    theta = 2.0 * np.pi * (np.arange(4)[:, None] * pos[None, :]) / size
    twiddle = np.concatenate([np.cos(theta), np.sin(theta)], 0).astype(np.float32)
    return Names(
        full=jnp.asarray(halves(full)),
        full_inv=jnp.asarray(halves(full.T)),
        band=jnp.asarray(halves(band)),
        band_inv=jnp.asarray(halves(band.T)),
        twiddle=jnp.asarray(twiddle),
    )


def col_tables(size):
    quarter = size // 4
    pos = np.arange(quarter)
    angle = 2.0 * np.pi * ((pos[:, None] * pos[None, :]) % quarter) / quarter
    both = np.concatenate([np.cos(angle), np.sin(angle)], 0) / math.sqrt(size)
    theta = 2.0 * np.pi * (np.arange(1, 4)[:, None] * pos[None, :]) / size
    twiddle = np.stack([np.cos(theta), np.sin(theta)]).astype(np.float32)
    twiddle = np.ascontiguousarray(np.broadcast_to(twiddle[..., None], twiddle.shape + (lanes,)))
    return Names(both=halves(both), twiddle=twiddle)


def split(value):
    high = value.astype(bf16)
    return high, (value - high.astype(f32)).astype(bf16)


def dot3(left, right):
    def dot(a, b):
        return jnp.dot(a, b, preferred_element_type=f32)

    return dot(left[0], right[0]) + (dot(left[0], right[1]) + dot(left[1], right[0]))


def turn(value):
    rolled = pltpu.roll(value, lanes // 2, 1)
    lane = lax.broadcasted_iota(jnp.int32, value.shape, 1)
    return jnp.where(lane < lanes // 2, rolled, -rolled)


def row_spread(blocks, twiddle_ref):
    (r0, i0), (r1, i1), (r2, i2), (r3, i3) = blocks
    sr, si, tr, ti = r0 + r2, i0 + i2, r1 + r3, i1 + i3
    dr, di, er, ei = r0 - r2, i0 - i2, r1 - r3, i1 - i3
    mixed = [(sr + tr, si + ti), (dr + ei, di - er), (sr - tr, si - ti), (dr - ei, di + er)]
    out = [mixed[0]]
    for j in range(1, 4):
        cosine, sine = twiddle_ref[j : j + 1, :], twiddle_ref[4 + j : 5 + j, :]
        re, im = mixed[j]
        out.append((re * cosine + im * sine, im * cosine - re * sine))
    return out


def row_gather(parts, twiddle_ref):
    g = [parts[0]]
    for j in range(1, 4):
        cosine, sine = twiddle_ref[j : j + 1, :], twiddle_ref[4 + j : 5 + j, :]
        re, im = parts[j]
        g.append((re * cosine - im * sine, im * cosine + re * sine))
    (r0, i0), (r1, i1), (r2, i2), (r3, i3) = g
    sr, si, tr, ti = r0 + r2, i0 + i2, r1 + r3, i1 + i3
    dr, di, er, ei = r0 - r2, i0 - i2, r1 - r3, i1 - i3
    return [(sr + tr, si + ti), (dr - ei, di + er), (sr - tr, si - ti), (dr + ei, di - er)]


mesh_ids = pl.DeviceIdType.MESH
far_first = (14, 15, 6, 7, 10, 11, 12, 13, 2, 3, 4, 5, 8, 9, 1, 0)


def flip(index, mask):
    out = index
    for bit in (1, 2, 4, 8):
        if mask & bit:
            out = out + bit - 2 * bit * lax.rem(index // bit, 2)
    return out


def whole_kernel(spec, *refs):
    ref = Names(**dict(zip(spec.names, refs)))
    count, rows, quarter, devs, patterns = spec.count, spec.rows, spec.quarter, spec.devs, spec.patterns
    size, per, half, step = 4 * quarter, devs // 4, devs // 2, 16
    tile, place = lax.axis_index("tiles"), lax.axis_index("pat")
    work = place // half
    me = half * tile + lax.rem(place, half)
    native = tile == work
    foreign = jnp.logical_not(native)
    other = dict(tiles=1 - tile, pat=lax.rem(place + half, devs))

    def member(index):
        return dict(tiles=index // half, pat=work * half + lax.rem(index, half))

    barrier = pltpu.get_barrier_semaphore()
    everyone = spec.tiles * devs

    def signal(hop, carry):
        target = lax.rem(tile * devs + place + hop, everyone)
        pl.semaphore_signal(
            barrier, inc=1, device_id=dict(tiles=target // devs, pat=lax.rem(target, devs)),
            device_id_type=mesh_ids,
        )
        return carry

    lax.fori_loop(1, everyone, signal, 0)

    def local(source, target, sem):
        return pltpu.make_async_copy(source, target, sem)

    def away(source, target, sent, got, device):
        return pltpu.make_async_remote_copy(
            src_ref=source, dst_ref=target, send_sem=sent, recv_sem=got, device_id=device,
            device_id_type=mesh_ids,
        )

    def fetch(name):
        source = ref.slab_hbm.at[0] if name == "slab_own" else ref[name + "_hbm"]
        return local(source, ref[name], ref.loads.at[spec.loaded.index(name)])

    reach = pupil_radius
    spans = (slice(size - reach, size), slice(0, reach))

    def near(name, k):
        return local(ref[name + "_hbm"].at[:, spans[k]], ref[name].at[k], ref[name + "_sem"].at[k])

    for name in ("phase", "mask"):
        for k in range(2):
            near(name, k).start()
    for name in spec.loaded:
        fetch(name).start()

    def ready(name):
        fetch(name).wait()

    share = rows // 2
    neighbour = dict(tiles=1 - tile, pat=place)
    across = dict(tiles=tile, pat=lax.rem(place + half, devs))

    sources = dict(slab=ref.slab_hbm, lit=ref.lit_own, grad=ref.grad)
    targets = dict(slab=ref.slab, lit=ref.lit, grad=ref.result.at[1:3])
    part = dict(slab=3, lit=spec.sets, grad=2)

    def semaphore(name, kind, k):
        return ref[name + kind].at[k]

    def direct(name, k):
        return away(
            sources[name].at[k, :share], targets[name].at[k, :share], semaphore(name, "_sent", k),
            semaphore(name, "_got", k), other,
        )

    def hop(name, k):
        return away(
            sources[name].at[k, share:], ref[name + "_relay"].at[k], semaphore(name, "_sent", k),
            semaphore(name, "_via", k), neighbour,
        )

    def onward(name, k):
        return away(
            ref[name + "_relay"].at[k], targets[name].at[k, share:], semaphore(name, "_sent", k),
            semaphore(name, "_late" if name == "slab" else "_got", k), across,
        )

    def trade_native(name, k):
        @pl.when(native)
        def _():
            if name == "slab":
                for span, kind in ((pl.ds(0, share), "_got"), (pl.ds(share, share), "_late")):
                    local(sources[name].at[k, span], targets[name].at[k, span], semaphore(name, kind, k)).start()
            else:
                local(sources[name].at[k], targets[name].at[k], semaphore(name, "_got", k)).start()

    def trade_foreign(name, *blocks):
        @pl.when(foreign)
        def _():
            for k in blocks:
                direct(name, k).start()
                hop(name, k).start()

    def forward_on(name, *blocks):
        @pl.when(native)
        def _():
            for k in blocks:
                hop(name, k).wait_recv()
                onward(name, k).start()

    def traded(name, k):
        whole = targets[name].at[k]
        if name == "slab":
            halves = (whole.at[:share], whole.at[share:])
            local(halves[0], halves[0], semaphore(name, "_got", k)).wait()
            local(halves[1], halves[1], semaphore(name, "_late", k)).wait()
        else:
            local(whole, whole, semaphore(name, "_got", k)).wait()

    def trade_ends(name):
        for k in range(part[name]):

            @pl.when(native)
            def _():
                onward(name, k).wait_send()

            @pl.when(foreign)
            def _():
                whole = sources[name].at[k]
                local(whole, whole, semaphore(name, "_sent", k)).wait()

    def port(name):
        return Names(
            stage=ref[name + "_stage"], y=ref[name + "_y"], sent=ref[name + "_sent"], got=ref[name + "_got"]
        )

    def push_one(x, slot, mask, span=None):
        dest = flip(me, mask)
        source = x.stage.at[slot, dest] if span is None else x.stage.at[slot, dest, span]
        target = x.y.at[slot, me] if span is None else x.y.at[slot, me, span]
        if mask:
            away(source, target, x.sent.at[slot], x.got.at[slot], member(dest)).start()
        else:
            local(source, target, x.got.at[slot]).start()

    def push(x, slot):
        for mask in far_first:
            push_one(x, slot, mask)

    def leave_one(x, slot, mask):
        dest = flip(place, mask)

        def start_away():
            away(
                x.stage.at[slot, dest], x.y.at[slot, me], x.sent.at[slot], x.got.at[slot],
                dict(tiles=work, pat=dest),
            ).start()

        if mask:
            start_away()
        else:

            @pl.when(native)
            def _():
                local(x.stage.at[slot, dest], x.y.at[slot, me], x.got.at[slot]).start()

            pl.when(foreign)(start_away)

    def land(x, slot):
        local(x.y.at[slot], x.y.at[slot], x.got.at[slot]).wait()

    def drain(x, slots):
        for slot in range(slots):
            part = x.stage.at[slot, pl.ds(0, devs - 1)]
            local(part, part, x.sent.at[slot]).wait()

    hi, lo, zs = ref.hi, ref.lo, ref.zs
    cut = [slice(a * quarter, (a + 1) * quarter) for a in range(4)]

    def spot(l, base):
        return pl.ds(pl.multiple_of(l * rows + base, step), step)

    def each_chunk(chunk, carry=0):
        def at_chunk(i, carry):
            base = pl.multiple_of(i * step, step)
            return chunk(base, pl.ds(base, step), carry)

        return lax.fori_loop(0, rows // step, at_chunk, carry)

    def gathered(l, base):
        at = spot(l, base)
        parts = [(zs[j, at, :quarter], zs[j, at, quarter:]) for j in range(4)]
        return row_gather(parts, ref.row_twiddle)

    def scattered(l, base, blocks):
        at = spot(l, base)
        for j, (re, im) in enumerate(row_spread(blocks, ref.row_twiddle)):
            high, low = split(re)
            hi[j, at, :quarter] = high
            lo[j, at, :quarter] = low
            high, low = split(im)
            hi[j, at, quarter:] = high
            lo[j, at, quarter:] = low

    def led_rows(l):
        return pl.ds(pl.multiple_of(l * rows, rows), rows)

    def inverse_full(y, slot, l):
        for j in range(4):
            for q in range(per):
                high, low = split(y[slot, per * j + q])
                ref.ghi[j * rows : (j + 1) * rows, q * lanes : (q + 1) * lanes] = high
                ref.glo[j * rows : (j + 1) * rows, q * lanes : (q + 1) * lanes] = low
        value = dot3((ref.ghi[...], ref.glo[...]), (ref.full_inv[0], ref.full_inv[1]))
        zs[:, led_rows(l), :] = value.reshape(4, rows, 2 * quarter)

    def emit_full(x, slot, l):
        home = me // per
        for far in (3, 1, 2, 0):
            j = flip(home, far)
            value = dot3((hi[j, led_rows(l), :], lo[j, led_rows(l), :]), (ref.full[0], ref.full[1]))
            for q in range(per):
                x.stage[slot, per * j + q] = value[:, q * lanes : (q + 1) * lanes]
            for bits in (3, 2, 1, 0):
                push_one(x, slot, per * far + bits)

    def braid(first, second):
        middle = lanes // 2
        lane = lax.broadcasted_iota(jnp.int32, first.shape, 1)
        return (
            jnp.where(lane < middle, first, pltpu.roll(second, middle, 1)),
            jnp.where(lane < middle, pltpu.roll(first, middle, 1), second),
        )

    def inverse_band(x, l):
        for pair in range(2):
            turned = x.y[l, 2 * per * pair : 2 * per * (pair + 1)].reshape(lanes, lanes).T
            for k, block in enumerate(braid(turned[:rows], turned[rows:])):
                at = slice((2 * pair + k) * rows, (2 * pair + k + 1) * rows)
                high, low = split(block)
                ref.ghi[at, :lanes] = high
                ref.glo[at, :lanes] = low
        value = dot3((ref.ghi[:, :lanes], ref.glo[:, :lanes]), (ref.band_inv[0], ref.band_inv[1]))
        zs[:, led_rows(l), :] = value.reshape(4, rows, 2 * quarter)

    def emit_band(x, l):
        left = [part[:, led_rows(l), :].reshape(4 * rows, 2 * quarter) for part in (hi, lo)]
        flipped = dot3(left, (ref.band[0], ref.band[1])).T
        deep = x.y.shape[2]
        for pair in range(2):
            at = slice(pair * lanes, (pair + 1) * lanes)
            for k, block in enumerate(braid(flipped[:rows, at], flipped[rows:, at])):
                for q in range(per):
                    x.stage[l, per * (2 * pair + k) + q] = block[q * deep : (q + 1) * deep]
        push(x, l)

    def tilt(l, here, a, value, sign):
        rc, rs = ref.tilt_r[2 * l, here, :], ref.tilt_r[2 * l + 1, here, :]
        cc, cs = ref.tilt_c[2 * l, :, cut[a]], ref.tilt_c[2 * l + 1, :, cut[a]]
        rc = jnp.concatenate([rc] * (quarter // lanes), 1)
        rs = jnp.concatenate([rs] * (quarter // lanes), 1)
        er = rc * cc - rs * cs
        ei = sign * (rc * cs + rs * cc)
        re, im = value
        return re * er - im * ei, re * ei + im * er

    def spread(x, slot):
        def at_part(i, carry):
            here = pl.ds(pl.multiple_of(i * rows, rows), rows)
            x0, x1, x2, x3 = [x.y[slot, per * a + i] for a in range(4)]
            s, t, d, e = x0 + x2, x1 + x3, x0 - x2, turn(x1 - x3)
            for j, value in enumerate((s + t, d + e, s - t, d - e)):
                if j:
                    value = value * ref.col_twiddle[0, j - 1, here, :] + turn(value) * ref.col_twiddle[1, j - 1, here, :]
                high, low = split(value)
                ref.chi[here, j * lanes : (j + 1) * lanes] = high
                ref.clo[here, j * lanes : (j + 1) * lanes] = low
            return carry

        lax.fori_loop(0, per, at_part, 0)

    def col_dot(high, low, take, sign):
        for pair in range(2):
            at = slice(2 * pair * lanes, 2 * (pair + 1) * lanes)
            y = dot3((ref.both[0], ref.both[1]), (high[:, at], low[:, at]))
            for k in range(2):
                at = slice(k * lanes, (k + 1) * lanes)
                take(2 * pair + k, y[:quarter, at] + sign * turn(y[quarter:, at]))

    def shaped(z, l, j, sign):
        return z * ref.prop[0, l, j] - sign * (turn(z) * ref.prop[1, l, j])

    def stow(j, value):
        high, low = split(value)
        ref.dhi[:, j * lanes : (j + 1) * lanes] = high
        ref.dlo[:, j * lanes : (j + 1) * lanes] = low

    def col_inverse(x, slot, send=push_one, far_parts=(3, 1, 2, 0)):
        def take(j, value):
            if j:
                value = value * ref.col_twiddle[0, j - 1] - turn(value) * ref.col_twiddle[1, j - 1]
            ref.cz[j] = value

        col_dot(ref.dhi, ref.dlo, take, -1.0)
        home = lax.rem(me, per)
        for bits in (3, 2, 1, 0):
            i = flip(home, bits)
            here = pl.ds(pl.multiple_of(i * rows, rows), rows)
            g0, g1, g2, g3 = [ref.cz[j, here, :] for j in range(4)]
            s, t, d, e = g0 + g2, g1 + g3, g0 - g2, turn(g1 - g3)
            for a, value in enumerate((s + t, d - e, s - t, d + e)):
                x.stage[slot, per * a + i] = value
            for far in far_parts:
                send(x, slot, per * far + bits)

    def each_led(stage):
        def at_led(l, carry):
            stage(l)
            return carry

        lax.fori_loop(0, count, at_led, 0)

    def columns(x, out, sign):
        def stage(l):
            land(x, l)
            spread(x, l)
            col_dot(ref.chi, ref.clo, lambda j, z: stow(j, shaped(z, l, j, sign)), 1.0)
            col_inverse(out, l)

        each_led(stage)

    def pupil_columns(x, out, sign):
        deep = x.y.shape[2]

        def stage(l):
            land(x, l)
            blocks = []
            for a in range(4):
                pairs = [braid(x.y[l, s], x.y[l, s + 1]) for s in range(per * a, per * (a + 1), 2)]
                blocks.append(tuple(jnp.concatenate([pair[k] for pair in pairs], 1) for k in range(2)))
            mixed = [jnp.concatenate(part, 1) for part in row_spread(blocks, ref.row_twiddle)]
            z = dot3(split(jnp.concatenate(mixed, 0)), (ref.band[0], ref.band[1]))
            if sign < 0.0:
                z = z - ref.pulled[l] * ref.spectrum[l]
            z = z * ref.shape[0] + sign * (pltpu.roll(z, lanes // 2, 1) * ref.shape[1])
            if sign > 0.0:
                ref.spectrum[l] = z
                ref.energy[l] = jnp.sum(z * z, 0, keepdims=True)
            y = dot3(split(z), (ref.band_inv[0], ref.band_inv[1]))
            parts = [(y[j * deep : (j + 1) * deep, :quarter], y[j * deep : (j + 1) * deep, quarter:]) for j in range(4)]
            for a, (re, im) in enumerate(row_gather(parts, ref.row_twiddle)):
                for k in range(quarter // lanes):
                    at = slice(k * lanes, (k + 1) * lanes)
                    first, second = braid(re[:, at], im[:, at])
                    out.stage[l, per * a + 2 * k] = first
                    out.stage[l, per * a + 2 * k + 1] = second
            push(out, l)

        each_led(stage)

    def shape_pupil():
        local(ref.pupil, ref.pupil, ref.pupil_got).wait()
        band, deep = ref.pupil.shape[2], ref.pupil.shape[1]
        freq = lax.broadcasted_iota(jnp.int32, (band, 4 * lanes), 0)
        slot = lax.broadcasted_iota(jnp.int32, (band, 4 * lanes), 1)
        wanted = 4 * lax.rem(slot, lanes // 2) + slot // lanes
        pick = jnp.where(freq == wanted, 1.0, 0.0).astype(bf16)
        value, out = ref.pupil[...].reshape(2 * deep, band), 0.0
        for k in range(3):
            high = value.astype(bf16)
            out = out + jnp.dot(high, pick, preferred_element_type=f32)
            value = value - high.astype(f32)
        lane = lax.broadcasted_iota(jnp.int32, (deep, lanes), 1)
        for j in range(4):
            at = slice(j * lanes, (j + 1) * lanes)
            ref.shape[0, j * deep : (j + 1) * deep] = out[:deep, at]
            ref.shape[1, j * deep : (j + 1) * deep] = jnp.where(lane < lanes // 2, -out[deep:, at], out[deep:, at])

    def phases(source, target):
        def chunk(base, here, carry):
            phase = source[here, :]
            target[0, here, :] = jnp.cos(phase)
            target[1, here, :] = jnp.sin(phase)
            return carry

        each_chunk(chunk)

    def fold(value):
        total_rows = value[:8]
        for k in range(1, value.shape[0] // 8):
            total_rows = total_rows + value[8 * k : 8 * k + 8]
        out = total_rows[:, :lanes]
        for k in range(1, value.shape[1] // lanes):
            out = out + total_rows[:, lanes * k : lanes * (k + 1)]
        return out

    def fold_all(p):
        def chunk(base, here, carry):
            return carry + fold(ref.measured[p, here, :].astype(f32))

        return jnp.sum(each_chunk(chunk, jnp.zeros((8, lanes), f32)), 0, keepdims=True)

    def slab_phases(s):
        traded("slab", s)
        phases(ref.slab.at[s], ref.tr.at[s])

    for k in range(3):
        trade_native("slab", k)
    turn_size = 2.0 * math.pi / size
    col = lax.broadcasted_iota(jnp.int32, (8, size), 1)
    row = me * rows + lax.broadcasted_iota(jnp.int32, (rows, lanes), 0)
    for l in range(count):
        for index, freq, tilts in ((col, ref.freq[l, 1], ref.tilt_c), (row, ref.freq[l, 0], ref.tilt_r)):
            angle = jnp.bitwise_and(index * freq, size - 1).astype(f32) * turn_size
            deep = tilts.shape[1]
            tilts[2 * l] = jnp.cos(angle)[:deep]
            tilts[2 * l + 1] = jnp.sin(angle)[:deep]

    pl.semaphore_wait(barrier, everyone - 1)
    pieces = (pl.ds(0, share // 2), pl.ds(share // 2, share // 2))

    def piece(source, target, sent, k, device):
        return away(source, target, sent, ref.piece_got.at[k], device)

    def first_hop(k):
        at = pieces[k]
        return piece(
            sources["slab"].at[0, share:].at[at], ref.slab_relay.at[0, at], semaphore("slab", "_sent", 0), k, neighbour
        )

    def first_onward(k):
        at = pieces[k]
        return away(
            ref.slab_relay.at[0, at], targets["slab"].at[0, share:].at[at], semaphore("slab", "_sent", 0),
            semaphore("slab", "_late", 0), across,
        )

    @pl.when(foreign)
    def _():
        direct("slab", 0).start()
        for k in range(2):
            first_hop(k).start()

    ready("row_twiddle")
    ready("full")
    x0, x1, x2, x3 = port("x0"), port("x1"), port("x2"), port("x3")

    def enter(first, count_rows):
        def chunk(i, carry):
            base = pl.multiple_of(first + i * step, step)
            here = pl.ds(base, step)
            blocks = []
            for c in cut:
                phase = ref.slab[0, here, c]
                blocks.append((jnp.cos(phase), jnp.sin(phase)))
            scattered(0, base, blocks)
            return carry

        lax.fori_loop(0, count_rows // step, chunk, 0)
        span = pl.ds(first, count_rows)
        left = [part[:, span, :].reshape(4 * count_rows, 2 * quarter) for part in (hi, lo)]
        value = dot3(left, (ref.full[0], ref.full[1]))
        for j in range(4):
            for q in range(per):
                x0.stage[0, per * j + q, span] = value[
                    j * count_rows : (j + 1) * count_rows, q * lanes : (q + 1) * lanes
                ]
        for mask in far_first:
            push_one(x0, 0, mask, span)


    for name in ("phase", "mask"):
        for k in range(2):
            near(name, k).wait()
    for j in range(4):
        line = pl.ds(j, rows // 4, stride=4)
        for k in range(2):
            opening = ref.mask[k, line, :].astype(f32)
            angle = ref.phase[k, line, :]
            at = slice(k * reach, (k + 1) * reach)
            ref.own[j, 0, :, at] = opening * jnp.cos(angle)
            ref.own[j, 1, :, at] = opening * jnp.sin(angle)
    owners = spec.owners

    def pupil_copy(jj, w, q):
        return away(
            ref.own.at[2 * tile + jj], ref.pupil, ref.pupil_sent.at[2 * jj + w], ref.pupil_got,
            dict(tiles=tile, pat=w * half + jj * per + q),
        )

    for q in range(per):

        @pl.when(place == owners[q])
        def _():
            for jj in range(2):
                for w in range(2):
                    pupil_copy(jj, w, q).start()


    @pl.when(native)
    def _():
        for k in range(2):
            first_hop(k).wait_recv()
            first_onward(k).start()
        traded("slab", 0)
        enter(0, rows)

    cutoff = size // 2 * (size // 2)

    def centred(index):
        return jnp.where(index >= size // 2, index - size, index)

    def spectrum(i, carry):
        here = pl.ds(pl.multiple_of(i * step, step), step)
        row = lax.broadcasted_iota(jnp.int32, (step, lanes), 0) + i * step
        lane = lax.broadcasted_iota(jnp.int32, (step, lanes), 1)
        lane = jnp.where(lane < lanes // 2, lane, lane - lanes // 2)
        col = 4 * (lax.rem(me, per) * (lanes // 2) + lane) + me // per
        for l in range(count):
            v = centred(col + ref.freq[l, 1])
            for j in range(4):
                u = centred(4 * row + j + ref.freq[l, 0])
                radius = u * u + v * v
                inside = radius <= cutoff
                height = jnp.sqrt(jnp.maximum(cutoff - radius, 0).astype(f32))
                shift = spread_rate * (height - float(size // 2))
                ref.prop[0, l, j, here, :] = jnp.where(inside, jnp.cos(shift), 0.0)
                ref.prop[1, l, j, here, :] = jnp.where(inside, jnp.sin(shift), 0.0)
        return carry

    lax.fori_loop(0, quarter // step, spectrum, 0)

    @pl.when(foreign)
    def _():
        direct("slab", 0).wait_recv()
        enter(0, share)
        onward("slab", 0).wait_recv()
        enter(share, rows - share)


    ready("measured")
    counts = port("counts")
    lines = [fold_all(p) for p in range(patterns)]
    lines.append(jnp.zeros((counts.stage.shape[2] - patterns, lanes), f32))
    lines = jnp.concatenate(lines, 0)
    for d in range(devs):
        counts.stage[0, d] = lines
    for mask in far_first:
        dest = flip(place, mask)
        if mask:
            away(
                counts.stage.at[0, dest], counts.y.at[0, place], counts.sent.at[0], counts.got.at[0],
                dict(tiles=tile, pat=dest),
            ).start()
        else:
            local(counts.stage.at[0, dest], counts.y.at[0, place], counts.got.at[0]).start()
    ready("col_twiddle")
    ready("both")
    ready("full_inv")
    trade_foreign("slab", 1)
    land(x0, 0)
    forward_on("slab", 1)
    spread(x0, 0)

    def keep_spectrum(j, z):
        ref.cs[j] = z

    col_dot(ref.chi, ref.clo, keep_spectrum, 1.0)

    def first(l):
        for j in range(4):
            stow(j, shaped(ref.cs[j], l, j, 1.0))
        col_inverse(x1, l)

    each_led(first)
    trade_foreign("slab", 2)
    land(counts, 0)
    count_sum = jnp.sum(jnp.sum(counts.y[0], 0), 1, keepdims=True)
    area = spec.area
    code = [[ref.code[l, p].astype(f32) for l in range(count)] for p in range(patterns)]
    lit_sets = [[l for l in range(count) if (c + 1) >> l & 1] for c in range(spec.sets)]
    member_of = []
    for leds in lit_sets:
        member_of.append([])
        for p in range(patterns):
            is_in = 1.0
            for l in range(count):
                is_in = is_in * (code[p][l] if l in leds else 1.0 - code[p][l])
            member_of[-1].append(is_in)
    share_of = [[member_of[c][p] * (area / count_sum[p : p + 1]) for p in range(patterns)] for c in range(spec.sets)]

    def gather_counts(base, here, carry):
        for c in cut:
            seen = [ref.measured[p, here, c].astype(f32) for p in range(patterns)]
            for k in range(spec.sets):
                ref.lit_own[k, here, c] = sum(share_of[k][p] * seen[p] for p in range(patterns))
        return carry

    each_chunk(gather_counts)
    for k in range(spec.sets):
        trade_native("lit", k)
    trade_foreign("lit", 0)
    slab_phases(1)

    def forward(l):
        land(x1, l)
        inverse_full(x1.y, l, l)

        def chunk(base, here, carry):
            fields, at, blocks = gathered(l, base), spot(l, base), []
            for a, c in enumerate(cut):
                tr, ti = ref.tr[1, 0, here, c], ref.tr[1, 1, here, c]
                re, im = fields[a]
                re, im = re * tr - im * ti, re * ti + im * tr
                ref.passed1[0, at, c] = re
                ref.passed1[1, at, c] = im
                blocks.append((re, im))
            scattered(l, base, blocks)
            return carry

        each_chunk(chunk)
        emit_full(x2, l, l)

    each_led(forward)
    forward_on("slab", 2)
    forward_on("lit", 0)
    trade_foreign("lit", 1)
    columns(x2, x3, 1.0)
    trade_foreign("lit", *range(2, spec.sets))
    forward_on("lit", 1)
    slab_phases(2)
    b0, b1, b2, b3, sums = port("b0"), port("b1"), port("b2"), port("b3"), port("sums")
    ready("band")
    ready("band_inv")
    shape_pupil()

    def forward_band(l):
        land(x3, l)
        inverse_full(x3.y, l, l)

        def chunk(base, here, carry):
            fields, at, blocks = gathered(l, base), spot(l, base), []
            for a, c in enumerate(cut):
                tr, ti = ref.tr[2, 0, here, c], ref.tr[2, 1, here, c]
                re, im = fields[a]
                re, im = re * tr - im * ti, re * ti + im * tr
                ref.passed2[0, at, c] = re
                ref.passed2[1, at, c] = im
                blocks.append(tilt(l, here, a, (re, im), 1.0))
            scattered(l, base, blocks)
            return carry

        each_chunk(chunk)
        emit_band(b0, l)

    each_led(forward_band)
    forward_on("lit", *range(2, spec.sets))
    pupil_columns(b0, b1, 1.0)
    means = port("means")

    def announce(x, lines):
        lines = jnp.concatenate(lines + [jnp.zeros((x.stage.shape[2] - len(lines), lanes), f32)], 0)
        for d in range(devs):
            x.stage[0, d] = lines
        push(x, 0)

    def heard(x):
        land(x, 0)
        return jnp.sum(jnp.sum(x.y[0], 0), 1, keepdims=True)

    announce(means, [ref.energy[l] for l in range(count)])

    def camera(l):
        land(b1, l)
        inverse_band(b1, l)

    each_led(camera)
    for k in range(spec.sets):
        traded("lit", k)

    added = heard(means)
    pairs = [(l, m) for l in range(count) for m in range(l, count)]
    inverse_mean, number = [], []
    for k, leds in enumerate(lit_sets):
        members = sum(member_of[k])
        inverse = jnp.where(members > 0.0, area / sum(added[l : l + 1] for l in leds), 0.0)
        inverse_mean.append(inverse)
        number.append(members * inverse)

    def weigh(base, here, carry):
        fields = [gathered(l, base) for l in range(count)]
        adds, outgoing = [0.0] * spec.stat_rows, [[] for _ in range(count)]
        for a, c in enumerate(cut):
            power = [fields[l][a][0] * fields[l][a][0] + fields[l][a][1] * fields[l][a][1] for l in range(count)]
            values = [power[l] * power[m] for l, m in pairs]
            weight = [0.0] * count
            for k, leds in enumerate(lit_sets):
                seen = ref.lit[k, here, c]
                values += [seen * power[l] for l in leds]
                pull = (sum(power[l] for l in leds) * number[k] - seen) * inverse_mean[k]
                for l in leds:
                    weight[l] = weight[l] + pull
            for l in range(count):
                scale = 2.0 * weight[l]
                outgoing[l].append((scale * fields[l][a][0], scale * fields[l][a][1]))
            for k, value in enumerate(values):
                adds[k] = adds[k] + fold(value)
        for l in range(count):
            scattered(l, base, outgoing[l])
        return tuple(x + y for x, y in zip(carry, adds))

    stats = each_chunk(weigh, tuple(jnp.zeros((8, lanes), f32) for _ in range(spec.stat_rows)))
    announce(sums, [jnp.sum(line, 0, keepdims=True) for line in stats])
    each_led(lambda l: emit_band(b2, l))
    added = heard(sums)
    pulls = [0.0] * count
    cross_row = len(pairs)
    for k, leds in enumerate(lit_sets):
        square = 0.0
        for at, (l, m) in enumerate(pairs):
            if l in leds and m in leds:
                square = square + (1.0 if l == m else 2.0) * added[at : at + 1]
        cross = sum(added[cross_row + i : cross_row + i + 1] for i in range(len(leds)))
        cross_row += len(leds)
        couple = (number[k] * square * inverse_mean[k] - cross * inverse_mean[k]) / area
        for l in leds:
            pulls[l] = pulls[l] + couple * inverse_mean[k]
    for l in range(count):
        ref.pulled[l] = jnp.broadcast_to(2.0 * pulls[l], (1, lanes))
    pupil_columns(b2, b3, -1.0)
    y3, y2, y1, y0 = port("y3"), port("y2"), port("y1"), port("y0")
    ref.grad[...] = jnp.zeros(ref.grad.shape, f32)

    def back_band(l):
        land(b3, l)
        inverse_band(b3, l)

        def chunk(base, here, carry):
            fields, at, blocks = gathered(l, base), spot(l, base), []
            for a, c in enumerate(cut):
                re, im = tilt(l, here, a, fields[a], -1.0)
                pr, pi = ref.passed2[0, at, c], ref.passed2[1, at, c]
                ref.grad[1, here, c] += pr * im - pi * re
                tr, ti = ref.tr[2, 0, here, c], ref.tr[2, 1, here, c]
                blocks.append((re * tr + im * ti, im * tr - re * ti))
            scattered(l, base, blocks)
            return carry

        each_chunk(chunk)

        emit_full(y3, l, l)

        @pl.when(l == count - 1)
        def _():
            trade_native("grad", 1)
            trade_foreign("grad", 1)


    each_led(back_band)
    columns(y3, y2, -1.0)
    forward_on("grad", 1)

    def back(l):
        land(y2, l)
        inverse_full(y2.y, l, l)

        def chunk(base, here, carry):
            fields, at, blocks = gathered(l, base), spot(l, base), []
            for a, c in enumerate(cut):
                re, im = fields[a]
                pr, pi = ref.passed1[0, at, c], ref.passed1[1, at, c]
                ref.grad[0, here, c] += pr * im - pi * re
                tr, ti = ref.tr[1, 0, here, c], ref.tr[1, 1, here, c]
                blocks.append((re * tr + im * ti, im * tr - re * ti))
            scattered(l, base, blocks)
            return carry

        each_chunk(chunk)

        @pl.when(l == count - 1)
        def _():
            trade_native("grad", 0)
            trade_foreign("grad", 0)

        emit_full(y1, l, l)

    each_led(back)
    ready("slab_own")
    phases(ref.slab_own, ref.tr.at[0])
    ref.cs[...] = jnp.zeros(ref.cs.shape, f32)

    def last(l):
        land(y1, l)
        spread(y1, l)

        def add(j, z):
            ref.cs[j] += shaped(z, l, j, -1.0)

        col_dot(ref.chi, ref.clo, add, 1.0)

    last(0)
    forward_on("grad", 0)
    lax.fori_loop(1, count, lambda l, carry: last(l) or carry, 0)
    for j in range(4):
        stow(j, ref.cs[j])
    col_inverse(y0, 0, leave_one, (3, 2, 1, 0))
    land(y0, 0)
    inverse_full(y0.y, 0, 0)

    def leave(base, here, carry):
        fields = gathered(0, base)
        for a, c in enumerate(cut):
            tr, ti = ref.tr[0, 0, here, c], ref.tr[0, 1, here, c]
            re, im = fields[a]
            ref.grad0[here, c] = tr * im - ti * re
        return carry

    each_chunk(leave)
    final = local(ref.grad0, ref.result.at[0], ref.loads.at[len(spec.loaded)])
    final.start()

    for x, slots in (
        (x0, 1), (x1, count), (x2, count), (x3, count), (b0, count), (b1, count), (b2, count), (b3, count),
        (sums, 1), (means, 1), (counts, 1), (y3, count), (y2, count), (y1, count), (y0, 1),
    ):
        drain(x, slots)
    for q in range(per):

        @pl.when(place == owners[q])
        def _():
            for jj in range(2):
                for w in range(2):
                    pupil_copy(jj, w, q).wait_send()

    for name in part:
        trade_ends(name)
    for k in range(2):
        traded("grad", k)

    @pl.when(foreign)
    def _():
        block = y0.stage.at[0, 0]
        local(block, block, y0.sent.at[0]).wait()

    final.wait()


def body(tiles, slab_phase, pupil_phase, pupil_mask, led_code, led_freq, measured):
    devs = lax.axis_size("pat")
    slab_count, rows, size = slab_phase.shape
    patterns, count = led_code.shape
    quarter, cols, per = size // 4, size // devs, devs // 4
    band = 2 * pupil_radius
    band_cols = band // devs
    rt = row_tables(size, cols, band // 4)
    ct = col_tables(size)
    sets = 2**count - 1
    stat_rows = count * (count + 1) // 2 + count * 2 ** (count - 1)
    owners = [(q - pupil_radius // cols) % devs for q in range(per)]
    loads = dict(
        row_twiddle=rt.twiddle, full=rt.full,
        col_twiddle=jnp.asarray(ct.twiddle), both=jnp.asarray(ct.both), full_inv=rt.full_inv, band=rt.band,
        band_inv=rt.band_inv, measured=measured,
    )
    inputs = {name + "_hbm": value for name, value in loads.items()}
    inputs |= dict(phase_hbm=pupil_phase, mask_hbm=pupil_mask, slab_hbm=slab_phase, freq=led_freq, code=led_code.T)
    wide = 2 * quarter
    total = count * rows
    vmem, dma = pltpu.VMEM, pltpu.SemaphoreType.DMA
    scratch = {name: vmem(value.shape, value.dtype) for name, value in loads.items()}
    loads["slab_own"] = None
    scratch["slab_own"] = vmem((rows, size), f32)
    scratch |= dict(
        slab=vmem(slab_phase.shape, f32), lit=vmem((sets, rows, size), f32), lit_own=vmem((sets, rows, size), f32),
        phase=vmem((2, rows, pupil_radius), f32), mask=vmem((2, rows, pupil_radius), jnp.int32),
        phase_sem=dma((2,)), mask_sem=dma((2,)), own=vmem((4, 2, rows // 4, band), f32), pupil=vmem((2, band_cols, band), f32), shape=vmem((2, 4 * band_cols, lanes), f32),
        tilt_c=vmem((2 * count, 1, size), f32), tilt_r=vmem((2 * count, rows, lanes), f32),
        prop=vmem((2, count, 4, quarter, lanes), f32), tr=vmem((3, 2, rows, size), f32),
        passed1=vmem((2, total, size), f32), passed2=vmem((2, total, size), f32),
        spectrum=vmem((count, 4 * band_cols, lanes), f32), energy=vmem((count, 1, lanes), f32),
        pulled=vmem((count, 1, lanes), f32), grad=vmem((2, rows, size), f32), grad0=vmem((rows, size), f32),
        hi=vmem((4, total, wide), bf16), lo=vmem((4, total, wide), bf16), zs=vmem((4, total, wide), f32),
        ghi=vmem((4 * rows, wide), bf16), glo=vmem((4 * rows, wide), bf16),
        chi=vmem((quarter, 4 * lanes), bf16), clo=vmem((quarter, 4 * lanes), bf16),
        dhi=vmem((quarter, 4 * lanes), bf16), dlo=vmem((quarter, 4 * lanes), bf16),
        cz=vmem((4, quarter, lanes), f32), cs=vmem((4, quarter, lanes), f32),
        loads=dma((len(loads) + 1,)),
        pupil_sent=dma((4,)), pupil_got=dma, piece_got=dma((2,)),
    )
    for name, blocks in (("slab", 3), ("lit", sets), ("grad", 2)):
        scratch[name + "_relay"] = vmem((blocks, rows // 2, size), f32)
        for kind in ("_sent", "_got", "_late", "_via"):
            scratch[name + kind] = dma((blocks,))
    block, narrow = (devs, rows, lanes), (devs, band_cols, lanes)
    ports = dict(x0=(1, block), x1=(count, block), x2=(count, block), x3=(count, block))
    ports |= dict(b0=(count, narrow), b1=(count, narrow), b2=(count, narrow), b3=(count, narrow))
    ports |= dict(sums=(1, (devs, -(-stat_rows // 8) * 8, lanes)))
    ports |= dict(means=(1, (devs, -(-count // 8) * 8, lanes)))
    ports |= dict(counts=(1, (devs, -(-patterns // 8) * 8, lanes)))
    ports |= dict(y3=(count, block), y2=(count, block), y1=(count, block), y0=(1, block))
    for name, (slots, shape) in ports.items():
        scratch[name + "_stage"] = vmem((slots,) + shape, f32)
        scratch[name + "_y"] = vmem((slots,) + shape, f32)
        scratch[name + "_sent"] = dma((slots,))
        scratch[name + "_got"] = dma((slots,))
    spec = Names(
        count=count, rows=rows, quarter=quarter, devs=devs, tiles=tiles, patterns=patterns,
        area=float(size * size), stat_rows=stat_rows, sets=sets, owners=owners, loaded=list(loads),
        names=list(inputs) + ["result"] + list(scratch),
    )
    anywhere = pl.BlockSpec(memory_space=pl.ANY)
    smem = pl.BlockSpec(memory_space=pltpu.SMEM)
    return pl.pallas_call(
        functools.partial(whole_kernel, spec),
        out_shape=jax.ShapeDtypeStruct(slab_phase.shape, f32),
        in_specs=[smem if name in ("freq", "code") else anywhere for name in inputs],
        out_specs=anywhere,
        scratch_shapes=list(scratch.values()),
        compiler_params=pltpu.CompilerParams(
            collective_id=1, has_side_effects=True, vmem_limit_bytes=67043328
        ),
        name="whole",
    )(*inputs.values())


def solution(mesh):
    in_specs = (
        P("tiles", "pat", None),
        P("pat", None),
        P("pat", None),
        P(),
        P(),
        P("tiles", "pat", None),
    )
    out_specs = P("tiles", "pat", None)

    def run(slab_phase, *others):
        devs, tiles = mesh.shape["pat"], mesh.shape["tiles"]
        size, count = slab_phase.shape[-1], others[2].shape[1]
        fits = 2 * size == lanes * devs and count * size == lanes * devs and slab_phase.shape[0] == 3 * tiles
        fits = fits and tiles == 2 and devs == len(far_first)
        inner = functools.partial(body, tiles) if fits else plain_body
        return jax.shard_map(inner, mesh=mesh, in_specs=in_specs, out_specs=out_specs, check_vma=False)(
            slab_phase, *others
        )

    return run
```
